32 devices in a mesh: epoch: 4 (over y, x), strip: 8 (over z, core).
Axes of the slice: x: 2, y: 2, z: 4, core: 2. Of those that a mesh axis runs over, the one named last changes fastest.
Arguments:
- raw_tiles: float32 [4, 96, 256, 512], P('epoch', 'strip'), may hold values from -6 to 6
- tile_kind: int32 [4, 96], P('epoch', 'strip'), may hold values from 0 to 3
- tile_invvar: float32 [4, 96], P('epoch', 'strip'), may hold values from 0.2 to 5
- tile_heights: int32 [4, 8, 12], P('epoch'), may hold values from 1 to 256, 2048 in all within a row
- row_interp: float32 [4, 256, 256], replicated, may hold values from -0.4 to 1.9
- col_interp: float32 [4, 512, 512], replicated, may hold values from -0.4 to 1.9
- psf_profiles: float32 [2, 2, 31], replicated, may hold values from -1 to 1
- psf_poly: float32 [4, 2, 6], replicated, may hold values from -1 to 1
Outputs:
- difference: float32 [4, 2048, 4096], P('epoch', 'strip')
The draws below stay inside these ranges and needn't reach their ends.
Inputs may be any that keep to these rules, and one draw needn't show every extreme that they name: `tile_heights`: along the last dimension, the heights of one column block's tiles from the top of the patch down; they sum to 2048, and the tallest is exactly 256.
All inputs are finite; a program needn't handle non-finite values.
Results may differ from the reference program's by a relative error of at most 0.0003.
Values sent between devices are 32-bit elements; how exact they have to be, the bound alone decides.
No kernel may reach another device: no remote copies, remote signals or barrier semaphores. Data moves between devices by JAX's collectives and lax.ppermute only.
A program may use at most 128 MiB of HBM per device.

```python
import math
import jax
import jax.numpy as jnp
import numpy as np
from jax import lax

NCOL = 4096
TH = 256
TW = 512
KINDS = 4
KSIZE = 31
CB = 8
TILES = 96
PER_COL = 12
NROW = 2048
EPOCHS = 4


def interp_band(key, kinds_count, order):
    first_key, second_key, third_key = jax.random.split(key, 3)
    offset = jnp.arange(order)[None, :] - jnp.arange(order)[:, None]
    distance = jnp.abs(offset)
    shape_table = jnp.array([0.0, 0.3, -0.1, 0.04], jnp.float32)
    profile = jnp.take(shape_table, jnp.minimum(distance, 3))
    nearby = (distance >= 1) & (distance <= 3)
    spread = 0.3 / jnp.sqrt(jnp.float32(order))
    factor = jax.random.uniform(first_key, (kinds_count, order, order), jnp.float32, 0.5, 1.5)
    diagonal = jax.random.uniform(second_key, (kinds_count, order), jnp.float32, 1.4, 1.6)
    dense = jax.random.normal(third_key, (kinds_count, order, order), jnp.float32) * spread
    dense = jnp.clip(dense, -0.19, 0.19)
    off_part = jnp.where(nearby[None], profile[None] * factor, 0.0) + jnp.where(distance[None] >= 1, dense, 0.0)
    return off_part + diagonal[:, :, None] * jnp.eye(order, dtype=jnp.float32)[None]


def draw_row_interp(key, part):
    return interp_band(jax.random.fold_in(key, 11), KINDS, TH)


def draw_col_interp(key, part):
    return interp_band(jax.random.fold_in(key, 23), KINDS, TW)


def touch_ends(values, key, least, top_value):
    place = [jax.random.randint(jax.random.fold_in(key, axis), (), 0, length) for axis, length in enumerate(values.shape)]
    widest = values.shape.index(max(values.shape))
    next_to = place[:widest] + [(place[widest] + 1) % values.shape[widest]] + place[widest + 1:]
    return values.at[tuple(place)].set(least).at[tuple(next_to)].set(top_value)


def levels(rng, shape, cuts, smallest, largest):
    level = 1.0
    for axis_at, parts in cuts:
        steps = jax.random.uniform(jax.random.fold_in(jax.random.fold_in(rng, 6), axis_at), (parts,), jnp.float32, smallest / len(cuts), largest / len(cuts))
        level = level * jnp.repeat(jnp.exp(steps), shape[axis_at] // parts).reshape((-1,) + (1,) * (len(shape) - 1 - axis_at))
    return level


def split_up(count, total, bound, slope):
    portions = [(1 << 20) // math.isqrt(standing ** slope) + 1 for standing in range(2, count + 1)]
    spare, counts = total - bound - (count - 1), [1] * (count - 1)
    while spare > 0:
        candidates = [i for i in range(count - 1) if counts[i] < bound]
        pool, budget = sum([portions[i] for i in candidates]), spare
        for i in candidates:
            more = min(bound - counts[i], max(1, budget * portions[i] // pool), spare)
            counts[i] = counts[i] + more
            spare = spare - more
    return np.array([bound] + counts)


def uneven_parts(stream_key, count, total, most, skew):
    if count == 2:
        one = jax.random.randint(stream_key, (), max(1, total - most), min(most, total - 1) + 1)
        return jnp.stack([one, total - one])
    tallies = jnp.asarray(split_up(count, total, most, skew), jnp.int32)
    twos = (count - 1) // 2
    giver, taker = tallies[1:1 + 2 * twos:2], tallies[2:2 + 2 * twos:2]
    room = jnp.minimum(giver - 1, most - taker)
    moved = jax.random.randint(jax.random.fold_in(stream_key, 1), (twos,), 0, 1 << 20) % (room + 1)
    tallies = tallies.at[1:1 + 2 * twos:2].set(giver - moved).at[2:2 + 2 * twos:2].set(taker + moved)
    return tallies[jax.random.permutation(jax.random.fold_in(stream_key, 2), count)]


def scatter_about(rng, dims, deviation, bound, cuts=(), held_as=jnp.bfloat16):
    loudness = levels(rng, dims, cuts, -0.22, 0.18) if cuts else 1.0
    values = jax.random.normal(rng, dims, jnp.float32) * deviation * loudness
    return jnp.minimum(jnp.maximum(values, -bound), bound).astype(held_as)


def setup_inputs(seed: int = 0) -> dict:
    key_of = jax.random.split(jax.random.key(seed), 9)
    return {
        "raw_tiles": scatter_about(key_of[0], (EPOCHS, TILES, TH, TW), 1.0, 6.0, ((0, 4), (1, 8)), jnp.float32),
        "tile_kind": touch_ends(jax.random.randint(key_of[1], (EPOCHS, TILES), 0, KINDS), jax.random.fold_in(key_of[1], 1), 0, KINDS - 1).astype(jnp.int32),
        "tile_invvar": jnp.clip(jnp.exp(math.log(5.0) - 3.218876 * jax.random.uniform(key_of[2], (EPOCHS, TILES), jnp.float32) ** levels(key_of[2], (EPOCHS, TILES), ((0, 4), (1, 8)), -0.2, 0.2)), 0.2, 5.0),
        "tile_heights": jax.vmap(lambda own: uneven_parts(own, PER_COL, NROW, TH, 2))(jax.random.split(key_of[3], EPOCHS * CB)).reshape((EPOCHS, CB, PER_COL)).astype(jnp.int32),
        "row_interp": draw_row_interp(jax.random.fold_in(key_of[8], 71), 0),
        "col_interp": draw_col_interp(jax.random.fold_in(key_of[8], 71), 0),
        "psf_profiles": scatter_about(key_of[6], (2, 2, KSIZE), KSIZE ** -0.5, 1.0, (), jnp.float32),
        "psf_poly": jnp.clip(jax.random.uniform(key_of[7], (EPOCHS, 2, 6), jnp.float32, -1.0, 1.0), -1.0, 1.0),
    }


precise = lax.Precision.HIGHEST


def positions(first_cell, length, extent):
    counter = (first_cell + jnp.arange(length)).astype(jnp.float32)
    return (2.0 * counter + 1.0) / extent - 1.0


def coeff_maps(poly_rows, row_coords, col_coords):
    row_term = row_coords[:, None]
    col_term = col_coords[None, :]
    terms = poly_rows[..., None, None]
    return (terms[..., 0, :, :] + terms[..., 1, :, :] * row_term + terms[..., 2, :, :] * col_term
            + terms[..., 3, :, :] * row_term * row_term + terms[..., 4, :, :] * row_term * col_term
            + terms[..., 5, :, :] * col_term * col_term)


def reference(raw_tiles, tile_kind, tile_invvar, tile_heights, row_interp, col_interp, psf_profiles, psf_poly):
    def sky_epoch(bundle):
        raw, tile_kinds, invvar, heights = bundle
        live_rows = jnp.arange(TH)[None, :] < heights.reshape(-1)[:, None]
        masked = jnp.where(live_rows[:, :, None], raw, 0.0)
        half_warped = jnp.einsum('tij,tjk->tik', row_interp[tile_kinds], masked, precision=precise)
        warped = jnp.einsum('tik,tlk->til', half_warped, col_interp[tile_kinds], precision=precise)
        starts = (jnp.cumsum(heights, axis=1) - heights).astype(jnp.int32)
        sky_rows = jnp.arange(NROW).astype(jnp.int32)
        covering = (jnp.sum((sky_rows[None, :, None] >= starts[:, None, :]).astype(jnp.int32), axis=2) - 1).astype(jnp.int32)
        picked_start = jnp.take_along_axis(starts, covering, axis=1)
        local_row = (sky_rows[None, :] - picked_start).astype(jnp.int32)
        tile_ids = (jnp.arange(CB)[:, None] * PER_COL + covering).astype(jnp.int32)
        flattened = warped.reshape(TILES * TH, TW)
        placed = jnp.take(flattened, (tile_ids * TH + local_row).reshape(-1), axis=0).reshape(CB, NROW, TW)
        science = jnp.transpose(placed, (1, 0, 2)).reshape(NROW, NCOL)
        weights = jnp.transpose(invvar[tile_ids])
        return science, weights

    sciences, weights = lax.map(sky_epoch, (raw_tiles, tile_kind, tile_invvar, tile_heights))
    weighted_sum = jnp.sum(sciences.reshape(EPOCHS, NROW, CB, TW) * weights[..., None], axis=0)
    weight_sum = jnp.sum(weights, axis=0)
    template = (weighted_sum / weight_sum[:, :, None]).reshape(NROW, NCOL)
    margin = KSIZE // 2
    padded = jnp.pad(template, margin)
    convolved = []
    for basis_index in range(2):
        along_rows = jnp.zeros((NROW, NCOL + 2 * margin), jnp.float32)
        for offset in range(KSIZE):
            along_rows = along_rows + psf_profiles[basis_index, 0, offset] * padded[offset:offset + NROW, :]
        result = jnp.zeros((NROW, NCOL), jnp.float32)
        for offset in range(KSIZE):
            result = result + psf_profiles[basis_index, 1, offset] * along_rows[:, offset:offset + NCOL]
        convolved.append(result)
    row_coords = positions(0, NROW, NROW)
    col_coords = positions(0, NCOL, NCOL)

    def subtract(bundle):
        science, poly_rows = bundle
        coeffs = coeff_maps(poly_rows, row_coords, col_coords)
        return science - (coeffs[0] * convolved[0] + coeffs[1] * convolved[1])

    return lax.map(subtract, (sciences, psf_poly))
```

```python
import functools

import jax
import jax.numpy as jnp
from jax import lax
from jax.experimental import pallas as pl
from jax.experimental.pallas import tpu as pltpu
from jax.sharding import PartitionSpec as P

ROWS_DEV = 256
HALO = 16
LANES = 128
F32 = jnp.float32
BF16 = jnp.bfloat16


def split(x):
    hi = x.astype(BF16)
    lo = (x - hi.astype(F32)).astype(BF16)
    return hi, lo


def dot(a, b, trans_b=False):
    dims = (((1,), (1 if trans_b else 0,)), ((), ()))
    return lax.dot_general(a, b, dims, preferred_element_type=F32)


def dot3(a, b, trans_b=False):
    a_hi, a_lo = a
    b_hi, b_lo = b
    return dot(a_hi, b_hi, trans_b) + (dot(a_lo, b_hi, trans_b) + dot(a_hi, b_lo, trans_b))


def start_and_wait(copies):
    for copy in copies:
        copy.start()
    for copy in copies:
        copy.wait()


def slot_order(count, order):
    bits = len(order)
    key = lambda j: sum(((j >> order[i]) & 1) << (bits - 1 - i) for i in range(bits))
    slots = sorted(range(count), key=key)
    return slots[: count // 2], slots[count // 2 :]


def warp_kernel(
    geom, kind_ref, heights_ref, invvar_ref, raw_ref, rmat_ref, cmat_ref,
    sci_a, sci_b, keep_a, send_a, keep_b, send_b,
    sci_s, num_s, wt_s, chi_s, clo_s, top_s, sems,
):
    epochs, nrow, share, relative, orders = geom
    t = pl.program_id(0)
    tiles = pl.num_programs(0)
    _, tile_rows, tile_cols = raw_ref.shape
    per_col = heights_ref.shape[2]
    span = tile_rows + 8
    me = lax.axis_index("epoch")
    first_tile = lax.axis_index("strip") * tiles
    block = lax.div(first_tile, per_col)
    offset_in = lax.rem(first_tile, per_col)

    @pl.when(t == 0)
    def _():
        top_s[0] = lax.fori_loop(
            0, offset_in, lambda i, total: total + heights_ref[0, block, i], jnp.int32(0)
        )
        for k in range(cmat_ref.shape[0]):
            chi_s[k], clo_s[k] = split(cmat_ref[k])
        sci_s[...] = jnp.zeros_like(sci_s)
        num_s[...] = jnp.zeros_like(num_s)
        wt_s[...] = jnp.zeros_like(wt_s)

    kind = kind_ref[0, t]
    height = heights_ref[0, block, offset_in + t]
    weight = invvar_ref[0, t]
    top = top_s[0]
    top_s[0] = top + height
    start = pl.multiple_of(jnp.minimum(lax.div(top, 8) * 8, nrow - span), 8)
    off = top - start

    live = lax.broadcasted_iota(jnp.int32, (tile_rows, tile_cols), 0) < height
    image = split(jnp.where(live, raw_ref[0], 0.0))
    half = dot3(image, (chi_s[kind], clo_s[kind]), trans_b=True)
    rows = jnp.concatenate([rmat_ref[kind], jnp.zeros((8, tile_rows), F32)], axis=0)
    placed = dot3(split(pltpu.roll(rows, off, 0)), split(half))

    local = lax.broadcasted_iota(jnp.int32, (span, tile_cols), 0) - off
    own = (local >= 0) & (local < height)
    here = pl.ds(start, span)
    sci_s[here, :] = jnp.where(own, placed, sci_s[here, :])
    own_share = own[:, :share]
    for j in range(epochs):
        if relative:
            column = pl.ds(pl.multiple_of(jnp.bitwise_xor(me, j) * share, LANES), share)
        else:
            column = pl.ds(j * share, share)
        num_s[j, here, :] = jnp.where(own_share, weight * sci_s[here, column], num_s[j, here, :])
    flat = lax.broadcasted_iota(jnp.int32, wt_s.shape, 0) * share + lax.broadcasted_iota(
        jnp.int32, wt_s.shape, 1
    )
    wt_s[...] = jnp.where((flat >= top) & (flat < top + height), weight, wt_s[...])

    @pl.when(t == tiles - 1)
    def _():
        strips, rows_half, _ = sci_a.shape
        pairs = []
        for s in range(strips):
            for i, out in enumerate((sci_a, sci_b)):
                pairs.append((sci_s.at[pl.ds((2 * s + i) * rows_half, rows_half)], out.at[s]))
        nhalf = nrow // 2
        whalf = wt_s.shape[0] // 2
        for i, (order, outs) in enumerate(zip(orders, ((keep_a, send_a), (keep_b, send_b)))):
            for slots, out in zip(slot_order(epochs, order), outs):
                for place, j in enumerate(slots):
                    pairs.append((num_s.at[j, pl.ds(i * nhalf, nhalf)], out.at[place, pl.ds(0, nhalf)]))
                    pairs.append((wt_s.at[pl.ds(i * whalf, whalf)], out.at[place, pl.ds(nhalf, whalf)]))
        start_and_wait([pltpu.make_async_copy(a, b, sems.at[n]) for n, (a, b) in enumerate(pairs)])


def template_kernel(terms, *refs):
    term_refs, out_ref, pad_s = refs[:-2], refs[-2], refs[-1]
    strips, long, share = out_ref.shape
    rows_dev = long - 2 * HALO
    nrow = strips * rows_dev
    nhalf = nrow // 2
    whalf = nhalf // share
    edge = jnp.zeros((HALO, share), F32)
    pad_s[pl.ds(0, HALO), :] = edge
    pad_s[pl.ds(HALO + nrow, HALO), :] = edge
    for part in range(2):
        own = term_refs[part * terms : (part + 1) * terms]
        add = lambda place: functools.reduce(lambda a, b: a + b, [ref[0, place, :] for ref in own])
        weights = add(pl.ds(nhalf, whalf))
        for i in range(whalf):
            below = jnp.transpose(jnp.broadcast_to(weights[i : i + 1, :], (share, share)))
            pad_s[pl.ds(HALO + part * nhalf + i * share, share), :] = add(pl.ds(i * share, share)) / below
    for s in range(strips):
        out_ref[s] = pad_s[pl.ds(s * rows_dev, long), :]


def bands_kernel(psf_ref, toep_hi, toep_lo, band_ref):
    basis, _, ksize = psf_ref.shape
    margin = ksize // 2
    for k in range(basis):
        shape = (2 * LANES, LANES)
        tap = lax.broadcasted_iota(jnp.int32, shape, 0) - lax.broadcasted_iota(jnp.int32, shape, 1)
        tap = tap - (LANES // 2 - margin)
        value = jnp.zeros(shape, F32)
        for j in range(ksize):
            value = jnp.where(tap == j, psf_ref[k, 1, j], value)
        toep_hi[:, pl.ds(k * LANES, LANES)], toep_lo[:, pl.ds(k * LANES, LANES)] = split(value)
        shape = (LANES, LANES + 2 * HALO)
        tap = lax.broadcasted_iota(jnp.int32, shape, 1) - lax.broadcasted_iota(jnp.int32, shape, 0)
        tap = tap - (HALO - margin)
        value = jnp.zeros(shape, F32)
        for j in range(ksize):
            value = jnp.where(tap == j, psf_ref[k, 0, j], value)
        band_ref[k, pl.ds(0, LANES), :], band_ref[k, pl.ds(LANES, LANES), :] = split(value)


def match_kernel(geom, *refs):
    pieces, nrow, ncol = geom
    count = len(pieces)
    tile_refs = refs[:count]
    poly_ref, toep_hi, toep_lo, band_ref, sci_a, sci_b, out_ref, pad_s, row_s, sems = refs[count:]
    step = pl.program_id(0)
    tiles = pad_s.shape[0] - 2
    rows_dev = pad_s.shape[1] - 2 * HALO
    me = lax.axis_index("epoch")
    strip = lax.axis_index("strip")
    per_step = out_ref.shape[2] // LANES

    @pl.when(step == 0)
    def _():
        copies = []
        for ref, (slot, first, stride) in zip(tile_refs, pieces):
            place = first if slot is None else jnp.bitwise_xor(me, slot) + first
            for i in range(ref.shape[0]):
                copies.append(
                    pltpu.make_async_copy(ref.at[i], pad_s.at[1 + place + i * stride], sems.at[len(copies)])
                )
        for copy in copies:
            copy.start()
        pad_s[0] = jnp.zeros(pad_s.shape[1:], F32)
        pad_s[tiles + 1] = jnp.zeros(pad_s.shape[1:], F32)
        shape = (rows_dev, LANES)
        counter = (strip * rows_dev + lax.broadcasted_iota(jnp.int32, shape, 0)).astype(F32)
        u = (2.0 * counter + 1.0) / nrow - 1.0
        for k in range(2):
            p = [poly_ref[me, k, i] for i in range(6)]
            row_s[k, 0] = p[0] + u * (p[1] + p[3] * u)
            row_s[k, 1] = p[2] + p[4] * u
        for copy in copies:
            copy.wait()

    lane = lax.broadcasted_iota(jnp.int32, pad_s.shape[1:], 1)
    base = step * per_step
    shifted = []
    for m in range(per_step + 1):
        mixed = jnp.where(lane < LANES // 2, pad_s[base + m + 1], pad_s[base + m])
        shifted.append(split(pltpu.roll(mixed, LANES // 2, 1)))
    toep = (toep_hi[...], toep_lo[...])
    sci_refs = (sci_a, sci_b)
    for pair in range(per_step // 2):
        across = []
        for c in (2 * pair, 2 * pair + 1):
            window = tuple(
                jnp.concatenate([shifted[c][i], shifted[c + 1][i]], axis=1) for i in range(2)
            )
            across.append(dot3(window, toep))
        width = 2 * LANES
        cols = lax.broadcasted_iota(jnp.int32, (1, width), 1) + (base + 2 * pair) * LANES
        v = (2.0 * cols.astype(F32) + 1.0) / ncol - 1.0
        for part in range(rows_dev // LANES):
            total = sci_refs[part][0, :, pl.ds(pair * width, width)]
            for k in range(2):
                both = jnp.concatenate(
                    [a[part * LANES : part * LANES + LANES + 2 * HALO, k * LANES : (k + 1) * LANES] for a in across],
                    axis=1,
                )
                hi, lo = split(both)
                wide = dot(band_ref[k], hi)
                done = wide[:LANES] + (wide[LANES:] + dot(band_ref[k, pl.ds(0, LANES), :], lo))
                place = pl.ds(part * LANES, LANES)
                one = jnp.concatenate([row_s[k, 0, place, :]] * 2, axis=1)
                two = jnp.concatenate([row_s[k, 1, place, :]] * 2, axis=1)
                coeff = one + v * (two + poly_ref[me, k, 5] * v)
                total = total - coeff * done
            out_ref[0, pl.ds(part * LANES, LANES), pl.ds(pair * width, width)] = total


def swap(value, axis, bit):
    count = lax.axis_size(axis)
    return lax.ppermute(value, axis, [(i, i ^ (1 << bit)) for i in range(count)])


def shards(
    raw_tiles, tile_kind, tile_invvar, tile_heights, row_interp, col_interp, psf_profiles, psf_poly
):
    strips, epochs = lax.axis_size("strip"), lax.axis_size("epoch")
    _, tiles, tile_rows, tile_cols = raw_tiles.shape
    _, blocks, per_col = tile_heights.shape
    ncol, nrow = blocks * tile_cols, ROWS_DEV * strips
    sources = strips // blocks
    share = tile_cols // epochs
    relative = share % LANES == 0
    bits = epochs.bit_length() - 1
    orders = (tuple(range(bits)), tuple(reversed(range(bits))))
    nhalf = nrow // 2
    wrows = nrow // share
    long_half = nhalf + wrows // 2
    half_rows = ROWS_DEV // 2
    smem = pl.BlockSpec(memory_space=pltpu.SMEM)
    hbm = pl.BlockSpec(memory_space=pl.ANY)
    vmem = pl.BlockSpec(memory_space=pltpu.VMEM)
    kinds = col_interp.shape[0]

    sci_shape = jax.ShapeDtypeStruct((strips, half_rows, tile_cols), F32)
    num_shape = jax.ShapeDtypeStruct((epochs // 2, long_half, share), F32)
    sci_a, sci_b, keep_a, send_a, keep_b, send_b = pl.pallas_call(
        functools.partial(warp_kernel, (epochs, nrow, share, relative, orders)),
        grid=(tiles,),
        in_specs=[
            smem,
            smem,
            smem,
            pl.BlockSpec((1, tile_rows, tile_cols), lambda t: (t, 0, 0)),
            pl.BlockSpec((kinds, tile_rows, tile_rows), lambda t: (0, 0, 0), pipeline_mode=pl.Buffered(1)),
            pl.BlockSpec((kinds, tile_cols, tile_cols), lambda t: (0, 0, 0), pipeline_mode=pl.Buffered(1)),
        ],
        out_specs=[hbm] * 6,
        out_shape=[sci_shape, sci_shape] + [num_shape] * 4,
        scratch_shapes=[
            pltpu.VMEM((nrow, tile_cols), F32),
            pltpu.VMEM((epochs, nrow, share), F32),
            pltpu.VMEM((wrows, share), F32),
            pltpu.VMEM((kinds, tile_cols, tile_cols), BF16),
            pltpu.VMEM((kinds, tile_cols, tile_cols), BF16),
            pltpu.SMEM((1,), jnp.int32),
            pltpu.SemaphoreType.DMA((2 * strips + 4 * epochs,)),
        ],
        name="warp",
        cost_estimate=pl.CostEstimate(flops=15_000_000_000, bytes_accessed=20_000_000, transcendentals=0),
    )(tile_kind, tile_heights, tile_invvar, raw_tiles[0], row_interp, col_interp)

    got_a = lax.all_to_all(sci_a, "strip", split_axis=0, concat_axis=0, tiled=True)

    if not relative:
        me = lax.axis_index("epoch")
        fixed = []
        for order, pair in zip(orders, ((keep_a, send_a), (keep_b, send_b))):
            keep, send = slot_order(epochs, order)
            whole = jnp.concatenate(pair, axis=0)
            place = [(keep + send).index(j) for j in range(epochs)]
            byshare = whole[jnp.asarray(place)]
            wanted = jnp.bitwise_xor(jnp.asarray(keep + send), me)
            moved = jnp.take(byshare, wanted, axis=0)
            fixed.append((moved[: epochs // 2], moved[epochs // 2 :]))
        (keep_a, send_a), (keep_b, send_b) = fixed
    terms = [[keep_a], [keep_b]]
    sends = [send_a, send_b]
    for i in range(bits):
        for part in range(2):
            terms[part].append(swap(sends[part], "epoch", orders[part][i]))
        left = epochs >> (i + 1)
        if left > 1:
            sends = [
                functools.reduce(lambda a, b: a + b, [t[left // 2 : left] for t in own]) for own in terms
            ]
    if sources > 1:
        fixed = []
        for own in terms:
            total = functools.reduce(lambda a, b: a + b, [t[:1] for t in own])
            around = total
            for k in range(1, sources):
                ring = [(i, i // sources * sources + (i + k) % sources) for i in range(strips)]
                around = around + lax.ppermute(total, "strip", ring)
            fixed.append([around])
        terms = fixed

    long = ROWS_DEV + 2 * HALO
    first_slot = pl.BlockSpec((1, long_half, share), lambda i: (0, 0, 0))
    strips_out = pl.pallas_call(
        functools.partial(template_kernel, len(terms[0])),
        grid=(1,),
        in_specs=[first_slot] * (2 * len(terms[0])),
        out_specs=pl.BlockSpec((strips, long, share), lambda i: (0, 0, 0)),
        out_shape=jax.ShapeDtypeStruct((strips, long, share), F32),
        scratch_shapes=[pltpu.VMEM((nrow + 2 * HALO, share), F32)],
        name="template",
        cost_estimate=pl.CostEstimate(flops=2_000_000, bytes_accessed=5_000_000, transcendentals=0),
    )(*terms[0], *terms[1])
    mine = lax.all_to_all(strips_out, "strip", split_axis=0, concat_axis=0, tiled=True)
    sci_b, mine = lax.optimization_barrier((sci_b, mine))
    got_b = lax.all_to_all(sci_b, "strip", split_axis=0, concat_axis=0, tiled=True)
    if sources > 1:
        mine = mine[::sources]
        got_a = jnp.sum(got_a.reshape(blocks, sources, half_rows, tile_cols), axis=1)
        got_b = jnp.sum(got_b.reshape(blocks, sources, half_rows, tile_cols), axis=1)

    per_block = tile_cols // LANES
    if epochs == 4 and relative:
        near = [swap(mine, "epoch", b) for b in range(2)]
        cut = blocks // 2
        far_low = swap(near[1][:cut], "epoch", 0)
        far_high = swap(near[0][cut:], "epoch", 1)
        arrays = [mine, near[0], near[1], far_low, far_high]
        pieces = [(0, 0, per_block), (1, 0, per_block), (2, 0, per_block), (3, 0, per_block), (3, cut * per_block, per_block)]
    else:
        slots = [mine]
        for b in range(bits):
            slots = slots + [swap(s, "epoch", b) for s in slots]
        me = lax.axis_index("epoch")
        every = jnp.take(jnp.stack(slots), jnp.bitwise_xor(jnp.arange(epochs), me), axis=0)
        flat = jnp.transpose(every, (1, 2, 0, 3)).reshape(blocks, long, per_block, LANES)
        arrays = [jnp.transpose(flat, (0, 2, 1, 3)).reshape(blocks * per_block, long, LANES)]
        pieces = [(None, 0, 1)]

    basis, _, ksize = psf_profiles.shape
    toep_hi, toep_lo, band = pl.pallas_call(
        bands_kernel,
        in_specs=[smem],
        out_specs=[vmem] * 3,
        out_shape=[
            jax.ShapeDtypeStruct((2 * LANES, 2 * LANES), BF16),
            jax.ShapeDtypeStruct((2 * LANES, 2 * LANES), BF16),
            jax.ShapeDtypeStruct((basis, 2 * LANES, LANES + 2 * HALO), BF16),
        ],
        name="bands",
        cost_estimate=pl.CostEstimate(flops=10_000_000, bytes_accessed=500_000, transcendentals=0),
    )(psf_profiles)

    const = lambda b: (0, 0)
    sci_spec = pl.BlockSpec((1, half_rows, tile_cols), lambda b: (b, 0, 0))
    return pl.pallas_call(
        functools.partial(match_kernel, (pieces, nrow, ncol)),
        grid=(blocks,),
        in_specs=[hbm] * len(arrays)
        + [
            smem,
            pl.BlockSpec(toep_hi.shape, const),
            pl.BlockSpec(toep_lo.shape, const),
            pl.BlockSpec(band.shape, lambda b: (0, 0, 0)),
            sci_spec,
            sci_spec,
        ],
        out_specs=pl.BlockSpec((1, ROWS_DEV, tile_cols), lambda b: (0, 0, b)),
        out_shape=jax.ShapeDtypeStruct((1, ROWS_DEV, ncol), F32),
        scratch_shapes=[
            pltpu.VMEM((blocks * per_block + 2, long, LANES), F32),
            pltpu.VMEM((2, 2, ROWS_DEV, LANES), F32),
            pltpu.SemaphoreType.DMA((sum(a.shape[0] for a in arrays),)),
        ],
        name="match",
        cost_estimate=pl.CostEstimate(flops=15_000_000_000, bytes_accessed=15_000_000, transcendentals=0),
    )(*arrays, psf_poly, toep_hi, toep_lo, band, got_a, got_b)


def solution(mesh):
    in_specs = (
        P("epoch", "strip", None, None),
        P("epoch", "strip"),
        P("epoch", "strip"),
        P("epoch", None, None),
        P(),
        P(),
        P(),
        P(),
    )
    out_specs = P("epoch", "strip", None)
    return jax.shard_map(shards, mesh=mesh, in_specs=in_specs, out_specs=out_specs, check_vma=False)
```

```python
import functools

import jax
import jax.numpy as jnp
from jax import lax
from jax.experimental import pallas as pl
from jax.experimental.pallas import tpu as pltpu
from jax.sharding import PartitionSpec as P


ROWS_DEV = 256
HALO = 16
LANES = 128
F32 = jnp.float32
BF16 = jnp.bfloat16


def split(x):
    hi = x.astype(BF16)
    lo = (x - hi.astype(F32)).astype(BF16)
    return hi, lo


def dot(a, b, trans_b=False):
    dims = (((1,), (1 if trans_b else 0,)), ((), ()))
    return lax.dot_general(a, b, dims, preferred_element_type=F32)


def dot3(a, b, trans_b=False):
    a_hi, a_lo = a
    b_hi, b_lo = b
    return dot(a_hi, b_hi, trans_b) + (dot(a_lo, b_hi, trans_b) + dot(a_hi, b_lo, trans_b))


def start_and_wait(copies):
    for copy in copies:
        copy.start()
    for copy in copies:
        copy.wait()


def slot_order(count, order):
    bits = len(order)
    key = lambda j: sum(((j >> order[i]) & 1) << (bits - 1 - i) for i in range(bits))
    slots = sorted(range(count), key=key)
    return slots[: count // 2], slots[count // 2 :]


def warp_kernel(
    geom, part, kind_ref, heights_ref, invvar_ref, raw_ref, rmat_ref, cmat_ref, *refs
):
    epochs, nrow, share, orders = geom
    t = pl.program_id(0)
    tiles = pl.num_programs(0)
    _, tile_rows, tile_cols = raw_ref.shape
    width = cmat_ref.shape[1]
    per_col = heights_ref.shape[2]
    span = tile_rows + 8
    half = epochs // 2
    me = lax.axis_index("epoch")
    first_tile = lax.axis_index("strip") * tiles
    block = lax.div(first_tile, per_col)
    offset_in = lax.rem(first_tile, per_col)
    if part == 0:
        sci, num_out, sci_s, num_s, chi_s, clo_s, top_s, sems = refs
        slot = lambda q: q
    else:
        other, sci, *outs, sci_s, num_s, wt_s, chi_s, clo_s, top_s, sems, other_sems = refs
        slot = lambda q: jnp.bitwise_xor(me, half + q)
        brought = [
            pltpu.make_async_copy(other.at[q], num_s.at[jnp.bitwise_xor(me, q)], other_sems.at[q])
            for q in range(half)
        ]

    @pl.when(t == 0)
    def _():
        if part == 1:
            for copy in brought:
                copy.start()
        top_s[0] = lax.fori_loop(
            0, offset_in, lambda i, total: total + heights_ref[0, block, i], jnp.int32(0)
        )
        for k in range(cmat_ref.shape[0]):
            chi_s[k], clo_s[k] = split(cmat_ref[k])
        sci_s[...] = jnp.zeros_like(sci_s)
        for q in range(half):
            num_s[slot(q)] = jnp.zeros(num_s.shape[1:], F32)
        if part == 1:
            wt_s[...] = jnp.zeros_like(wt_s)

    kind = kind_ref[0, t]
    height = heights_ref[0, block, offset_in + t]
    weight = invvar_ref[0, t]
    top = top_s[0]
    top_s[0] = top + height
    start = pl.multiple_of(jnp.minimum(lax.div(top, 8) * 8, nrow - span), 8)
    off = top - start

    live = lax.broadcasted_iota(jnp.int32, (tile_rows, tile_cols), 0) < height
    image = split(jnp.where(live, raw_ref[0], 0.0))
    across = dot3(image, (chi_s[kind], clo_s[kind]), trans_b=True)
    rows = jnp.concatenate([rmat_ref[kind], jnp.zeros((8, tile_rows), F32)], axis=0)
    placed = dot3(split(pltpu.roll(rows, off, 0)), split(across))

    local = lax.broadcasted_iota(jnp.int32, (span, width), 0) - off
    own = (local >= 0) & (local < height)
    here = pl.ds(start, span)
    sci_s[here, :] = jnp.where(own, placed, sci_s[here, :])
    for q in range(half):
        scaled = weight * placed[:, q * share : (q + 1) * share]
        num_s[slot(q), here, :] = jnp.where(own[:, :share], scaled, num_s[slot(q), here, :])
    if part == 1:
        flat = lax.broadcasted_iota(jnp.int32, wt_s.shape, 0) * share + lax.broadcasted_iota(
            jnp.int32, wt_s.shape, 1
        )
        wt_s[...] = jnp.where((flat >= top) & (flat < top + height), weight, wt_s[...])

    @pl.when(t == tiles - 1)
    def _():
        strips, rows_dev, _ = sci.shape
        pairs = [(sci_s.at[pl.ds(s * rows_dev, rows_dev)], sci.at[s]) for s in range(strips)]
        if part == 0:
            pairs += [(num_s.at[q], num_out.at[q]) for q in range(half)]
        else:
            for copy in brought:
                copy.wait()
            nhalf = nrow // 2
            whalf = wt_s.shape[0] // 2
            for i, order in enumerate(orders):
                for slots, out in zip(slot_order(epochs, order), outs[2 * i : 2 * i + 2]):
                    for place, j in enumerate(slots):
                        pairs.append((num_s.at[j, pl.ds(i * nhalf, nhalf)], out.at[place, pl.ds(0, nhalf)]))
                        pairs.append((wt_s.at[pl.ds(i * whalf, whalf)], out.at[place, pl.ds(nhalf, whalf)]))
        start_and_wait([pltpu.make_async_copy(a, b, sems.at[n]) for n, (a, b) in enumerate(pairs)])


def template_kernel(terms, *refs):
    term_refs, out_ref, pad_s = refs[:-2], refs[-2], refs[-1]
    strips, long, share = out_ref.shape
    rows_dev = long - 2 * HALO
    nrow = strips * rows_dev
    nhalf = nrow // 2
    whalf = nhalf // share
    edge = jnp.zeros((HALO, share), F32)
    pad_s[pl.ds(0, HALO), :] = edge
    pad_s[pl.ds(HALO + nrow, HALO), :] = edge
    for part in range(2):
        own = term_refs[part * terms : (part + 1) * terms]
        add = lambda place: functools.reduce(lambda a, b: a + b, [ref[0, place, :] for ref in own])
        weights = add(pl.ds(nhalf, whalf))
        for i in range(whalf):
            below = jnp.transpose(jnp.broadcast_to(weights[i : i + 1, :], (share, share)))
            pad_s[pl.ds(HALO + part * nhalf + i * share, share), :] = add(pl.ds(i * share, share)) / below
    for s in range(strips):
        out_ref[s] = pad_s[pl.ds(s * rows_dev, long), :]


def bands_kernel(psf_ref, toep_hi, toep_lo, band_ref):
    basis, _, ksize = psf_ref.shape
    margin = ksize // 2
    for k in range(basis):
        shape = (2 * LANES, LANES)
        tap = lax.broadcasted_iota(jnp.int32, shape, 0) - lax.broadcasted_iota(jnp.int32, shape, 1)
        tap = tap - (LANES // 2 - margin)
        value = jnp.zeros(shape, F32)
        for j in range(ksize):
            value = jnp.where(tap == j, psf_ref[k, 1, j], value)
        toep_hi[:, pl.ds(k * LANES, LANES)], toep_lo[:, pl.ds(k * LANES, LANES)] = split(value)
        shape = (LANES, LANES + 2 * HALO)
        tap = lax.broadcasted_iota(jnp.int32, shape, 1) - lax.broadcasted_iota(jnp.int32, shape, 0)
        tap = tap - (HALO - margin)
        value = jnp.zeros(shape, F32)
        for j in range(ksize):
            value = jnp.where(tap == j, psf_ref[k, 0, j], value)
        band_ref[k, pl.ds(0, LANES), :], band_ref[k, pl.ds(LANES, LANES), :] = split(value)


def match_kernel(geom, *refs):
    pieces, nrow, ncol = geom
    count = len(pieces)
    tile_refs = refs[:count]
    poly_ref, toep_hi, toep_lo, band_ref, sci_a, sci_b, out_ref, pad_s, row_s, sems = refs[count:]
    step = pl.program_id(0)
    tiles = pad_s.shape[0] - 2
    rows_dev = pad_s.shape[1] - 2 * HALO
    me = lax.axis_index("epoch")
    strip = lax.axis_index("strip")
    per_step = out_ref.shape[2] // LANES

    @pl.when(step == 0)
    def _():
        copies = []
        for ref, (slot, first, stride) in zip(tile_refs, pieces):
            place = first if slot is None else jnp.bitwise_xor(me, slot) + first
            for i in range(ref.shape[0]):
                copies.append(
                    pltpu.make_async_copy(ref.at[i], pad_s.at[1 + place + i * stride], sems.at[len(copies)])
                )
        for copy in copies:
            copy.start()
        pad_s[0] = jnp.zeros(pad_s.shape[1:], F32)
        pad_s[tiles + 1] = jnp.zeros(pad_s.shape[1:], F32)
        shape = (rows_dev, LANES)
        counter = (strip * rows_dev + lax.broadcasted_iota(jnp.int32, shape, 0)).astype(F32)
        u = (2.0 * counter + 1.0) / nrow - 1.0
        for k in range(2):
            p = [poly_ref[me, k, i] for i in range(6)]
            row_s[k, 0] = p[0] + u * (p[1] + p[3] * u)
            row_s[k, 1] = p[2] + p[4] * u
        for copy in copies:
            copy.wait()

    lane = lax.broadcasted_iota(jnp.int32, pad_s.shape[1:], 1)
    base = step * per_step
    shifted = []
    for m in range(per_step + 1):
        mixed = jnp.where(lane < LANES // 2, pad_s[base + m + 1], pad_s[base + m])
        shifted.append(split(pltpu.roll(mixed, LANES // 2, 1)))
    toep = (toep_hi[...], toep_lo[...])
    sci_refs = (sci_a, sci_b)
    for pair in range(per_step // 2):
        across = []
        for c in (2 * pair, 2 * pair + 1):
            window = tuple(
                jnp.concatenate([shifted[c][i], shifted[c + 1][i]], axis=1) for i in range(2)
            )
            across.append(dot3(window, toep))
        width = 2 * LANES
        cols = lax.broadcasted_iota(jnp.int32, (1, width), 1) + (base + 2 * pair) * LANES
        v = (2.0 * cols.astype(F32) + 1.0) / ncol - 1.0
        for part in range(rows_dev // LANES):
            total = sci_refs[pair][0, pl.ds(part * LANES, LANES), :]
            for k in range(2):
                both = jnp.concatenate(
                    [a[part * LANES : part * LANES + LANES + 2 * HALO, k * LANES : (k + 1) * LANES] for a in across],
                    axis=1,
                )
                hi, lo = split(both)
                wide = dot(band_ref[k], hi)
                done = wide[:LANES] + (wide[LANES:] + dot(band_ref[k, pl.ds(0, LANES), :], lo))
                place = pl.ds(part * LANES, LANES)
                one = jnp.concatenate([row_s[k, 0, place, :]] * 2, axis=1)
                two = jnp.concatenate([row_s[k, 1, place, :]] * 2, axis=1)
                coeff = one + v * (two + poly_ref[me, k, 5] * v)
                total = total - coeff * done
            out_ref[0, pl.ds(part * LANES, LANES), pl.ds(pair * width, width)] = total


def swap(value, axis, bit):
    count = lax.axis_size(axis)
    return lax.ppermute(value, axis, [(i, i ^ (1 << bit)) for i in range(count)])


def shards(
    raw_tiles, tile_kind, tile_invvar, tile_heights, row_interp, col_interp, psf_profiles, psf_poly
):
    strips, epochs = lax.axis_size("strip"), lax.axis_size("epoch")
    _, tiles, tile_rows, tile_cols = raw_tiles.shape
    _, blocks, _ = tile_heights.shape
    ncol, nrow = blocks * tile_cols, ROWS_DEV * strips
    sources = strips // blocks
    share = tile_cols // epochs
    bits = epochs.bit_length() - 1
    orders = (tuple(range(bits)), tuple(reversed(range(bits))))
    nhalf = nrow // 2
    wrows = nrow // share
    long_half = nhalf + wrows // 2
    smem = pl.BlockSpec(memory_space=pltpu.SMEM)
    hbm = pl.BlockSpec(memory_space=pl.ANY)
    vmem = pl.BlockSpec(memory_space=pltpu.VMEM)
    kinds = col_interp.shape[0]

    width = tile_cols // 2
    sci_shape = jax.ShapeDtypeStruct((strips, ROWS_DEV, width), F32)
    num_shape = jax.ShapeDtypeStruct((epochs // 2, nrow, share), F32)
    send_shape = jax.ShapeDtypeStruct((epochs // 2, long_half, share), F32)

    def warp(part, more, outs):
        once = pl.Buffered(1)
        return pl.pallas_call(
            functools.partial(warp_kernel, (epochs, nrow, share, orders), part),
            grid=(tiles,),
            in_specs=[
                smem,
                smem,
                smem,
                pl.BlockSpec((1, tile_rows, tile_cols), lambda t: (t, 0, 0)),
                pl.BlockSpec((kinds, tile_rows, tile_rows), lambda t: (0, 0, 0), pipeline_mode=once),
                pl.BlockSpec((kinds, width, tile_cols), lambda t: (0, part, 0), pipeline_mode=once),
            ]
            + [hbm] * len(more),
            out_specs=[hbm] * len(outs),
            out_shape=outs,
            scratch_shapes=[
                pltpu.VMEM((nrow, width), F32),
                pltpu.VMEM((epochs // 2 if part == 0 else epochs, nrow, share), F32),
            ]
            + ([pltpu.VMEM((wrows, share), F32)] if part else [])
            + [
                pltpu.VMEM((kinds, width, tile_cols), BF16),
                pltpu.VMEM((kinds, width, tile_cols), BF16),
                pltpu.SMEM((1,), jnp.int32),
                pltpu.SemaphoreType.DMA((strips + 4 * epochs,)),
            ]
            + ([pltpu.SemaphoreType.DMA((epochs // 2,))] if part else []),
            cost_estimate=pl.CostEstimate(flops=8_000_000_000, bytes_accessed=15_000_000, transcendentals=0),
        )(tile_kind, tile_heights, tile_invvar, raw_tiles[0], row_interp, col_interp, *more)

    sci_a, num_a = warp(0, [], [sci_shape, num_shape])
    got_a = lax.all_to_all(sci_a, "strip", split_axis=0, concat_axis=0, tiled=True)
    sci_b, keep_a, send_a, keep_b, send_b = warp(1, [num_a], [sci_shape] + [send_shape] * 4)

    terms = [[keep_a], [keep_b]]
    sends = [send_a, send_b]
    for i in range(bits):
        for part in range(2):
            terms[part].append(swap(sends[part], "epoch", orders[part][i]))
        left = epochs >> (i + 1)
        if left > 1:
            sends = [
                functools.reduce(lambda a, b: a + b, [t[left // 2 : left] for t in own]) for own in terms
            ]
    if sources > 1:
        fixed = []
        for own in terms:
            total = functools.reduce(lambda a, b: a + b, [t[:1] for t in own])
            around = total
            for k in range(1, sources):
                ring = [(i, i // sources * sources + (i + k) % sources) for i in range(strips)]
                around = around + lax.ppermute(total, "strip", ring)
            fixed.append([around])
        terms = fixed

    long = ROWS_DEV + 2 * HALO
    first_slot = pl.BlockSpec((1, long_half, share), lambda i: (0, 0, 0))
    strips_out = pl.pallas_call(
        functools.partial(template_kernel, len(terms[0])),
        grid=(1,),
        in_specs=[first_slot] * (2 * len(terms[0])),
        out_specs=pl.BlockSpec((strips, long, share), lambda i: (0, 0, 0)),
        out_shape=jax.ShapeDtypeStruct((strips, long, share), F32),
        scratch_shapes=[pltpu.VMEM((nrow + 2 * HALO, share), F32)],
        name="template",
        cost_estimate=pl.CostEstimate(flops=2_000_000, bytes_accessed=5_000_000, transcendentals=0),
    )(*terms[0], *terms[1])
    strips_out, got_a = lax.optimization_barrier((strips_out, got_a))
    mine = lax.all_to_all(strips_out, "strip", split_axis=0, concat_axis=0, tiled=True)
    sci_b, mine = lax.optimization_barrier((sci_b, mine))
    got_b = lax.all_to_all(sci_b, "strip", split_axis=0, concat_axis=0, tiled=True)
    if sources > 1:
        mine = mine[::sources]
        got_a = jnp.sum(got_a.reshape(blocks, sources, ROWS_DEV, width), axis=1)
        got_b = jnp.sum(got_b.reshape(blocks, sources, ROWS_DEV, width), axis=1)

    per_block = tile_cols // LANES
    if epochs == 4 and share == LANES:
        near = [swap(mine, "epoch", b) for b in range(2)]
        cut = blocks // 2
        far_low = swap(near[1][:cut], "epoch", 0)
        far_high = swap(near[0][cut:], "epoch", 1)
        arrays = [mine, near[0], near[1], far_low, far_high]
        pieces = [(0, 0, per_block), (1, 0, per_block), (2, 0, per_block), (3, 0, per_block), (3, cut * per_block, per_block)]
    else:
        slots = [mine]
        for b in range(bits):
            slots = slots + [swap(s, "epoch", b) for s in slots]
        me = lax.axis_index("epoch")
        every = jnp.take(jnp.stack(slots), jnp.bitwise_xor(jnp.arange(epochs), me), axis=0)
        flat = jnp.transpose(every, (1, 2, 0, 3)).reshape(blocks, long, per_block, LANES)
        arrays = [jnp.transpose(flat, (0, 2, 1, 3)).reshape(blocks * per_block, long, LANES)]
        pieces = [(None, 0, 1)]

    basis, _, _ = psf_profiles.shape
    toep_hi, toep_lo, band = pl.pallas_call(
        bands_kernel,
        in_specs=[smem],
        out_specs=[vmem] * 3,
        out_shape=[
            jax.ShapeDtypeStruct((2 * LANES, 2 * LANES), BF16),
            jax.ShapeDtypeStruct((2 * LANES, 2 * LANES), BF16),
            jax.ShapeDtypeStruct((basis, 2 * LANES, LANES + 2 * HALO), BF16),
        ],
        name="bands",
        cost_estimate=pl.CostEstimate(flops=10_000_000, bytes_accessed=500_000, transcendentals=0),
    )(psf_profiles)

    const = lambda b: (0, 0)
    sci_spec = pl.BlockSpec((1, ROWS_DEV, width), lambda b: (b, 0, 0))
    return pl.pallas_call(
        functools.partial(match_kernel, (pieces, nrow, ncol)),
        grid=(blocks,),
        in_specs=[hbm] * len(arrays)
        + [
            smem,
            pl.BlockSpec(toep_hi.shape, const),
            pl.BlockSpec(toep_lo.shape, const),
            pl.BlockSpec(band.shape, lambda b: (0, 0, 0)),
            sci_spec,
            sci_spec,
        ],
        out_specs=pl.BlockSpec((1, ROWS_DEV, tile_cols), lambda b: (0, 0, b)),
        out_shape=jax.ShapeDtypeStruct((1, ROWS_DEV, ncol), F32),
        scratch_shapes=[
            pltpu.VMEM((blocks * per_block + 2, long, LANES), F32),
            pltpu.VMEM((2, 2, ROWS_DEV, LANES), F32),
            pltpu.SemaphoreType.DMA((sum(a.shape[0] for a in arrays),)),
        ],
        name="match",
        cost_estimate=pl.CostEstimate(flops=15_000_000_000, bytes_accessed=15_000_000, transcendentals=0),
    )(*arrays, psf_poly, toep_hi, toep_lo, band, got_a, got_b)


def solution(mesh):
    in_specs = (
        P("epoch", "strip", None, None),
        P("epoch", "strip"),
        P("epoch", "strip"),
        P("epoch", None, None),
        P(),
        P(),
        P(),
        P(),
    )
    out_specs = P("epoch", "strip", None)

    return jax.shard_map(shards, mesh=mesh, in_specs=in_specs, out_specs=out_specs, check_vma=False)
```

```python
import functools

import jax
import jax.numpy as jnp
from jax import lax
from jax.experimental import pallas as pl
from jax.experimental.pallas import tpu as pltpu
from jax.sharding import PartitionSpec as P


ROWS_DEV = 256
HALO = 16
FIRST_PART = 3
LANES = 128
F32 = jnp.float32
BF16 = jnp.bfloat16


def split(x):
    hi = x.astype(BF16)
    lo = (x - hi.astype(F32)).astype(BF16)
    return hi, lo


def dot(a, b, trans_b=False):
    dims = (((1,), (1 if trans_b else 0,)), ((), ()))
    return lax.dot_general(a, b, dims, preferred_element_type=F32)


def dot3(a, b, trans_b=False):
    a_hi, a_lo = a
    b_hi, b_lo = b
    both = dot(jnp.concatenate([a_hi, a_lo], axis=0), b_hi, trans_b)
    rows = a_hi.shape[0]
    return both[:rows] + (both[rows:] + dot(a_hi, b_lo, trans_b))


def start_and_wait(copies):
    for copy in copies:
        copy.start()
    for copy in copies:
        copy.wait()


def slot_order(count, order):
    bits = len(order)
    key = lambda j: sum(((j >> order[i]) & 1) << (bits - 1 - i) for i in range(bits))
    slots = sorted(range(count), key=key)
    return slots[: count // 2], slots[count // 2 :]


def warp_kernel(
    geom, kind_ref, heights_ref, invvar_ref, raw_ref, rmat_ref, cmat_ref,
    sci_a, sci_b, keep_a, send_a, keep_b, send_b,
    sci_s, num_s, wt_s, chi_s, clo_s, top_s, sems,
):
    epochs, nrow, share, orders, tiles = geom
    step = pl.program_id(0)
    together, tile_rows, tile_cols = raw_ref.shape
    per_col = heights_ref.shape[2]
    span = tile_rows + 8
    me = lax.axis_index("epoch")
    first_tile = lax.axis_index("strip") * tiles
    block = lax.div(first_tile, per_col)
    offset_in = lax.rem(first_tile, per_col)

    @pl.when(step == 0)
    def _():
        top_s[0] = lax.fori_loop(
            0, offset_in, lambda i, total: total + heights_ref[0, block, i], jnp.int32(0)
        )

        def divide(i, carry):
            k = lax.div(i, 4)
            here = pl.ds(pl.multiple_of(lax.rem(i, 4) * (tile_cols // 4), tile_cols // 4), tile_cols // 4)
            chi_s[k, here, :], clo_s[k, here, :] = split(cmat_ref[k, here, :])
            return carry

        lax.fori_loop(0, 4 * cmat_ref.shape[0], divide, 0)
        if tiles != per_col:
            sci_s[...] = jnp.zeros_like(sci_s)
            num_s[...] = jnp.zeros_like(num_s)
            wt_s[...] = jnp.zeros_like(wt_s)

    def warped(i, top):
        t = step * together + i
        kind = kind_ref[0, t]
        height = heights_ref[0, block, offset_in + t]
        start = pl.multiple_of(jnp.minimum(lax.div(top, 8) * 8, nrow - span), 8)
        off = top - start
        across = dot3(split(raw_ref[i]), (chi_s[kind], clo_s[kind]), trans_b=True)
        live = lax.broadcasted_iota(jnp.int32, (tile_rows, tile_rows), 1) < height
        rows = jnp.concatenate(
            [jnp.where(live, rmat_ref[kind], 0.0), jnp.zeros((8, tile_rows), F32)], axis=0
        )
        return t, height, start, off, dot3(split(pltpu.roll(rows, off, 0)), split(across))

    top = top_s[0]
    results = []
    for i in range(together):
        results.append((top, warped(i, top)))
        top = top + results[-1][1][1]
    top_s[0] = top

    for top, (t, height, start, off, placed) in results:
        weight = invvar_ref[0, t]
        local = lax.broadcasted_iota(jnp.int32, (span, share), 0) - off
        own = (local >= 0) & (local < height)
        here = pl.ds(start, span)
        for q in range(epochs):
            columns = pl.ds(q * share, share)
            piece = placed[:, q * share : (q + 1) * share]
            slot = jnp.bitwise_xor(me, q)
            sci_s[here, columns] = jnp.where(own, piece, sci_s[here, columns])
            num_s[slot, here, :] = jnp.where(own, weight * piece, num_s[slot, here, :])
        flat = lax.broadcasted_iota(jnp.int32, wt_s.shape, 0) * share + lax.broadcasted_iota(
            jnp.int32, wt_s.shape, 1
        )
        wt_s[...] = jnp.where((flat >= top) & (flat < top + height), weight, wt_s[...])

    @pl.when(step == pl.num_programs(0) - 1)
    def _():
        strips, rows_a, _ = sci_a.shape
        rows_b = sci_b.shape[1]
        pairs = []
        nhalf = nrow // 2
        whalf = wt_s.shape[0] // 2
        for i, (order, outs) in enumerate(zip(orders, ((keep_a, send_a), (keep_b, send_b)))):
            for slots, out in zip(slot_order(epochs, order), outs):
                for place, j in enumerate(slots):
                    pairs.append((num_s.at[j, pl.ds(i * nhalf, nhalf)], out.at[place, pl.ds(0, nhalf)]))
                    pairs.append((wt_s.at[pl.ds(i * whalf, whalf)], out.at[place, pl.ds(nhalf, whalf)]))
        for s in range(strips):
            base = s * (rows_a + rows_b)
            pairs.append((sci_s.at[pl.ds(base, rows_a)], sci_a.at[s]))
            pairs.append((sci_s.at[pl.ds(base + rows_a, rows_b)], sci_b.at[s]))
        start_and_wait([pltpu.make_async_copy(a, b, sems.at[n]) for n, (a, b) in enumerate(pairs)])


def template_kernel(terms, *refs):
    term_refs, out_ref, pad_s = refs[:-2], refs[-2], refs[-1]
    strips, long, share = out_ref.shape
    rows_dev = long - 2 * HALO
    nrow = strips * rows_dev
    nhalf = nrow // 2
    whalf = nhalf // share
    edge = jnp.zeros((HALO, share), F32)
    pad_s[pl.ds(0, HALO), :] = edge
    pad_s[pl.ds(HALO + nrow, HALO), :] = edge
    for part in range(2):
        own = term_refs[part * terms : (part + 1) * terms]
        add = lambda place: functools.reduce(lambda a, b: a + b, [ref[0, place, :] for ref in own])
        weights = add(pl.ds(nhalf, whalf))
        for i in range(whalf):
            below = jnp.transpose(jnp.broadcast_to(weights[i : i + 1, :], (share, share)))
            pad_s[pl.ds(HALO + part * nhalf + i * share, share), :] = add(pl.ds(i * share, share)) / below
    for s in range(strips):
        out_ref[s] = pad_s[pl.ds(s * rows_dev, long), :]


def bands_kernel(psf_ref, toep_hi, toep_lo, band_ref):
    basis, _, ksize = psf_ref.shape
    margin = ksize // 2
    for k in range(basis):
        shape = (2 * LANES, LANES)
        tap = lax.broadcasted_iota(jnp.int32, shape, 0) - lax.broadcasted_iota(jnp.int32, shape, 1)
        tap = tap - (LANES // 2 - margin)
        value = jnp.zeros(shape, F32)
        for j in range(ksize):
            value = jnp.where(tap == j, psf_ref[k, 1, j], value)
        toep_hi[:, pl.ds(k * LANES, LANES)], toep_lo[:, pl.ds(k * LANES, LANES)] = split(value)
        shape = (LANES, LANES + 2 * HALO)
        tap = lax.broadcasted_iota(jnp.int32, shape, 1) - lax.broadcasted_iota(jnp.int32, shape, 0)
        tap = tap - (HALO - margin)
        value = jnp.zeros(shape, F32)
        for j in range(ksize):
            value = jnp.where(tap == j, psf_ref[k, 0, j], value)
        band_ref[k, pl.ds(0, LANES), :], band_ref[k, pl.ds(LANES, LANES), :] = split(value)


def match_kernel(geom, *refs):
    pieces, nrow, ncol = geom
    count = len(pieces)
    tile_refs = refs[:count]
    poly_ref, toep_hi, toep_lo, band_ref, out_ref, pad_s, row_s, sems = refs[count:]
    step = pl.program_id(0)
    tiles = pad_s.shape[0] - 2
    rows_dev = pad_s.shape[1] - 2 * HALO
    me = lax.axis_index("epoch")
    strip = lax.axis_index("strip")
    per_step = out_ref.shape[1] // LANES

    @pl.when(step == 0)
    def _():
        copies = []
        for ref, (slot, first, stride) in zip(tile_refs, pieces):
            place = first if slot is None else jnp.bitwise_xor(me, slot) + first
            for i in range(ref.shape[0]):
                copies.append(
                    pltpu.make_async_copy(ref.at[i], pad_s.at[1 + place + i * stride], sems.at[len(copies)])
                )
        for copy in copies:
            copy.start()
        pad_s[0] = jnp.zeros(pad_s.shape[1:], F32)
        pad_s[tiles + 1] = jnp.zeros(pad_s.shape[1:], F32)
        shape = (rows_dev, LANES)
        counter = (strip * rows_dev + lax.broadcasted_iota(jnp.int32, shape, 0)).astype(F32)
        u = (2.0 * counter + 1.0) / nrow - 1.0
        for k in range(2):
            p = [poly_ref[me, k, i] for i in range(6)]
            row_s[k, 0] = p[0] + u * (p[1] + p[3] * u)
            row_s[k, 1] = p[2] + p[4] * u
        for copy in copies:
            copy.wait()

    lane = lax.broadcasted_iota(jnp.int32, pad_s.shape[1:], 1)
    base = step * per_step
    shifted = []
    for m in range(per_step + 1):
        mixed = jnp.where(lane < LANES // 2, pad_s[base + m + 1], pad_s[base + m])
        shifted.append(split(pltpu.roll(mixed, LANES // 2, 1)))
    toep = (toep_hi[...], toep_lo[...])
    for pair in range(per_step // 2):
        across = []
        for c in (2 * pair, 2 * pair + 1):
            window = tuple(
                jnp.concatenate([shifted[c][i], shifted[c + 1][i]], axis=1) for i in range(2)
            )
            across.append(dot3(window, toep))
        width = 2 * LANES
        cols = lax.broadcasted_iota(jnp.int32, (1, width), 1) + (base + 2 * pair) * LANES
        v = (2.0 * cols.astype(F32) + 1.0) / ncol - 1.0
        for part in range(rows_dev // LANES):
            total = 0.0
            for k in range(2):
                both = jnp.concatenate(
                    [a[part * LANES : part * LANES + LANES + 2 * HALO, k * LANES : (k + 1) * LANES] for a in across],
                    axis=1,
                )
                hi, lo = split(both)
                wide = dot(band_ref[k], hi)
                done = wide[:LANES] + (wide[LANES:] + dot(band_ref[k, pl.ds(0, LANES), :], lo))
                place = pl.ds(part * LANES, LANES)
                one = jnp.concatenate([row_s[k, 0, place, :]] * 2, axis=1)
                two = jnp.concatenate([row_s[k, 1, place, :]] * 2, axis=1)
                coeff = one + v * (two + poly_ref[me, k, 5] * v)
                total = total + coeff * done
            out_ref[pl.ds(part * LANES, LANES), pl.ds(pair * width, width)] = total


def subtract_kernel(sci_a, sci_b, matched_ref, out_ref):
    rows = sci_a.shape[1]
    out_ref[0, pl.ds(0, rows), :] = sci_a[0] - matched_ref[pl.ds(0, rows), :]
    rest = pl.ds(rows, sci_b.shape[1])
    out_ref[0, rest, :] = sci_b[0] - matched_ref[rest, :]


def swap(value, axis, bit):
    count = lax.axis_size(axis)
    return lax.ppermute(value, axis, [(i, i ^ (1 << bit)) for i in range(count)])


def shards(
    raw_tiles, tile_kind, tile_invvar, tile_heights, row_interp, col_interp, psf_profiles, psf_poly
):
    strips, epochs = lax.axis_size("strip"), lax.axis_size("epoch")
    _, tiles, tile_rows, tile_cols = raw_tiles.shape
    _, blocks, _ = tile_heights.shape
    ncol, nrow = blocks * tile_cols, ROWS_DEV * strips
    sources = strips // blocks
    share = tile_cols // epochs
    bits = epochs.bit_length() - 1
    orders = (tuple(range(bits)), tuple(reversed(range(bits))))
    nhalf = nrow // 2
    wrows = nrow // share
    long_half = nhalf + wrows // 2
    smem = pl.BlockSpec(memory_space=pltpu.SMEM)
    hbm = pl.BlockSpec(memory_space=pl.ANY)
    vmem = pl.BlockSpec(memory_space=pltpu.VMEM)
    kinds = col_interp.shape[0]

    first_rows = ROWS_DEV * FIRST_PART // 8
    sci_shapes = [
        jax.ShapeDtypeStruct((strips, rows, tile_cols), F32) for rows in (first_rows, ROWS_DEV - first_rows)
    ]
    send_shape = jax.ShapeDtypeStruct((epochs // 2, long_half, share), F32)
    together = 2 if tiles % 2 == 0 else 1
    once = pl.Buffered(1)
    sci_a, sci_b, keep_a, send_a, keep_b, send_b = pl.pallas_call(
        functools.partial(warp_kernel, (epochs, nrow, share, orders, tiles)),
        grid=(tiles // together,),
        in_specs=[
            smem,
            smem,
            smem,
            pl.BlockSpec((together, tile_rows, tile_cols), lambda t: (t, 0, 0)),
            pl.BlockSpec((kinds, tile_rows, tile_rows), lambda t: (0, 0, 0), pipeline_mode=once),
            pl.BlockSpec((kinds, tile_cols, tile_cols), lambda t: (0, 0, 0), pipeline_mode=once),
        ],
        out_specs=[hbm] * 6,
        out_shape=sci_shapes + [send_shape] * 4,
        scratch_shapes=[
            pltpu.VMEM((nrow, tile_cols), F32),
            pltpu.VMEM((epochs, nrow, share), F32),
            pltpu.VMEM((wrows, share), F32),
            pltpu.VMEM((kinds, tile_cols, tile_cols), BF16),
            pltpu.VMEM((kinds, tile_cols, tile_cols), BF16),
            pltpu.SMEM((1,), jnp.int32),
            pltpu.SemaphoreType.DMA((2 * strips + 4 * epochs,)),
        ],
        name="warp",
        cost_estimate=pl.CostEstimate(flops=8_000_000_000, bytes_accessed=20_000_000, transcendentals=0),
    )(tile_kind, tile_heights, tile_invvar, raw_tiles[0], row_interp, col_interp)

    got_a = lax.all_to_all(sci_a, "strip", split_axis=0, concat_axis=0, tiled=True)

    basis, _, _ = psf_profiles.shape
    build_bands = pl.pallas_call(
        bands_kernel,
        in_specs=[smem],
        out_specs=[vmem] * 3,
        out_shape=[
            jax.ShapeDtypeStruct((2 * LANES, 2 * LANES), BF16),
            jax.ShapeDtypeStruct((2 * LANES, 2 * LANES), BF16),
            jax.ShapeDtypeStruct((basis, 2 * LANES, LANES + 2 * HALO), BF16),
        ],
        name="bands",
        cost_estimate=pl.CostEstimate(flops=10_000_000, bytes_accessed=500_000, transcendentals=0),
    )
    toep_hi, toep_lo, band = build_bands(psf_profiles)

    terms = [[keep_a], [keep_b]]
    sends = [send_a, send_b]
    for i in range(bits):
        for part in range(2):
            terms[part].append(swap(sends[part], "epoch", orders[part][i]))
        left = epochs >> (i + 1)
        if left > 1:
            sends = [
                functools.reduce(lambda a, b: a + b, [t[left // 2 : left] for t in own]) for own in terms
            ]
    if sources > 1:
        fixed = []
        for own in terms:
            total = functools.reduce(lambda a, b: a + b, [t[:1] for t in own])
            around = total
            for k in range(1, sources):
                ring = [(i, i // sources * sources + (i + k) % sources) for i in range(strips)]
                around = around + lax.ppermute(total, "strip", ring)
            fixed.append([around])
        terms = fixed

    long = ROWS_DEV + 2 * HALO
    first_slot = pl.BlockSpec((1, long_half, share), lambda i: (0, 0, 0))
    strips_out = pl.pallas_call(
        functools.partial(template_kernel, len(terms[0])),
        grid=(1,),
        in_specs=[first_slot] * (2 * len(terms[0])),
        out_specs=pl.BlockSpec((strips, long, share), lambda i: (0, 0, 0)),
        out_shape=jax.ShapeDtypeStruct((strips, long, share), F32),
        scratch_shapes=[pltpu.VMEM((nrow + 2 * HALO, share), F32)],
        name="template",
        cost_estimate=pl.CostEstimate(flops=2_000_000, bytes_accessed=5_000_000, transcendentals=0),
    )(*terms[0], *terms[1])
    strips_out, got_a = lax.optimization_barrier((strips_out, got_a))
    mine = lax.all_to_all(strips_out, "strip", split_axis=0, concat_axis=0, tiled=True)
    sci_b, mine = lax.optimization_barrier((sci_b, mine))
    got_b = lax.all_to_all(sci_b, "strip", split_axis=0, concat_axis=0, tiled=True)
    if sources > 1:
        mine = mine[::sources]
        got_a = jnp.sum(got_a.reshape((blocks, sources) + got_a.shape[1:]), axis=1)
        got_b = jnp.sum(got_b.reshape((blocks, sources) + got_b.shape[1:]), axis=1)

    per_block = tile_cols // LANES
    if epochs == 4 and share == LANES:
        near = [swap(mine, "epoch", b) for b in range(2)]
        cut = blocks // 2
        far_low = swap(near[1][:cut], "epoch", 0)
        far_high = swap(near[0][cut:], "epoch", 1)
        arrays = [mine, near[0], near[1], far_low, far_high]
        pieces = [(0, 0, per_block), (1, 0, per_block), (2, 0, per_block), (3, 0, per_block), (3, cut * per_block, per_block)]
    else:
        slots = [mine]
        for b in range(bits):
            slots = slots + [swap(s, "epoch", b) for s in slots]
        me = lax.axis_index("epoch")
        every = jnp.take(jnp.stack(slots), jnp.bitwise_xor(jnp.arange(epochs), me), axis=0)
        flat = jnp.transpose(every, (1, 2, 0, 3)).reshape(blocks, long, per_block, LANES)
        arrays = [jnp.transpose(flat, (0, 2, 1, 3)).reshape(blocks * per_block, long, LANES)]
        pieces = [(None, 0, 1)]

    const = lambda b: (0, 0)
    convolve = pl.pallas_call(
        functools.partial(match_kernel, (pieces, nrow, ncol)),
        grid=(blocks,),
        in_specs=[hbm] * len(arrays)
        + [
            smem,
            pl.BlockSpec(toep_hi.shape, const),
            pl.BlockSpec(toep_lo.shape, const),
            pl.BlockSpec(band.shape, lambda b: (0, 0, 0)),
        ],
        out_specs=pl.BlockSpec((ROWS_DEV, tile_cols), lambda b: (0, b)),
        out_shape=jax.ShapeDtypeStruct((ROWS_DEV, ncol), F32),
        scratch_shapes=[
            pltpu.VMEM((blocks * per_block + 2, long, LANES), F32),
            pltpu.VMEM((2, 2, ROWS_DEV, LANES), F32),
            pltpu.SemaphoreType.DMA((sum(a.shape[0] for a in arrays),)),
        ],
        name="convolve",
        cost_estimate=pl.CostEstimate(flops=15_000_000_000, bytes_accessed=10_000_000, transcendentals=0),
    )
    matched = convolve(*arrays, psf_poly, toep_hi, toep_lo, band)
    return pl.pallas_call(
        subtract_kernel,
        grid=(blocks,),
        in_specs=[
            pl.BlockSpec((1,) + got_a.shape[1:], lambda b: (b, 0, 0)),
            pl.BlockSpec((1,) + got_b.shape[1:], lambda b: (b, 0, 0)),
            pl.BlockSpec((ROWS_DEV, tile_cols), lambda b: (0, b)),
        ],
        out_specs=pl.BlockSpec((1, ROWS_DEV, tile_cols), lambda b: (0, 0, b)),
        out_shape=jax.ShapeDtypeStruct((1, ROWS_DEV, ncol), F32),
        name="subtract",
        cost_estimate=pl.CostEstimate(flops=1_000_000, bytes_accessed=12_000_000, transcendentals=0),
    )(got_a, got_b, matched)


def solution(mesh):
    in_specs = (
        P("epoch", "strip", None, None),
        P("epoch", "strip"),
        P("epoch", "strip"),
        P("epoch", None, None),
        P(),
        P(),
        P(),
        P(),
    )
    out_specs = P("epoch", "strip", None)

    return jax.shard_map(shards, mesh=mesh, in_specs=in_specs, out_specs=out_specs, check_vma=False)
```

```python
import functools

import jax
import jax.numpy as jnp
from jax import lax
from jax.experimental import pallas as pl
from jax.experimental.pallas import tpu as pltpu
from jax.sharding import PartitionSpec as P


ROWS_DEV = 256
HALO = 16
FIRST_PART = 3
LANES = 128
F32 = jnp.float32
BF16 = jnp.bfloat16


def split(x):
    hi = x.astype(BF16)
    lo = (x - hi.astype(F32)).astype(BF16)
    return hi, lo


def dot(a, b, trans_b=False):
    dims = (((1,), (1 if trans_b else 0,)), ((), ()))
    return lax.dot_general(a, b, dims, preferred_element_type=F32)


def dot3(a, b, trans_b=False):
    a_hi, a_lo = a
    b_hi, b_lo = b
    both = dot(jnp.concatenate([a_hi, a_lo], axis=0), b_hi, trans_b)
    rows = a_hi.shape[0]
    return both[:rows] + (both[rows:] + dot(a_hi, b_lo, trans_b))


def start_and_wait(copies):
    for copy in copies:
        copy.start()
    for copy in copies:
        copy.wait()


def slot_order(count, order):
    bits = len(order)
    key = lambda j: sum(((j >> order[i]) & 1) << (bits - 1 - i) for i in range(bits))
    slots = sorted(range(count), key=key)
    return slots[: count // 2], slots[count // 2 :]


def warp_kernel(
    geom, kind_ref, heights_ref, invvar_ref, raw_ref, rmat_ref, cmat_ref,
    sci_a, sci_b, keep_a, send_a, keep_b, send_b,
    sci_s, num_s, wt_s, chi_s, clo_s, top_s, sems,
):
    epochs, nrow, share, orders, tiles = geom
    step = pl.program_id(0)
    together, tile_rows, tile_cols = raw_ref.shape
    per_col = heights_ref.shape[2]
    span = tile_rows + 8
    me = lax.axis_index("epoch")
    first_tile = lax.axis_index("strip") * tiles
    block = lax.div(first_tile, per_col)
    offset_in = lax.rem(first_tile, per_col)

    @pl.when(step == 0)
    def _():
        top_s[0] = lax.fori_loop(
            0, offset_in, lambda i, total: total + heights_ref[0, block, i], jnp.int32(0)
        )

        def divide(i, carry):
            k = lax.div(i, 4)
            here = pl.ds(pl.multiple_of(lax.rem(i, 4) * (tile_cols // 4), tile_cols // 4), tile_cols // 4)
            chi_s[k, here, :], clo_s[k, here, :] = split(cmat_ref[k, here, :])
            return carry

        lax.fori_loop(0, 4 * cmat_ref.shape[0], divide, 0)
        if tiles != per_col:
            sci_s[...] = jnp.zeros_like(sci_s)
            num_s[...] = jnp.zeros_like(num_s)
            wt_s[...] = jnp.zeros_like(wt_s)

    def warped(i, top):
        t = step * together + i
        kind = kind_ref[0, t]
        height = heights_ref[0, block, offset_in + t]
        start = pl.multiple_of(jnp.minimum(lax.div(top, 8) * 8, nrow - span), 8)
        off = top - start
        across = dot3(split(raw_ref[i]), (chi_s[kind], clo_s[kind]), trans_b=True)
        live = lax.broadcasted_iota(jnp.int32, (tile_rows, tile_rows), 1) < height
        rows = jnp.concatenate(
            [jnp.where(live, rmat_ref[kind], 0.0), jnp.zeros((8, tile_rows), F32)], axis=0
        )
        return t, height, start, off, dot3(split(pltpu.roll(rows, off, 0)), split(across))

    top = top_s[0]
    results = []
    for i in range(together):
        results.append((top, warped(i, top)))
        top = top + results[-1][1][1]
    top_s[0] = top

    for top, (t, height, start, off, placed) in results:
        weight = invvar_ref[0, t]
        local = lax.broadcasted_iota(jnp.int32, (span, share), 0) - off
        own = (local >= 0) & (local < height)
        here = pl.ds(start, span)
        for q in range(epochs):
            columns = pl.ds(q * share, share)
            piece = placed[:, q * share : (q + 1) * share]
            slot = jnp.bitwise_xor(me, q)
            sci_s[here, columns] = jnp.where(own, piece, sci_s[here, columns])
            num_s[slot, here, :] = jnp.where(own, weight * piece, num_s[slot, here, :])
        flat = lax.broadcasted_iota(jnp.int32, wt_s.shape, 0) * share + lax.broadcasted_iota(
            jnp.int32, wt_s.shape, 1
        )
        wt_s[...] = jnp.where((flat >= top) & (flat < top + height), weight, wt_s[...])

    @pl.when(step == pl.num_programs(0) - 1)
    def _():
        strips, rows_a, _ = sci_a.shape
        rows_b = sci_b.shape[1]
        pairs = []
        nhalf = nrow // 2
        whalf = wt_s.shape[0] // 2
        for i, (order, outs) in enumerate(zip(orders, ((keep_a, send_a), (keep_b, send_b)))):
            for slots, out in zip(slot_order(epochs, order), outs):
                for place, j in enumerate(slots):
                    pairs.append((num_s.at[j, pl.ds(i * nhalf, nhalf)], out.at[place, pl.ds(0, nhalf)]))
                    pairs.append((wt_s.at[pl.ds(i * whalf, whalf)], out.at[place, pl.ds(nhalf, whalf)]))
        for s in range(strips):
            base = s * (rows_a + rows_b)
            pairs.append((sci_s.at[pl.ds(base, rows_a)], sci_a.at[s]))
            pairs.append((sci_s.at[pl.ds(base + rows_a, rows_b)], sci_b.at[s]))
        start_and_wait([pltpu.make_async_copy(a, b, sems.at[n]) for n, (a, b) in enumerate(pairs)])


def template_kernel(terms, *refs):
    term_refs, out_refs, pad_s = refs[: 2 * terms], refs[2 * terms : -1], refs[-1]
    strips = len(out_refs)
    long, share = out_refs[0].shape
    rows_dev = long - 2 * HALO
    nrow = strips * rows_dev
    nhalf = nrow // 2
    whalf = nhalf // share
    edge = jnp.zeros((HALO, share), F32)
    pad_s[pl.ds(0, HALO), :] = edge
    pad_s[pl.ds(HALO + nrow, HALO), :] = edge
    for part in range(2):
        own = term_refs[part * terms : (part + 1) * terms]
        add = lambda place: functools.reduce(lambda a, b: a + b, [ref[0, place, :] for ref in own])
        weights = add(pl.ds(nhalf, whalf))
        for i in range(whalf):
            below = jnp.transpose(jnp.broadcast_to(weights[i : i + 1, :], (share, share)))
            pad_s[pl.ds(HALO + part * nhalf + i * share, share), :] = add(pl.ds(i * share, share)) / below
    for k in range(strips):
        strip = jnp.bitwise_xor(lax.axis_index("strip"), k)
        out_refs[k][...] = pad_s[pl.ds(pl.multiple_of(strip * rows_dev, rows_dev), long), :]


def bands_kernel(psf_ref, toep_hi, toep_lo, band_ref):
    basis, _, ksize = psf_ref.shape
    margin = ksize // 2
    for k in range(basis):
        shape = (2 * LANES, LANES)
        tap = lax.broadcasted_iota(jnp.int32, shape, 0) - lax.broadcasted_iota(jnp.int32, shape, 1)
        tap = tap - (LANES // 2 - margin)
        value = jnp.zeros(shape, F32)
        for j in range(ksize):
            value = jnp.where(tap == j, psf_ref[k, 1, j], value)
        toep_hi[:, pl.ds(k * LANES, LANES)], toep_lo[:, pl.ds(k * LANES, LANES)] = split(value)
        shape = (LANES, LANES + 2 * HALO)
        tap = lax.broadcasted_iota(jnp.int32, shape, 1) - lax.broadcasted_iota(jnp.int32, shape, 0)
        tap = tap - (HALO - margin)
        value = jnp.zeros(shape, F32)
        for j in range(ksize):
            value = jnp.where(tap == j, psf_ref[k, 0, j], value)
        band_ref[k, pl.ds(0, LANES), :], band_ref[k, pl.ds(LANES, LANES), :] = split(value)


def match_kernel(geom, *refs):
    pieces, nrow, ncol = geom
    count = len(pieces)
    tile_refs = refs[:count]
    poly_ref, toep_hi, toep_lo, band_ref, out_ref, pad_s, row_s, sems = refs[count:]
    step = pl.program_id(0)
    tiles = pad_s.shape[0] - 2
    rows_dev = pad_s.shape[1] - 2 * HALO
    me = lax.axis_index("epoch")
    strip = lax.axis_index("strip")
    per_step = out_ref.shape[1] // LANES

    @pl.when(step == 0)
    def _():
        copies = []
        for ref, (slot, first) in zip(tile_refs, pieces):
            for i in range(ref.shape[0]):
                if slot is None:
                    place = i
                else:
                    block = jnp.bitwise_xor(strip, first + i)
                    place = block * per_step + jnp.bitwise_xor(me, slot)
                copies.append(pltpu.make_async_copy(ref.at[i], pad_s.at[1 + place], sems.at[len(copies)]))
        for copy in copies:
            copy.start()
        pad_s[0] = jnp.zeros(pad_s.shape[1:], F32)
        pad_s[tiles + 1] = jnp.zeros(pad_s.shape[1:], F32)
        shape = (rows_dev, LANES)
        counter = (strip * rows_dev + lax.broadcasted_iota(jnp.int32, shape, 0)).astype(F32)
        u = (2.0 * counter + 1.0) / nrow - 1.0
        for k in range(2):
            p = [poly_ref[me, k, i] for i in range(6)]
            row_s[k, 0] = p[0] + u * (p[1] + p[3] * u)
            row_s[k, 1] = p[2] + p[4] * u
        for copy in copies:
            copy.wait()

    lane = lax.broadcasted_iota(jnp.int32, pad_s.shape[1:], 1)
    base = step * per_step
    shifted = []
    for m in range(per_step + 1):
        mixed = jnp.where(lane < LANES // 2, pad_s[base + m + 1], pad_s[base + m])
        shifted.append(split(pltpu.roll(mixed, LANES // 2, 1)))
    toep = (toep_hi[...], toep_lo[...])
    for pair in range(per_step // 2):
        across = []
        for c in (2 * pair, 2 * pair + 1):
            window = tuple(
                jnp.concatenate([shifted[c][i], shifted[c + 1][i]], axis=1) for i in range(2)
            )
            across.append(dot3(window, toep))
        width = 2 * LANES
        cols = lax.broadcasted_iota(jnp.int32, (1, width), 1) + (base + 2 * pair) * LANES
        v = (2.0 * cols.astype(F32) + 1.0) / ncol - 1.0
        for part in range(rows_dev // LANES):
            total = 0.0
            for k in range(2):
                both = jnp.concatenate(
                    [a[part * LANES : part * LANES + LANES + 2 * HALO, k * LANES : (k + 1) * LANES] for a in across],
                    axis=1,
                )
                hi, lo = split(both)
                wide = dot(band_ref[k], hi)
                done = wide[:LANES] + (wide[LANES:] + dot(band_ref[k, pl.ds(0, LANES), :], lo))
                place = pl.ds(part * LANES, LANES)
                one = jnp.concatenate([row_s[k, 0, place, :]] * 2, axis=1)
                two = jnp.concatenate([row_s[k, 1, place, :]] * 2, axis=1)
                coeff = one + v * (two + poly_ref[me, k, 5] * v)
                total = total + coeff * done
            out_ref[pl.ds(part * LANES, LANES), pl.ds(pair * width, width)] = total


def subtract_kernel(sci_a, sci_b, matched_ref, out_ref):
    b = pl.program_id(0)
    rows, width = sci_a.shape[1:]
    columns = pl.ds(pl.multiple_of(b * width, width), width)
    out_ref[0, pl.ds(0, rows), :] = sci_a[b] - matched_ref[pl.ds(0, rows), columns]
    rest = pl.ds(rows, sci_b.shape[1])
    out_ref[0, rest, :] = sci_b[b] - matched_ref[rest, columns]


def swap(value, axis, bit):
    count = lax.axis_size(axis)
    return lax.ppermute(value, axis, [(i, i ^ (1 << bit)) for i in range(count)])


def shards(
    raw_tiles, tile_kind, tile_invvar, tile_heights, row_interp, col_interp, psf_profiles, psf_poly
):
    strips, epochs = lax.axis_size("strip"), lax.axis_size("epoch")
    _, tiles, tile_rows, tile_cols = raw_tiles.shape
    _, blocks, _ = tile_heights.shape
    ncol, nrow = blocks * tile_cols, ROWS_DEV * strips
    sources = strips // blocks
    share = tile_cols // epochs
    bits = epochs.bit_length() - 1
    orders = (tuple(range(bits)), tuple(reversed(range(bits))))
    nhalf = nrow // 2
    wrows = nrow // share
    long_half = nhalf + wrows // 2
    smem = pl.BlockSpec(memory_space=pltpu.SMEM)
    hbm = pl.BlockSpec(memory_space=pl.ANY)
    vmem = pl.BlockSpec(memory_space=pltpu.VMEM)
    kinds = col_interp.shape[0]

    first_rows = ROWS_DEV * FIRST_PART // 8
    sci_shapes = [
        jax.ShapeDtypeStruct((strips, rows, tile_cols), F32) for rows in (first_rows, ROWS_DEV - first_rows)
    ]
    send_shape = jax.ShapeDtypeStruct((epochs // 2, long_half, share), F32)
    together = 2 if tiles % 2 == 0 else 1
    once = pl.Buffered(1)
    sci_a, sci_b, keep_a, send_a, keep_b, send_b = pl.pallas_call(
        functools.partial(warp_kernel, (epochs, nrow, share, orders, tiles)),
        grid=(tiles // together,),
        in_specs=[
            smem,
            smem,
            smem,
            pl.BlockSpec((together, tile_rows, tile_cols), lambda t: (t, 0, 0)),
            pl.BlockSpec((kinds, tile_rows, tile_rows), lambda t: (0, 0, 0), pipeline_mode=once),
            pl.BlockSpec((kinds, tile_cols, tile_cols), lambda t: (0, 0, 0), pipeline_mode=once),
        ],
        out_specs=[hbm] * 6,
        out_shape=sci_shapes + [send_shape] * 4,
        scratch_shapes=[
            pltpu.VMEM((nrow, tile_cols), F32),
            pltpu.VMEM((epochs, nrow, share), F32),
            pltpu.VMEM((wrows, share), F32),
            pltpu.VMEM((kinds, tile_cols, tile_cols), BF16),
            pltpu.VMEM((kinds, tile_cols, tile_cols), BF16),
            pltpu.SMEM((1,), jnp.int32),
            pltpu.SemaphoreType.DMA((2 * strips + 4 * epochs,)),
        ],
        name="warp",
        cost_estimate=pl.CostEstimate(flops=8_000_000_000, bytes_accessed=20_000_000, transcendentals=0),
    )(tile_kind, tile_heights, tile_invvar, raw_tiles[0], row_interp, col_interp)

    got_a = lax.all_to_all(sci_a, "strip", split_axis=0, concat_axis=0, tiled=True)

    basis, _, _ = psf_profiles.shape
    build_bands = pl.pallas_call(
        bands_kernel,
        in_specs=[smem],
        out_specs=[vmem] * 3,
        out_shape=[
            jax.ShapeDtypeStruct((2 * LANES, 2 * LANES), BF16),
            jax.ShapeDtypeStruct((2 * LANES, 2 * LANES), BF16),
            jax.ShapeDtypeStruct((basis, 2 * LANES, LANES + 2 * HALO), BF16),
        ],
        name="bands",
        cost_estimate=pl.CostEstimate(flops=10_000_000, bytes_accessed=500_000, transcendentals=0),
    )
    toep_hi, toep_lo, band = build_bands(psf_profiles)

    terms = [[keep_a], [keep_b]]
    sends = [send_a, send_b]
    for i in range(bits):
        for part in range(2):
            terms[part].append(swap(sends[part], "epoch", orders[part][i]))
        left = epochs >> (i + 1)
        if left > 1:
            sends = [
                functools.reduce(lambda a, b: a + b, [t[left // 2 : left] for t in own]) for own in terms
            ]
    if sources > 1:
        fixed = []
        for own in terms:
            total = functools.reduce(lambda a, b: a + b, [t[:1] for t in own])
            around = total
            for k in range(1, sources):
                ring = [(i, i // sources * sources + (i + k) % sources) for i in range(strips)]
                around = around + lax.ppermute(total, "strip", ring)
            fixed.append([around])
        terms = fixed

    long = ROWS_DEV + 2 * HALO
    parts = pl.pallas_call(
        functools.partial(template_kernel, len(terms[0])),
        in_specs=[vmem] * (2 * len(terms[0])),
        out_specs=[vmem] * strips,
        out_shape=[jax.ShapeDtypeStruct((long, share), F32)] * strips,
        scratch_shapes=[pltpu.VMEM((nrow + 2 * HALO, share), F32)],
        name="template",
        cost_estimate=pl.CostEstimate(flops=2_000_000, bytes_accessed=5_000_000, transcendentals=0),
    )(*terms[0], *terms[1])
    came = [None] * strips
    came[0] = parts[0]
    for k in reversed(range(1, strips)):
        came[k] = lax.ppermute(parts[k], "strip", [(i, i ^ k) for i in range(strips)])
    mine = jnp.stack(came[:: sources])
    sci_b, got_a = lax.optimization_barrier((sci_b, got_a))
    got_b = lax.all_to_all(sci_b, "strip", split_axis=0, concat_axis=0, tiled=True)
    if sources > 1:
        got_a = jnp.sum(got_a.reshape((blocks, sources) + got_a.shape[1:]), axis=1)
        got_b = jnp.sum(got_b.reshape((blocks, sources) + got_b.shape[1:]), axis=1)

    per_block = tile_cols // LANES
    if epochs == 4 and share == LANES:
        near = [swap(mine, "epoch", b) for b in range(2)]
        cut = blocks // 2
        far_low = swap(near[1][:cut], "epoch", 0)
        far_high = swap(near[0][cut:], "epoch", 1)
        arrays = [mine, near[0], near[1], far_low, far_high]
        pieces = [(0, 0), (1, 0), (2, 0), (3, 0), (3, cut)]
    else:
        slots = [mine]
        for b in range(bits):
            slots = slots + [swap(s, "epoch", b) for s in slots]
        me = lax.axis_index("epoch")
        every = jnp.take(jnp.stack(slots), jnp.bitwise_xor(jnp.arange(epochs), me), axis=0)
        home = lax.axis_index("strip") // sources
        every = jnp.take(every, jnp.bitwise_xor(jnp.arange(blocks), home), axis=1)
        flat = jnp.transpose(every, (1, 2, 0, 3)).reshape(blocks, long, per_block, LANES)
        arrays = [jnp.transpose(flat, (0, 2, 1, 3)).reshape(blocks * per_block, long, LANES)]
        pieces = [(None, 0)]

    const = lambda b: (0, 0)
    convolve = pl.pallas_call(
        functools.partial(match_kernel, (pieces, nrow, ncol)),
        grid=(blocks,),
        in_specs=[hbm] * len(arrays)
        + [
            smem,
            pl.BlockSpec(toep_hi.shape, const),
            pl.BlockSpec(toep_lo.shape, const),
            pl.BlockSpec(band.shape, lambda b: (0, 0, 0)),
        ],
        out_specs=pl.BlockSpec((ROWS_DEV, tile_cols), lambda b: (0, b)),
        out_shape=jax.ShapeDtypeStruct((ROWS_DEV, ncol), F32),
        scratch_shapes=[
            pltpu.VMEM((blocks * per_block + 2, long, LANES), F32),
            pltpu.VMEM((2, 2, ROWS_DEV, LANES), F32),
            pltpu.SemaphoreType.DMA((sum(a.shape[0] for a in arrays),)),
        ],
        name="convolve",
        cost_estimate=pl.CostEstimate(flops=15_000_000_000, bytes_accessed=10_000_000, transcendentals=0),
    )
    matched = convolve(*arrays, psf_poly, toep_hi, toep_lo, band)
    return pl.pallas_call(
        subtract_kernel,
        grid=(blocks,),
        in_specs=[vmem] * 3,
        out_specs=pl.BlockSpec((1, ROWS_DEV, tile_cols), lambda b: (0, 0, b)),
        out_shape=jax.ShapeDtypeStruct((1, ROWS_DEV, ncol), F32),
        name="subtract",
        cost_estimate=pl.CostEstimate(flops=1_000_000, bytes_accessed=12_000_000, transcendentals=0),
    )(got_a, got_b, matched)


def solution(mesh):
    in_specs = (
        P("epoch", "strip", None, None),
        P("epoch", "strip"),
        P("epoch", "strip"),
        P("epoch", None, None),
        P(),
        P(),
        P(),
        P(),
    )
    out_specs = P("epoch", "strip", None)

    return jax.shard_map(shards, mesh=mesh, in_specs=in_specs, out_specs=out_specs, check_vma=False)
```

```python
import functools

import jax
import jax.numpy as jnp
from jax import lax
from jax.experimental import pallas as pl
from jax.experimental.pallas import tpu as pltpu
from jax.sharding import PartitionSpec as P


ROWS_DEV = 256
HALO = 16
FIRST_PART = 3
LANES = 128
F32 = jnp.float32
BF16 = jnp.bfloat16


def split(x):
    hi = x.astype(BF16)
    lo = (x - hi.astype(F32)).astype(BF16)
    return hi, lo


def dot(a, b, trans_b=False):
    dims = (((1,), (1 if trans_b else 0,)), ((), ()))
    return lax.dot_general(a, b, dims, preferred_element_type=F32)


def dot3(a, b, trans_b=False):
    a_hi, a_lo = a
    b_hi, b_lo = b
    both = dot(jnp.concatenate([a_hi, a_lo], axis=0), b_hi, trans_b)
    rows = a_hi.shape[0]
    return both[:rows] + (both[rows:] + dot(a_hi, b_lo, trans_b))


def start_and_wait(copies):
    for copy in copies:
        copy.start()
    for copy in copies:
        copy.wait()


def slot_order(count, order):
    bits = len(order)
    key = lambda j: sum(((j >> order[i]) & 1) << (bits - 1 - i) for i in range(bits))
    slots = sorted(range(count), key=key)
    return slots[: count // 2], slots[count // 2 :]


def warp_kernel(
    geom, kind_ref, heights_ref, invvar_ref, raw_ref, rmat_ref, cmat_ref,
    sci_a, sci_b, keep_a, send_a, keep_b, send_b,
    sci_s, num_s, wt_s, chi_s, clo_s, top_s, sems,
):
    epochs, nrow, share, orders, tiles = geom
    step = pl.program_id(0)
    together, tile_rows, tile_cols = raw_ref.shape
    per_col = heights_ref.shape[2]
    span = tile_rows + 8
    me = lax.axis_index("epoch")
    first_tile = lax.axis_index("strip") * tiles
    block = lax.div(first_tile, per_col)
    offset_in = lax.rem(first_tile, per_col)

    @pl.when(step == 0)
    def _():
        top_s[0] = lax.fori_loop(
            0, offset_in, lambda i, total: total + heights_ref[0, block, i], jnp.int32(0)
        )

        def divide(i, carry):
            k = lax.div(i, 4)
            here = pl.ds(pl.multiple_of(lax.rem(i, 4) * (tile_cols // 4), tile_cols // 4), tile_cols // 4)
            chi_s[k, here, :], clo_s[k, here, :] = split(cmat_ref[k, here, :])
            return carry

        lax.fori_loop(0, 4 * cmat_ref.shape[0], divide, 0)
        if tiles != per_col:
            sci_s[...] = jnp.zeros_like(sci_s)
            num_s[...] = jnp.zeros_like(num_s)
            wt_s[...] = jnp.zeros_like(wt_s)

    def warped(i, top):
        t = step * together + i
        kind = kind_ref[0, t]
        height = heights_ref[0, block, offset_in + t]
        start = pl.multiple_of(jnp.minimum(lax.div(top, 8) * 8, nrow - span), 8)
        off = top - start
        across = dot3(split(raw_ref[i]), (chi_s[kind], clo_s[kind]), trans_b=True)
        live = lax.broadcasted_iota(jnp.int32, (tile_rows, tile_rows), 1) < height
        rows = jnp.concatenate(
            [jnp.where(live, rmat_ref[kind], 0.0), jnp.zeros((8, tile_rows), F32)], axis=0
        )
        return t, height, start, off, dot3(split(pltpu.roll(rows, off, 0)), split(across))

    top = top_s[0]
    results = []
    for i in range(together):
        results.append((top, warped(i, top)))
        top = top + results[-1][1][1]
    top_s[0] = top

    for top, (t, height, start, off, placed) in results:
        weight = invvar_ref[0, t]
        local = lax.broadcasted_iota(jnp.int32, (span, share), 0) - off
        own = (local >= 0) & (local < height)
        here = pl.ds(start, span)
        for q in range(epochs):
            columns = pl.ds(q * share, share)
            piece = placed[:, q * share : (q + 1) * share]
            slot = jnp.bitwise_xor(me, q)
            sci_s[here, columns] = jnp.where(own, piece, sci_s[here, columns])
            num_s[slot, here, :] = jnp.where(own, weight * piece, num_s[slot, here, :])
        flat = lax.broadcasted_iota(jnp.int32, wt_s.shape, 0) * share + lax.broadcasted_iota(
            jnp.int32, wt_s.shape, 1
        )
        wt_s[...] = jnp.where((flat >= top) & (flat < top + height), weight, wt_s[...])

    @pl.when(step == pl.num_programs(0) - 1)
    def _():
        strips, rows_a, _ = sci_a.shape
        rows_b = sci_b.shape[1]
        pairs = []
        nhalf = nrow // 2
        whalf = wt_s.shape[0] // 2
        for i, (order, outs) in enumerate(zip(orders, ((keep_a, send_a), (keep_b, send_b)))):
            for slots, out in zip(slot_order(epochs, order), outs):
                for place, j in enumerate(slots):
                    pairs.append((num_s.at[j, pl.ds(i * nhalf, nhalf)], out.at[place, pl.ds(0, nhalf)]))
                    pairs.append((wt_s.at[pl.ds(i * whalf, whalf)], out.at[place, pl.ds(nhalf, whalf)]))
        for s in range(strips):
            base = s * (rows_a + rows_b)
            pairs.append((sci_s.at[pl.ds(base, rows_a)], sci_a.at[s]))
            pairs.append((sci_s.at[pl.ds(base + rows_a, rows_b)], sci_b.at[s]))
        start_and_wait([pltpu.make_async_copy(a, b, sems.at[n]) for n, (a, b) in enumerate(pairs)])


def template_kernel(terms, *refs):
    term_refs, out_refs, pad_s = refs[: 2 * terms], refs[2 * terms : -1], refs[-1]
    strips = len(out_refs)
    long, share = out_refs[0].shape
    rows_dev = long - 2 * HALO
    nrow = strips * rows_dev
    nhalf = nrow // 2
    whalf = nhalf // share
    edge = jnp.zeros((HALO, share), F32)
    pad_s[pl.ds(0, HALO), :] = edge
    pad_s[pl.ds(HALO + nrow, HALO), :] = edge
    for part in range(2):
        own = term_refs[part * terms : (part + 1) * terms]
        add = lambda place: functools.reduce(lambda a, b: a + b, [ref[0, place, :] for ref in own])
        weights = add(pl.ds(nhalf, whalf))
        for i in range(whalf):
            below = jnp.transpose(jnp.broadcast_to(weights[i : i + 1, :], (share, share)))
            pad_s[pl.ds(HALO + part * nhalf + i * share, share), :] = add(pl.ds(i * share, share)) / below
    for k in range(strips):
        strip = jnp.bitwise_xor(lax.axis_index("strip"), k)
        out_refs[k][...] = pad_s[pl.ds(pl.multiple_of(strip * rows_dev, rows_dev), long), :]


def bands_kernel(psf_ref, toep_hi, toep_lo, band_ref):
    basis, _, ksize = psf_ref.shape
    margin = ksize // 2
    for k in range(basis):
        shape = (2 * LANES, LANES)
        tap = lax.broadcasted_iota(jnp.int32, shape, 0) - lax.broadcasted_iota(jnp.int32, shape, 1)
        tap = tap - (LANES // 2 - margin)
        value = jnp.zeros(shape, F32)
        for j in range(ksize):
            value = jnp.where(tap == j, psf_ref[k, 1, j], value)
        toep_hi[:, pl.ds(k * LANES, LANES)], toep_lo[:, pl.ds(k * LANES, LANES)] = split(value)
        shape = (LANES, LANES + 2 * HALO)
        tap = lax.broadcasted_iota(jnp.int32, shape, 1) - lax.broadcasted_iota(jnp.int32, shape, 0)
        tap = tap - (HALO - margin)
        value = jnp.zeros(shape, F32)
        for j in range(ksize):
            value = jnp.where(tap == j, psf_ref[k, 0, j], value)
        band_ref[k, pl.ds(0, LANES), :], band_ref[k, pl.ds(LANES, LANES), :] = split(value)


def match_kernel(geom, *refs):
    pieces, nrow, ncol = geom
    count = len(pieces)
    tile_refs = refs[:count]
    poly_ref, toep_hi, toep_lo, band_ref, out_ref, pad_s, row_s, sems = refs[count:]
    step = pl.program_id(0)
    tiles = pad_s.shape[0] - 2
    rows_dev = pad_s.shape[1] - 2 * HALO
    me = lax.axis_index("epoch")
    strip = lax.axis_index("strip")
    per_step = out_ref.shape[1] // LANES

    @pl.when(step == 0)
    def _():
        copies = []
        for ref, (slot, first) in zip(tile_refs, pieces):
            for i in range(ref.shape[0]):
                if slot is None:
                    place = i
                else:
                    block = jnp.bitwise_xor(strip, first + i)
                    place = block * per_step + jnp.bitwise_xor(me, slot)
                copies.append(pltpu.make_async_copy(ref.at[i], pad_s.at[1 + place], sems.at[len(copies)]))
        for copy in copies:
            copy.start()
        pad_s[0] = jnp.zeros(pad_s.shape[1:], F32)
        pad_s[tiles + 1] = jnp.zeros(pad_s.shape[1:], F32)
        shape = (rows_dev, LANES)
        counter = (strip * rows_dev + lax.broadcasted_iota(jnp.int32, shape, 0)).astype(F32)
        u = (2.0 * counter + 1.0) / nrow - 1.0
        for k in range(2):
            p = [poly_ref[me, k, i] for i in range(6)]
            row_s[k, 0] = p[0] + u * (p[1] + p[3] * u)
            row_s[k, 1] = p[2] + p[4] * u
        for copy in copies:
            copy.wait()

    lane = lax.broadcasted_iota(jnp.int32, pad_s.shape[1:], 1)
    base = step * per_step
    shifted = []
    for m in range(per_step + 1):
        mixed = jnp.where(lane < LANES // 2, pad_s[base + m + 1], pad_s[base + m])
        shifted.append(split(pltpu.roll(mixed, LANES // 2, 1)))
    toep = (toep_hi[...], toep_lo[...])
    for pair in range(per_step // 2):
        across = []
        for c in (2 * pair, 2 * pair + 1):
            window = tuple(
                jnp.concatenate([shifted[c][i], shifted[c + 1][i]], axis=1) for i in range(2)
            )
            across.append(dot3(window, toep))
        width = 2 * LANES
        cols = lax.broadcasted_iota(jnp.int32, (1, width), 1) + (base + 2 * pair) * LANES
        v = (2.0 * cols.astype(F32) + 1.0) / ncol - 1.0
        for part in range(rows_dev // LANES):
            total = 0.0
            for k in range(2):
                both = jnp.concatenate(
                    [a[part * LANES : part * LANES + LANES + 2 * HALO, k * LANES : (k + 1) * LANES] for a in across],
                    axis=1,
                )
                hi, lo = split(both)
                wide = dot(band_ref[k], hi)
                done = wide[:LANES] + (wide[LANES:] + dot(band_ref[k, pl.ds(0, LANES), :], lo))
                place = pl.ds(part * LANES, LANES)
                one = jnp.concatenate([row_s[k, 0, place, :]] * 2, axis=1)
                two = jnp.concatenate([row_s[k, 1, place, :]] * 2, axis=1)
                coeff = one + v * (two + poly_ref[me, k, 5] * v)
                total = total + coeff * done
            out_ref[pl.ds(part * LANES, LANES), pl.ds(pair * width, width)] = total


def subtract_kernel(sci_a, sci_b, matched_ref, out_ref):
    b = pl.program_id(0)
    rows, width = sci_a.shape[1:]
    columns = pl.ds(pl.multiple_of(b * width, width), width)
    out_ref[0, pl.ds(0, rows), :] = sci_a[b] - matched_ref[pl.ds(0, rows), columns]
    rest = pl.ds(rows, sci_b.shape[1])
    out_ref[0, rest, :] = sci_b[b] - matched_ref[rest, columns]


def swap(value, axis, bit):
    count = lax.axis_size(axis)
    return lax.ppermute(value, axis, [(i, i ^ (1 << bit)) for i in range(count)])


def shards(
    raw_tiles, tile_kind, tile_invvar, tile_heights, row_interp, col_interp, psf_profiles, psf_poly
):
    strips, epochs = lax.axis_size("strip"), lax.axis_size("epoch")
    _, tiles, tile_rows, tile_cols = raw_tiles.shape
    _, blocks, _ = tile_heights.shape
    ncol, nrow = blocks * tile_cols, ROWS_DEV * strips
    sources = strips // blocks
    share = tile_cols // epochs
    bits = epochs.bit_length() - 1
    orders = (tuple(range(bits)), tuple(reversed(range(bits))))
    nhalf = nrow // 2
    wrows = nrow // share
    long_half = nhalf + wrows // 2
    smem = pl.BlockSpec(memory_space=pltpu.SMEM)
    hbm = pl.BlockSpec(memory_space=pl.ANY)
    vmem = pl.BlockSpec(memory_space=pltpu.VMEM)
    kinds = col_interp.shape[0]

    first_rows = ROWS_DEV * FIRST_PART // 8
    sci_shapes = [
        jax.ShapeDtypeStruct((strips, rows, tile_cols), F32) for rows in (first_rows, ROWS_DEV - first_rows)
    ]
    send_shape = jax.ShapeDtypeStruct((epochs // 2, long_half, share), F32)
    together = 2 if tiles % 2 == 0 else 1
    once = pl.Buffered(1)
    sci_a, sci_b, keep_a, send_a, keep_b, send_b = pl.pallas_call(
        functools.partial(warp_kernel, (epochs, nrow, share, orders, tiles)),
        grid=(tiles // together,),
        in_specs=[
            smem,
            smem,
            smem,
            pl.BlockSpec((together, tile_rows, tile_cols), lambda t: (t, 0, 0)),
            pl.BlockSpec((kinds, tile_rows, tile_rows), lambda t: (0, 0, 0), pipeline_mode=once),
            pl.BlockSpec((kinds, tile_cols, tile_cols), lambda t: (0, 0, 0), pipeline_mode=once),
        ],
        out_specs=[hbm] * 6,
        out_shape=sci_shapes + [send_shape] * 4,
        scratch_shapes=[
            pltpu.VMEM((nrow, tile_cols), F32),
            pltpu.VMEM((epochs, nrow, share), F32),
            pltpu.VMEM((wrows, share), F32),
            pltpu.VMEM((kinds, tile_cols, tile_cols), BF16),
            pltpu.VMEM((kinds, tile_cols, tile_cols), BF16),
            pltpu.SMEM((1,), jnp.int32),
            pltpu.SemaphoreType.DMA((2 * strips + 4 * epochs,)),
        ],
        name="warp",
        cost_estimate=pl.CostEstimate(flops=8_000_000_000, bytes_accessed=20_000_000, transcendentals=0),
    )(tile_kind, tile_heights, tile_invvar, raw_tiles[0], row_interp, col_interp)

    got_a = lax.all_to_all(sci_a, "strip", split_axis=0, concat_axis=0, tiled=True)

    basis, _, _ = psf_profiles.shape
    build_bands = pl.pallas_call(
        bands_kernel,
        in_specs=[smem],
        out_specs=[vmem] * 3,
        out_shape=[
            jax.ShapeDtypeStruct((2 * LANES, 2 * LANES), BF16),
            jax.ShapeDtypeStruct((2 * LANES, 2 * LANES), BF16),
            jax.ShapeDtypeStruct((basis, 2 * LANES, LANES + 2 * HALO), BF16),
        ],
        name="bands",
        cost_estimate=pl.CostEstimate(flops=10_000_000, bytes_accessed=500_000, transcendentals=0),
    )
    toep_hi, toep_lo, band = build_bands(psf_profiles)

    terms = [[keep_a], [keep_b]]
    sends = [send_a, send_b]
    for i in range(bits):
        for part in range(2):
            terms[part].append(swap(sends[part], "epoch", orders[part][i]))
        left = epochs >> (i + 1)
        if left > 1:
            sends = [
                functools.reduce(lambda a, b: a + b, [t[left // 2 : left] for t in own]) for own in terms
            ]
    if sources > 1:
        fixed = []
        for own in terms:
            total = functools.reduce(lambda a, b: a + b, [t[:1] for t in own])
            around = total
            for k in range(1, sources):
                ring = [(i, i // sources * sources + (i + k) % sources) for i in range(strips)]
                around = around + lax.ppermute(total, "strip", ring)
            fixed.append([around])
        terms = fixed

    long = ROWS_DEV + 2 * HALO
    parts = pl.pallas_call(
        functools.partial(template_kernel, len(terms[0])),
        in_specs=[vmem] * (2 * len(terms[0])),
        out_specs=[vmem] * strips,
        out_shape=[jax.ShapeDtypeStruct((long, share), F32)] * strips,
        scratch_shapes=[pltpu.VMEM((nrow + 2 * HALO, share), F32)],
        name="template",
        cost_estimate=pl.CostEstimate(flops=2_000_000, bytes_accessed=5_000_000, transcendentals=0),
    )(*terms[0], *terms[1])
    came = [None] * strips
    came[0] = parts[0]
    for k in reversed(range(1, strips)):
        came[k] = lax.ppermute(parts[k], "strip", [(i, i ^ k) for i in range(strips)])
    mine = jnp.stack(came[:: sources])
    sci_b, got_a, mine = lax.optimization_barrier((sci_b, got_a, mine))
    got_b = lax.all_to_all(sci_b, "strip", split_axis=0, concat_axis=0, tiled=True)
    if sources > 1:
        got_a = jnp.sum(got_a.reshape((blocks, sources) + got_a.shape[1:]), axis=1)
        got_b = jnp.sum(got_b.reshape((blocks, sources) + got_b.shape[1:]), axis=1)

    per_block = tile_cols // LANES
    if epochs == 4 and share == LANES:
        near = []
        for b in range(2):
            near.append(swap(mine, "epoch", b))
        cut = blocks // 2
        far_low = swap(near[1][:cut], "epoch", 0)
        far_high = swap(near[0][cut:], "epoch", 1)
        arrays = [mine, near[0], near[1], far_low, far_high]
        pieces = [(0, 0), (1, 0), (2, 0), (3, 0), (3, cut)]
    else:
        slots = [mine]
        for b in range(bits):
            slots = slots + [swap(s, "epoch", b) for s in slots]
        me = lax.axis_index("epoch")
        every = jnp.take(jnp.stack(slots), jnp.bitwise_xor(jnp.arange(epochs), me), axis=0)
        home = lax.axis_index("strip") // sources
        every = jnp.take(every, jnp.bitwise_xor(jnp.arange(blocks), home), axis=1)
        flat = jnp.transpose(every, (1, 2, 0, 3)).reshape(blocks, long, per_block, LANES)
        arrays = [jnp.transpose(flat, (0, 2, 1, 3)).reshape(blocks * per_block, long, LANES)]
        pieces = [(None, 0)]

    const = lambda b: (0, 0)
    convolve = pl.pallas_call(
        functools.partial(match_kernel, (pieces, nrow, ncol)),
        grid=(blocks,),
        in_specs=[hbm] * len(arrays)
        + [
            smem,
            pl.BlockSpec(toep_hi.shape, const),
            pl.BlockSpec(toep_lo.shape, const),
            pl.BlockSpec(band.shape, lambda b: (0, 0, 0)),
        ],
        out_specs=pl.BlockSpec((ROWS_DEV, tile_cols), lambda b: (0, b)),
        out_shape=jax.ShapeDtypeStruct((ROWS_DEV, ncol), F32),
        scratch_shapes=[
            pltpu.VMEM((blocks * per_block + 2, long, LANES), F32),
            pltpu.VMEM((2, 2, ROWS_DEV, LANES), F32),
            pltpu.SemaphoreType.DMA((sum(a.shape[0] for a in arrays),)),
        ],
        name="convolve",
        cost_estimate=pl.CostEstimate(flops=15_000_000_000, bytes_accessed=10_000_000, transcendentals=0),
    )
    matched = convolve(*arrays, psf_poly, toep_hi, toep_lo, band)
    return pl.pallas_call(
        subtract_kernel,
        grid=(blocks,),
        in_specs=[vmem] * 3,
        out_specs=pl.BlockSpec((1, ROWS_DEV, tile_cols), lambda b: (0, 0, b)),
        out_shape=jax.ShapeDtypeStruct((1, ROWS_DEV, ncol), F32),
        name="subtract",
        cost_estimate=pl.CostEstimate(flops=1_000_000, bytes_accessed=12_000_000, transcendentals=0),
    )(got_a, got_b, matched)


def solution(mesh):
    in_specs = (
        P("epoch", "strip", None, None),
        P("epoch", "strip"),
        P("epoch", "strip"),
        P("epoch", None, None),
        P(),
        P(),
        P(),
        P(),
    )
    out_specs = P("epoch", "strip", None)

    return jax.shard_map(shards, mesh=mesh, in_specs=in_specs, out_specs=out_specs, check_vma=False)
```

```python
import functools

import jax
import jax.numpy as jnp
from jax import lax
from jax.experimental import pallas as pl
from jax.experimental.pallas import tpu as pltpu
from jax.sharding import PartitionSpec as P


ROWS_DEV = 256
HALO = 16
FIRST_PART = 3
LANES = 128
F32 = jnp.float32
BF16 = jnp.bfloat16


def split(x):
    hi = x.astype(BF16)
    lo = (x - hi.astype(F32)).astype(BF16)
    return hi, lo


def dot(a, b, trans_b=False):
    dims = (((1,), (1 if trans_b else 0,)), ((), ()))
    return lax.dot_general(a, b, dims, preferred_element_type=F32)


def dot3(a, b, trans_b=False):
    a_hi, a_lo = a
    b_hi, b_lo = b
    both = dot(jnp.concatenate([a_hi, a_lo], axis=0), b_hi, trans_b)
    rows = a_hi.shape[0]
    return both[:rows] + (both[rows:] + dot(a_hi, b_lo, trans_b))


def start_and_wait(copies):
    for copy in copies:
        copy.start()
    for copy in copies:
        copy.wait()


def slot_order(count, order):
    bits = len(order)
    key = lambda j: sum(((j >> order[i]) & 1) << (bits - 1 - i) for i in range(bits))
    slots = sorted(range(count), key=key)
    return slots[: count // 2], slots[count // 2 :]


def warp_kernel(
    geom, kind_ref, heights_ref, invvar_ref, raw_ref, rmat_ref, cmat_ref,
    sci_a, sci_b, keep_a, send_a, keep_b, send_b,
    sci_s, num_s, wt_s, rmat_s, cmat_s, chi_s, clo_s, top_s, ready_s, fetch_sems, sems, wt_sems,
):
    epochs, nrow, share, orders, tiles = geom
    step = pl.program_id(0)
    together, tile_rows, tile_cols = raw_ref.shape
    last = pl.num_programs(0) - 1
    per_col = heights_ref.shape[2]
    span = tile_rows + 8
    me = lax.axis_index("epoch")
    first_tile = lax.axis_index("strip") * tiles
    block = lax.div(first_tile, per_col)
    offset_in = lax.rem(first_tile, per_col)
    kinds = cmat_ref.shape[0]
    strips, rows_a, _ = sci_a.shape
    rows_dev = rows_a + sci_b.shape[1]
    nhalf = nrow // 2
    outs = (keep_a, send_a), (keep_b, send_b)

    def fetches(k):
        return [
            pltpu.make_async_copy(cmat_ref.at[k], cmat_s.at[k], fetch_sems.at[k, 0]),
            pltpu.make_async_copy(rmat_ref.at[k], rmat_s.at[k], fetch_sems.at[k, 1]),
        ]

    def strip_copies(s):
        base = s * rows_dev
        part = base // nhalf
        pairs = [
            (sci_s.at[pl.ds(base, rows_a)], sci_a.at[s]),
            (sci_s.at[pl.ds(base + rows_a, rows_dev - rows_a)], sci_b.at[s]),
        ]
        for slots, out in zip(slot_order(epochs, orders[part]), outs[part]):
            for place, j in enumerate(slots):
                pairs.append(
                    (num_s.at[j, pl.ds(base, rows_dev)], out.at[place, pl.ds(base - part * nhalf, rows_dev)])
                )
        return [pltpu.make_async_copy(a, b, sems.at[s, n]) for n, (a, b) in enumerate(pairs)]

    @pl.when(step == 0)
    def _():
        top_s[0] = lax.fori_loop(
            0, offset_in, lambda i, total: total + heights_ref[0, block, i], jnp.int32(0)
        )
        top_s[1] = 0
        first = kind_ref[0, 0]
        for i in range(kinds):
            ready_s[i] = 0
            for copy in fetches(lax.rem(first + i, kinds)):
                copy.start()
        if tiles != per_col:
            sci_s[...] = jnp.zeros_like(sci_s)
            num_s[...] = jnp.zeros_like(num_s)
            wt_s[...] = jnp.zeros_like(wt_s)

    def warped(i, top):
        t = step * together + i
        kind = kind_ref[0, t]
        height = heights_ref[0, block, offset_in + t]
        start = pl.multiple_of(jnp.minimum(lax.div(top, 8) * 8, nrow - span), 8)
        off = top - start
        across = dot3(split(raw_ref[i]), (chi_s[kind], clo_s[kind]), trans_b=True)
        live = lax.broadcasted_iota(jnp.int32, (tile_rows, tile_rows), 1) < height
        rows = jnp.concatenate(
            [jnp.where(live, rmat_s[kind], 0.0), jnp.zeros((8, tile_rows), F32)], axis=0
        )
        return t, height, start, off, dot3(split(pltpu.roll(rows, off, 0)), split(across))

    for i in range(together):
        kind = kind_ref[0, step * together + i]

        @pl.when(ready_s[kind] == 0)
        def _():
            for copy in fetches(kind):
                copy.wait()
            ready_s[kind] = 1

            def divide(n, carry):
                here = pl.ds(pl.multiple_of(n * (tile_cols // 8), tile_cols // 8), tile_cols // 8)
                chi_s[kind, here, :], clo_s[kind, here, :] = split(cmat_s[kind, here, :])
                return carry

            lax.fori_loop(0, 8, divide, 0)

    top = top_s[0]
    results = []
    for i in range(together):
        results.append((top, warped(i, top)))
        top = top + results[-1][1][1]
    top_s[0] = top
    after = top

    for top, (t, height, start, off, placed) in results:
        weight = invvar_ref[0, t]
        local = lax.broadcasted_iota(jnp.int32, (span, share), 0) - off
        own = (local >= 0) & (local < height)
        here = pl.ds(start, span)
        for q in range(epochs):
            columns = pl.ds(q * share, share)
            piece = placed[:, q * share : (q + 1) * share]
            slot = jnp.bitwise_xor(me, q)
            sci_s[here, columns] = jnp.where(own, piece, sci_s[here, columns])
            num_s[slot, here, :] = jnp.where(own, weight * piece, num_s[slot, here, :])
        flat = lax.broadcasted_iota(jnp.int32, wt_s.shape, 0) * share + lax.broadcasted_iota(
            jnp.int32, wt_s.shape, 1
        )
        wt_s[...] = jnp.where((flat >= top) & (flat < top + height), weight, wt_s[...])

    before = top_s[1]
    final = jnp.where(step == last, nrow, jnp.minimum(lax.div(after, 8) * 8, nrow - span))
    top_s[1] = final
    for s in range(strips):
        end = (s + 1) * rows_dev

        @pl.when((before < end) & (end <= final))
        def _():
            for copy in strip_copies(s):
                copy.start()

    @pl.when(step == last)
    def _():
        whalf = wt_s.shape[0] // 2
        copies = []
        for part, order in enumerate(orders):
            for slots, out in zip(slot_order(epochs, order), outs[part]):
                for place in range(len(slots)):
                    copies.append(
                        pltpu.make_async_copy(
                            wt_s.at[pl.ds(part * whalf, whalf)],
                            out.at[place, pl.ds(nhalf, whalf)],
                            wt_sems.at[len(copies)],
                        )
                    )
        start_and_wait(copies)
        for s in range(strips):
            for copy in strip_copies(s):
                copy.wait()
        for k in range(kinds):

            @pl.when(ready_s[k] == 0)
            def _():
                for copy in fetches(k):
                    copy.wait()


def template_kernel(terms, *refs):
    term_refs, out_refs, pad_s = refs[: 2 * terms], refs[2 * terms : -1], refs[-1]
    strips = len(out_refs)
    long, share = out_refs[0].shape
    rows_dev = long - 2 * HALO
    nrow = strips * rows_dev
    nhalf = nrow // 2
    whalf = nhalf // share
    edge = jnp.zeros((HALO, share), F32)
    pad_s[pl.ds(0, HALO), :] = edge
    pad_s[pl.ds(HALO + nrow, HALO), :] = edge
    for part in range(2):
        own = term_refs[part * terms : (part + 1) * terms]
        add = lambda place: functools.reduce(lambda a, b: a + b, [ref[0, place, :] for ref in own])
        weights = add(pl.ds(nhalf, whalf))
        for i in range(whalf):
            below = jnp.transpose(jnp.broadcast_to(weights[i : i + 1, :], (share, share)))
            pad_s[pl.ds(HALO + part * nhalf + i * share, share), :] = add(pl.ds(i * share, share)) / below
    for k in range(strips):
        strip = jnp.bitwise_xor(lax.axis_index("strip"), k)
        out_refs[k][...] = pad_s[pl.ds(pl.multiple_of(strip * rows_dev, rows_dev), long), :]


def bands_kernel(psf_ref, toep_hi, toep_lo, band_ref):
    basis, _, ksize = psf_ref.shape
    margin = ksize // 2
    for k in range(basis):
        shape = (2 * LANES, LANES)
        tap = lax.broadcasted_iota(jnp.int32, shape, 0) - lax.broadcasted_iota(jnp.int32, shape, 1)
        tap = tap - (LANES // 2 - margin)
        value = jnp.zeros(shape, F32)
        for j in range(ksize):
            value = jnp.where(tap == j, psf_ref[k, 1, j], value)
        toep_hi[:, pl.ds(k * LANES, LANES)], toep_lo[:, pl.ds(k * LANES, LANES)] = split(value)
        shape = (LANES, LANES + 2 * HALO)
        tap = lax.broadcasted_iota(jnp.int32, shape, 1) - lax.broadcasted_iota(jnp.int32, shape, 0)
        tap = tap - (HALO - margin)
        value = jnp.zeros(shape, F32)
        for j in range(ksize):
            value = jnp.where(tap == j, psf_ref[k, 0, j], value)
        band_ref[k, pl.ds(0, LANES), :], band_ref[k, pl.ds(LANES, LANES), :] = split(value)


def match_kernel(geom, *refs):
    slots, nrow, ncol = geom
    count = max(len(slots), 1) + (len(slots) > 1)
    tile_refs = refs[:count]
    poly_ref, toep_hi, toep_lo, band_ref, sci_ref, out_ref, pad_s, row_s, sems = refs[count:]
    step = pl.program_id(0)
    blocks = pl.num_programs(0)
    tiles = pad_s.shape[0] - 2
    rows_dev = pad_s.shape[1] - 2 * HALO
    me = lax.axis_index("epoch")
    strip = lax.axis_index("strip")
    per_step = out_ref.shape[1] // LANES

    def bring(b):
        if not slots:
            for i in range(per_step):
                place = b * per_step + i
                pltpu.make_async_copy(tile_refs[0].at[place], pad_s.at[1 + place], sems.at[b, i]).start()
            return
        at = jnp.bitwise_xor(strip, b)
        for n, slot in enumerate(slots):
            target = pad_s.at[1 + b * per_step + jnp.bitwise_xor(me, slot)]
            if n < len(slots) - 1:
                pltpu.make_async_copy(tile_refs[n].at[at], target, sems.at[b, n]).start()
                continue
            cut = tile_refs[n].shape[0]

            @pl.when(at < cut)
            def _():
                pltpu.make_async_copy(tile_refs[n].at[at], target, sems.at[b, n]).start()

            @pl.when(at >= cut)
            def _():
                pltpu.make_async_copy(tile_refs[n + 1].at[at - cut], target, sems.at[b, n]).start()

    def await_block(b):
        for i in range(per_step):
            pltpu.make_async_copy(tile_refs[0].at[0], pad_s.at[1], sems.at[b, i]).wait()

    @pl.when(step == 0)
    def _():
        for b in range(tiles // per_step):
            bring(b)
        pad_s[0] = jnp.zeros(pad_s.shape[1:], F32)
        pad_s[tiles + 1] = jnp.zeros(pad_s.shape[1:], F32)
        shape = (rows_dev, LANES)
        counter = (strip * rows_dev + lax.broadcasted_iota(jnp.int32, shape, 0)).astype(F32)
        u = (2.0 * counter + 1.0) / nrow - 1.0
        for k in range(2):
            p = [poly_ref[me, k, i] for i in range(6)]
            row_s[k, 0] = p[0] + u * (p[1] + p[3] * u)
            row_s[k, 1] = p[2] + p[4] * u
        await_block(0)

    @pl.when(step < blocks - 1)
    def _():
        await_block(step + 1)

    lane = lax.broadcasted_iota(jnp.int32, pad_s.shape[1:], 1)
    base = step * per_step
    shifted = []
    for m in range(per_step + 1):
        mixed = jnp.where(lane < LANES // 2, pad_s[base + m + 1], pad_s[base + m])
        shifted.append(split(pltpu.roll(mixed, LANES // 2, 1)))
    toep = (toep_hi[...], toep_lo[...])
    for pair in range(per_step // 2):
        across = []
        for c in (2 * pair, 2 * pair + 1):
            window = tuple(
                jnp.concatenate([shifted[c][i], shifted[c + 1][i]], axis=1) for i in range(2)
            )
            across.append(dot3(window, toep))
        width = 2 * LANES
        cols = lax.broadcasted_iota(jnp.int32, (1, width), 1) + (base + 2 * pair) * LANES
        v = (2.0 * cols.astype(F32) + 1.0) / ncol - 1.0
        for part in range(rows_dev // LANES):
            total = 0.0
            for k in range(2):
                both = jnp.concatenate(
                    [a[part * LANES : part * LANES + LANES + 2 * HALO, k * LANES : (k + 1) * LANES] for a in across],
                    axis=1,
                )
                hi, lo = split(both)
                wide = dot(band_ref[k], hi)
                done = wide[:LANES] + (wide[LANES:] + dot(band_ref[k, pl.ds(0, LANES), :], lo))
                place = pl.ds(part * LANES, LANES)
                one = jnp.concatenate([row_s[k, 0, place, :]] * 2, axis=1)
                two = jnp.concatenate([row_s[k, 1, place, :]] * 2, axis=1)
                coeff = one + v * (two + poly_ref[me, k, 5] * v)
                total = total + coeff * done
            columns = pl.ds(pair * width, width)
            ready = min(max(sci_ref.shape[1] - part * LANES, 0), LANES)
            if ready:
                here = pl.ds(part * LANES, ready)
                out_ref[here, columns] = sci_ref[0, here, columns] - total[:ready]
            if ready < LANES:
                out_ref[pl.ds(part * LANES + ready, LANES - ready), columns] = total[ready:]


def subtract_kernel(sci_ref, matched_ref, out_ref):
    i = pl.program_id(0)
    blocks, _, width = sci_ref.shape
    rows = out_ref.shape[1]
    for b in range(blocks):
        columns = pl.ds(b * width, width)
        science = sci_ref[b, pl.ds(pl.multiple_of(i * rows, rows), rows), :]
        out_ref[0, :, columns] = science - matched_ref[0, :, columns]


def swap(value, axis, bit):
    count = lax.axis_size(axis)
    return lax.ppermute(value, axis, [(i, i ^ (1 << bit)) for i in range(count)])


def shards(
    raw_tiles, tile_kind, tile_invvar, tile_heights, row_interp, col_interp, psf_profiles, psf_poly
):
    strips, epochs = lax.axis_size("strip"), lax.axis_size("epoch")
    _, tiles, tile_rows, tile_cols = raw_tiles.shape
    _, blocks, _ = tile_heights.shape
    ncol, nrow = blocks * tile_cols, ROWS_DEV * strips
    sources = strips // blocks
    share = tile_cols // epochs
    bits = epochs.bit_length() - 1
    orders = (tuple(range(bits)), tuple(reversed(range(bits))))
    nhalf = nrow // 2
    wrows = nrow // share
    long_half = nhalf + wrows // 2
    smem = pl.BlockSpec(memory_space=pltpu.SMEM)
    hbm = pl.BlockSpec(memory_space=pl.ANY)
    vmem = pl.BlockSpec(memory_space=pltpu.VMEM)
    kinds = col_interp.shape[0]

    first_rows = ROWS_DEV * FIRST_PART // 8
    sci_shapes = [
        jax.ShapeDtypeStruct((strips, rows, tile_cols), F32) for rows in (first_rows, ROWS_DEV - first_rows)
    ]
    send_shape = jax.ShapeDtypeStruct((epochs // 2, long_half, share), F32)
    together = 2 if tiles % 2 == 0 else 1
    sci_a, sci_b, keep_a, send_a, keep_b, send_b = pl.pallas_call(
        functools.partial(warp_kernel, (epochs, nrow, share, orders, tiles)),
        grid=(tiles // together,),
        in_specs=[
            smem,
            smem,
            smem,
            pl.BlockSpec((together, tile_rows, tile_cols), lambda t: (t, 0, 0)),
            hbm,
            hbm,
        ],
        out_specs=[hbm] * 6,
        out_shape=sci_shapes + [send_shape] * 4,
        scratch_shapes=[
            pltpu.VMEM((nrow, tile_cols), F32),
            pltpu.VMEM((epochs, nrow, share), F32),
            pltpu.VMEM((wrows, share), F32),
            pltpu.VMEM((kinds, tile_rows, tile_rows), F32),
            pltpu.VMEM((kinds, tile_cols, tile_cols), F32),
            pltpu.VMEM((kinds, tile_cols, tile_cols), BF16),
            pltpu.VMEM((kinds, tile_cols, tile_cols), BF16),
            pltpu.SMEM((2,), jnp.int32),
            pltpu.SMEM((kinds,), jnp.int32),
            pltpu.SemaphoreType.DMA((kinds, 2)),
            pltpu.SemaphoreType.DMA((strips, 2 + epochs)),
            pltpu.SemaphoreType.DMA((2 * epochs,)),
        ],
        name="warp",
        cost_estimate=pl.CostEstimate(flops=8_000_000_000, bytes_accessed=20_000_000, transcendentals=0),
    )(tile_kind, tile_heights, tile_invvar, raw_tiles[0], row_interp, col_interp)

    got_a = lax.all_to_all(sci_a, "strip", split_axis=0, concat_axis=0, tiled=True)

    basis, _, _ = psf_profiles.shape
    build_bands = pl.pallas_call(
        bands_kernel,
        in_specs=[smem],
        out_specs=[vmem] * 3,
        out_shape=[
            jax.ShapeDtypeStruct((2 * LANES, 2 * LANES), BF16),
            jax.ShapeDtypeStruct((2 * LANES, 2 * LANES), BF16),
            jax.ShapeDtypeStruct((basis, 2 * LANES, LANES + 2 * HALO), BF16),
        ],
        name="bands",
        cost_estimate=pl.CostEstimate(flops=10_000_000, bytes_accessed=500_000, transcendentals=0),
    )
    toep_hi, toep_lo, band = build_bands(psf_profiles)

    terms = [[keep_a], [keep_b]]
    sends = [send_a, send_b]
    for i in range(bits):
        for part in range(2):
            terms[part].append(swap(sends[part], "epoch", orders[part][i]))
        left = epochs >> (i + 1)
        if left > 1:
            sends = [
                functools.reduce(lambda a, b: a + b, [t[left // 2 : left] for t in own]) for own in terms
            ]
    if sources > 1:
        fixed = []
        for own in terms:
            total = functools.reduce(lambda a, b: a + b, [t[:1] for t in own])
            around = total
            for k in range(1, sources):
                ring = [(i, i // sources * sources + (i + k) % sources) for i in range(strips)]
                around = around + lax.ppermute(total, "strip", ring)
            fixed.append([around])
        terms = fixed

    long = ROWS_DEV + 2 * HALO
    parts = pl.pallas_call(
        functools.partial(template_kernel, len(terms[0])),
        in_specs=[vmem] * (2 * len(terms[0])),
        out_specs=[vmem] * strips,
        out_shape=[jax.ShapeDtypeStruct((long, share), F32)] * strips,
        scratch_shapes=[pltpu.VMEM((nrow + 2 * HALO, share), F32)],
        name="template",
        cost_estimate=pl.CostEstimate(flops=2_000_000, bytes_accessed=5_000_000, transcendentals=0),
    )(*terms[0], *terms[1])
    came = [None] * strips
    came[0] = parts[0]
    for k in reversed(range(1, strips)):
        came[k] = lax.ppermute(parts[k], "strip", [(i, i ^ k) for i in range(strips)])
    mine = jnp.stack(came[:: sources])
    sci_b, got_a, mine = lax.optimization_barrier((sci_b, got_a, mine))
    got_b = lax.all_to_all(sci_b, "strip", split_axis=0, concat_axis=0, tiled=True)
    if sources > 1:
        got_a = jnp.sum(got_a.reshape((blocks, sources) + got_a.shape[1:]), axis=1)
        got_b = jnp.sum(got_b.reshape((blocks, sources) + got_b.shape[1:]), axis=1)

    per_block = tile_cols // LANES
    if epochs == 4 and share == LANES:
        near = []
        for b in range(2):
            near.append(swap(mine, "epoch", b))
        cut = blocks // 2
        far_low = swap(near[1][:cut], "epoch", 0)
        far_high = swap(near[0][cut:], "epoch", 1)
        arrays = [mine, near[0], near[1], far_low, far_high]
        held = (0, 1, 2, 3)
    else:
        slots = [mine]
        for b in range(bits):
            slots = slots + [swap(s, "epoch", b) for s in slots]
        me = lax.axis_index("epoch")
        every = jnp.take(jnp.stack(slots), jnp.bitwise_xor(jnp.arange(epochs), me), axis=0)
        home = lax.axis_index("strip") // sources
        every = jnp.take(every, jnp.bitwise_xor(jnp.arange(blocks), home), axis=1)
        flat = jnp.transpose(every, (1, 2, 0, 3)).reshape(blocks, long, per_block, LANES)
        arrays = [jnp.transpose(flat, (0, 2, 1, 3)).reshape(blocks * per_block, long, LANES)]
        held = ()

    const = lambda b: (0, 0)
    convolve = pl.pallas_call(
        functools.partial(match_kernel, (held, nrow, ncol)),
        grid=(blocks,),
        in_specs=[hbm] * len(arrays)
        + [
            smem,
            pl.BlockSpec(toep_hi.shape, const),
            pl.BlockSpec(toep_lo.shape, const),
            pl.BlockSpec(band.shape, lambda b: (0, 0, 0)),
            pl.BlockSpec((1,) + got_a.shape[1:], lambda b: (b, 0, 0)),
        ],
        out_specs=pl.BlockSpec((ROWS_DEV, tile_cols), lambda b: (0, b)),
        out_shape=jax.ShapeDtypeStruct((ROWS_DEV, ncol), F32),
        scratch_shapes=[
            pltpu.VMEM((blocks * per_block + 2, long, LANES), F32),
            pltpu.VMEM((2, 2, ROWS_DEV, LANES), F32),
            pltpu.SemaphoreType.DMA((blocks, per_block)),
        ],
        name="convolve",
        compiler_params=pltpu.CompilerParams(vmem_limit_bytes=32 << 20),
        cost_estimate=pl.CostEstimate(flops=15_000_000_000, bytes_accessed=10_000_000, transcendentals=0),
    )
    matched = convolve(*arrays, psf_poly, toep_hi, toep_lo, band, got_a)
    unit = ROWS_DEV // 8
    rest = pl.BlockSpec((1, unit, ncol), lambda i: (0, FIRST_PART + i, 0))
    return pl.pallas_call(
        subtract_kernel,
        grid=(8 - FIRST_PART,),
        in_specs=[vmem, rest],
        out_specs=rest,
        out_shape=jax.ShapeDtypeStruct((1, ROWS_DEV, ncol), F32),
        input_output_aliases={1: 0},
        name="subtract",
        compiler_params=pltpu.CompilerParams(vmem_limit_bytes=16 << 20),
        cost_estimate=pl.CostEstimate(flops=1_000_000, bytes_accessed=6_000_000, transcendentals=0),
    )(pltpu.with_memory_space_constraint(got_b, pltpu.VMEM), matched[None])


def solution(mesh):
    in_specs = (
        P("epoch", "strip", None, None),
        P("epoch", "strip"),
        P("epoch", "strip"),
        P("epoch", None, None),
        P(),
        P(),
        P(),
        P(),
    )
    out_specs = P("epoch", "strip", None)

    return jax.shard_map(shards, mesh=mesh, in_specs=in_specs, out_specs=out_specs, check_vma=False)
```

```python
import functools

import jax
import jax.numpy as jnp
from jax import lax
from jax.experimental import pallas as pl
from jax.experimental.pallas import tpu as pltpu
from jax.sharding import PartitionSpec as P


ROWS_DEV = 256
HALO = 16
EDGE = 96
LANES = 128
F32 = jnp.float32
BF16 = jnp.bfloat16


def split(x):
    hi = x.astype(BF16)
    lo = (x - hi.astype(F32)).astype(BF16)
    return hi, lo


def dot(a, b, trans_b=False):
    dims = (((1,), (1 if trans_b else 0,)), ((), ()))
    return lax.dot_general(a, b, dims, preferred_element_type=F32)


def dot3(a, b, trans_b=False):
    a_hi, a_lo = a
    b_hi, b_lo = b
    both = dot(jnp.concatenate([a_hi, a_lo], axis=0), b_hi, trans_b)
    rows = a_hi.shape[0]
    return both[:rows] + (both[rows:] + dot(a_hi, b_lo, trans_b))


def start_and_wait(copies):
    for copy in copies:
        copy.start()
    for copy in copies:
        copy.wait()


def slot_order(count, order):
    bits = len(order)
    key = lambda j: sum(((j >> order[i]) & 1) << (bits - 1 - i) for i in range(bits))
    slots = sorted(range(count), key=key)
    return slots[: count // 2], slots[count // 2 :]


def warp_kernel(
    geom, kind_ref, heights_ref, invvar_ref, raw_ref, rmat_ref, cmat_ref,
    sci_a, sci_b, keep_a, send_a, keep_b, send_b,
    sci_s, num_s, wt_s, rmat_s, cmat_s, chi_s, clo_s, top_s, ready_s, fetch_sems, sems, wt_sems,
):
    epochs, nrow, share, orders, tiles = geom
    step = pl.program_id(0)
    together, tile_rows, tile_cols = raw_ref.shape
    last = pl.num_programs(0) - 1
    per_col = heights_ref.shape[2]
    span = tile_rows + 8
    me = lax.axis_index("epoch")
    first_tile = lax.axis_index("strip") * tiles
    block = lax.div(first_tile, per_col)
    offset_in = lax.rem(first_tile, per_col)
    kinds = cmat_ref.shape[0]
    strips, rows_a, _ = sci_a.shape
    rows_b = sci_b.shape[1]
    edge = rows_b // 2
    rows_dev = rows_a + rows_b
    nhalf = nrow // 2
    bhalf = strips // 2 * rows_b
    outs = (keep_a, send_a), (keep_b, send_b)

    def fetches(k):
        return [
            pltpu.make_async_copy(cmat_ref.at[k], cmat_s.at[k], fetch_sems.at[k, 0]),
            pltpu.make_async_copy(rmat_ref.at[k], rmat_s.at[k], fetch_sems.at[k, 1]),
        ]

    def strip_copies(s):
        base = s * rows_dev
        part = base // nhalf
        pairs = [(sci_s.at[pl.ds(base + edge, rows_a)], sci_a.at[s])]
        for i in range(2):
            source = pl.ds(base + i * (rows_dev - edge), edge)
            pairs.append((sci_s.at[source], sci_b.at[s, pl.ds(i * edge, edge)]))
            target = pl.ds((s - part * (strips // 2)) * rows_b + i * edge, edge)
            for slots, out in zip(slot_order(epochs, orders[part]), outs[part]):
                for place, j in enumerate(slots):
                    pairs.append((num_s.at[j, source], out.at[place, target]))
        return [pltpu.make_async_copy(a, b, sems.at[s, n]) for n, (a, b) in enumerate(pairs)]

    @pl.when(step == 0)
    def _():
        top_s[0] = lax.fori_loop(
            0, offset_in, lambda i, total: total + heights_ref[0, block, i], jnp.int32(0)
        )
        top_s[1] = 0
        first = kind_ref[0, 0]
        for i in range(kinds):
            ready_s[i] = 0
            for copy in fetches(lax.rem(first + i, kinds)):
                copy.start()
        if tiles != per_col:
            sci_s[...] = jnp.zeros_like(sci_s)
            num_s[...] = jnp.zeros_like(num_s)
            wt_s[...] = jnp.zeros_like(wt_s)

    def warped(i, top):
        t = step * together + i
        kind = kind_ref[0, t]
        height = heights_ref[0, block, offset_in + t]
        start = pl.multiple_of(jnp.minimum(lax.div(top, 8) * 8, nrow - span), 8)
        off = top - start
        across = dot3(split(raw_ref[i]), (chi_s[kind], clo_s[kind]), trans_b=True)
        live = lax.broadcasted_iota(jnp.int32, (tile_rows, tile_rows), 1) < height
        rows = jnp.concatenate(
            [jnp.where(live, rmat_s[kind], 0.0), jnp.zeros((8, tile_rows), F32)], axis=0
        )
        return t, height, start, off, dot3(split(pltpu.roll(rows, off, 0)), split(across))

    for i in range(together):
        kind = kind_ref[0, step * together + i]

        @pl.when(ready_s[kind] == 0)
        def _():
            for copy in fetches(kind):
                copy.wait()
            ready_s[kind] = 1

            def divide(n, carry):
                here = pl.ds(pl.multiple_of(n * (tile_cols // 8), tile_cols // 8), tile_cols // 8)
                chi_s[kind, here, :], clo_s[kind, here, :] = split(cmat_s[kind, here, :])
                return carry

            lax.fori_loop(0, 8, divide, 0)

    top = top_s[0]
    results = []
    for i in range(together):
        results.append((top, warped(i, top)))
        top = top + results[-1][1][1]
    top_s[0] = top
    after = top

    for top, (t, height, start, off, placed) in results:
        weight = invvar_ref[0, t]
        local = lax.broadcasted_iota(jnp.int32, (span, share), 0) - off
        own = (local >= 0) & (local < height)
        here = pl.ds(start, span)
        for q in range(epochs):
            columns = pl.ds(q * share, share)
            piece = placed[:, q * share : (q + 1) * share]
            slot = jnp.bitwise_xor(me, q)
            sci_s[here, columns] = jnp.where(own, piece, sci_s[here, columns])
            num_s[slot, here, :] = jnp.where(own, weight * piece, num_s[slot, here, :])
        flat = lax.broadcasted_iota(jnp.int32, wt_s.shape, 0) * share + lax.broadcasted_iota(
            jnp.int32, wt_s.shape, 1
        )
        wt_s[...] = jnp.where((flat >= top) & (flat < top + height), weight, wt_s[...])

    before = top_s[1]
    final = jnp.where(step == last, nrow, jnp.minimum(lax.div(after, 8) * 8, nrow - span))
    top_s[1] = final
    for s in range(strips):
        end = (s + 1) * rows_dev

        @pl.when((before < end) & (end <= final))
        def _():
            for copy in strip_copies(s):
                copy.start()

    @pl.when(step == last)
    def _():
        whalf = wt_s.shape[0] // 2
        copies = []
        for part, order in enumerate(orders):
            for slots, out in zip(slot_order(epochs, order), outs[part]):
                for place in range(len(slots)):
                    copies.append(
                        pltpu.make_async_copy(
                            wt_s.at[pl.ds(part * whalf, whalf)],
                            out.at[place, pl.ds(bhalf, whalf)],
                            wt_sems.at[len(copies)],
                        )
                    )
        start_and_wait(copies)
        for s in range(strips):
            for copy in strip_copies(s):
                copy.wait()
        for k in range(kinds):

            @pl.when(ready_s[k] == 0)
            def _():
                for copy in fetches(k):
                    copy.wait()


def added(refs, place):
    return functools.reduce(lambda a, b: a + b, [ref[0, place, :] for ref in refs])


def upright(row, width):
    return jnp.transpose(jnp.broadcast_to(row, (width, width)))


def template_kernel(terms, *refs):
    term_refs, out_refs, pad_s = refs[: 2 * terms], refs[2 * terms : -1], refs[-1]
    strips = len(out_refs)
    long, share = out_refs[0].shape
    rows_b = long - 2 * HALO
    edge = rows_b // 2
    half = strips // 2
    total = strips * rows_b
    blank = jnp.zeros((HALO, share), F32)
    pad_s[pl.ds(0, HALO), :] = blank
    pad_s[pl.ds(HALO + total, HALO), :] = blank
    per_strip = ROWS_DEV // share
    for part in range(2):
        own = term_refs[part * terms : (part + 1) * terms]
        weights = added(own, pl.ds(half * rows_b, half * per_strip))
        for s in range(half):
            below = jnp.concatenate(
                [upright(weights[s * per_strip + i : s * per_strip + i + 1, :], share) for i in range(per_strip)],
                axis=0,
            )
            for i in range(2):
                first = s * rows_b + i * edge
                under = below[i * (ROWS_DEV - edge) : i * (ROWS_DEV - edge) + edge]
                pad_s[pl.ds(HALO + part * half * rows_b + first, edge), :] = added(own, pl.ds(first, edge)) / under
    for k in range(strips):
        strip = jnp.bitwise_xor(lax.axis_index("strip"), k)
        out_refs[k][...] = pad_s[pl.ds(pl.multiple_of(strip * rows_b, 8), long), :]


def weigh_kernel(geom, heights_ref, invvar_ref, sci_ref, *refs):
    epochs, orders, share = geom
    outs, num_s = refs[:4], refs[4]
    blocks, rows_a, _ = sci_ref.shape
    per_col = heights_ref.shape[2]
    tiles = invvar_ref.shape[1]
    sources = per_col // tiles
    me, strip = lax.axis_index("epoch"), lax.axis_index("strip")
    first = strip * ROWS_DEV + EDGE
    half = blocks // 2
    long = outs[0].shape[1]
    flat_shape = (long - half * rows_a, share)
    flat = lax.broadcasted_iota(jnp.int32, flat_shape, 0) * share + lax.broadcasted_iota(jnp.int32, flat_shape, 1)
    row = lax.broadcasted_iota(jnp.int32, (rows_a, share), 0) + first
    for part in range(2):
        wide = jnp.zeros(flat_shape, F32)
        for b in range(half):
            block = part * half + b
            sky = flat - b * rows_a
            mine = (sky >= 0) & (sky < rows_a)
            sky = sky + first
            weight = jnp.zeros((rows_a, share), F32)
            top = jnp.int32(0)
            for t in range(per_col):
                height = heights_ref[0, block, t]
                value = invvar_ref[jnp.bitwise_xor(block * sources + t // tiles, strip), t % tiles]
                weight = jnp.where((row >= top) & (row < top + height), value, weight)
                wide = jnp.where(mine & (sky >= top) & (sky < top + height), value, wide)
                top = top + height
            for q in range(epochs):
                piece = sci_ref[block, :, pl.ds(q * share, share)]
                num_s[jnp.bitwise_xor(me, q), pl.ds(b * rows_a, rows_a), :] = weight * piece
        for j in range(epochs):
            num_s[j, pl.ds(half * rows_a, flat_shape[0]), :] = wide
        for slots, out in zip(slot_order(epochs, orders[part]), outs[2 * part : 2 * part + 2]):
            for place, j in enumerate(slots):
                out[place] = num_s[j]


def middle_kernel(terms, *refs):
    term_refs, outer_refs, out_ref = refs[: 2 * terms], refs[2 * terms : -1], refs[-1]
    blocks, long, share = out_ref.shape
    above = EDGE + HALO
    rows_a = long - 2 * above
    home = lax.div(lax.axis_index("strip"), lax.axis_size("strip") // blocks)
    half = blocks // 2
    for k, ref in enumerate(outer_refs):
        out_ref[k, pl.ds(0, above), :] = ref[pl.ds(0, above), :]
        out_ref[k, pl.ds(above + rows_a, above), :] = ref[pl.ds(above, above), :]
    for part in range(2):
        own = term_refs[part * terms : (part + 1) * terms]
        weights = added(own, pl.ds(half * rows_a, own[0].shape[1] - half * rows_a))
        together = share // rows_a
        for n in range(half // together):
            below = upright(weights[n : n + 1, :], share)
            for i in range(together):
                b = n * together + i
                value = added(own, pl.ds(b * rows_a, rows_a)) / below[i * rows_a : (i + 1) * rows_a]
                out_ref[jnp.bitwise_xor(home, part * half + b), pl.ds(above, rows_a), :] = value


def bands_kernel(psf_ref, _, toep_hi, toep_lo, band_ref):
    basis, _, ksize = psf_ref.shape
    margin = ksize // 2
    for k in range(basis):
        shape = (2 * LANES, LANES)
        tap = lax.broadcasted_iota(jnp.int32, shape, 0) - lax.broadcasted_iota(jnp.int32, shape, 1)
        tap = tap - (LANES // 2 - margin)
        value = jnp.zeros(shape, F32)
        for j in range(ksize):
            value = jnp.where(tap == j, psf_ref[k, 1, j], value)
        toep_hi[:, pl.ds(k * LANES, LANES)], toep_lo[:, pl.ds(k * LANES, LANES)] = split(value)
        shape = (LANES, LANES + 2 * HALO)
        tap = lax.broadcasted_iota(jnp.int32, shape, 1) - lax.broadcasted_iota(jnp.int32, shape, 0)
        tap = tap - (HALO - margin)
        value = jnp.zeros(shape, F32)
        for j in range(ksize):
            value = jnp.where(tap == j, psf_ref[k, 0, j], value)
        band_ref[k, pl.ds(0, LANES), :], band_ref[k, pl.ds(LANES, LANES), :] = split(value)


def match_kernel(geom, *refs):
    slots, nrow, ncol = geom
    count = max(len(slots), 1) + (len(slots) > 1)
    tile_refs = refs[:count]
    poly_ref, toep_hi, toep_lo, band_ref, sci_ref, out_ref, pad_s, row_s, sems = refs[count:]
    step = pl.program_id(0)
    blocks = pl.num_programs(0)
    tiles = pad_s.shape[0] - 2
    rows_dev = pad_s.shape[1] - 2 * HALO
    me = lax.axis_index("epoch")
    strip = lax.axis_index("strip")
    per_step = out_ref.shape[1] // LANES

    def bring(b):
        if not slots:
            for i in range(per_step):
                place = b * per_step + i
                pltpu.make_async_copy(tile_refs[0].at[place], pad_s.at[1 + place], sems.at[b, i]).start()
            return
        at = jnp.bitwise_xor(strip, b)
        for n, slot in enumerate(slots):
            target = pad_s.at[1 + b * per_step + jnp.bitwise_xor(me, slot)]
            if n < len(slots) - 1:
                pltpu.make_async_copy(tile_refs[n].at[at], target, sems.at[b, n]).start()
                continue
            cut = tile_refs[n].shape[0]

            @pl.when(at < cut)
            def _():
                pltpu.make_async_copy(tile_refs[n].at[at], target, sems.at[b, n]).start()

            @pl.when(at >= cut)
            def _():
                pltpu.make_async_copy(tile_refs[n + 1].at[at - cut], target, sems.at[b, n]).start()

    def await_block(b):
        for i in range(per_step):
            pltpu.make_async_copy(tile_refs[0].at[0], pad_s.at[1], sems.at[b, i]).wait()

    @pl.when(step == 0)
    def _():
        for b in range(tiles // per_step):
            bring(b)
        pad_s[0] = jnp.zeros(pad_s.shape[1:], F32)
        pad_s[tiles + 1] = jnp.zeros(pad_s.shape[1:], F32)
        shape = (rows_dev, LANES)
        counter = (strip * rows_dev + lax.broadcasted_iota(jnp.int32, shape, 0)).astype(F32)
        u = (2.0 * counter + 1.0) / nrow - 1.0
        for k in range(2):
            p = [poly_ref[me, k, i] for i in range(6)]
            row_s[k, 0] = p[0] + u * (p[1] + p[3] * u)
            row_s[k, 1] = p[2] + p[4] * u
        await_block(0)

    @pl.when(step < blocks - 1)
    def _():
        await_block(step + 1)

    lane = lax.broadcasted_iota(jnp.int32, pad_s.shape[1:], 1)
    base = step * per_step
    shifted = []
    for m in range(per_step + 1):
        mixed = jnp.where(lane < LANES // 2, pad_s[base + m + 1], pad_s[base + m])
        shifted.append(split(pltpu.roll(mixed, LANES // 2, 1)))
    toep = (toep_hi[...], toep_lo[...])
    for pair in range(per_step // 2):
        across = []
        for c in (2 * pair, 2 * pair + 1):
            window = tuple(
                jnp.concatenate([shifted[c][i], shifted[c + 1][i]], axis=1) for i in range(2)
            )
            across.append(dot3(window, toep))
        width = 2 * LANES
        cols = lax.broadcasted_iota(jnp.int32, (1, width), 1) + (base + 2 * pair) * LANES
        v = (2.0 * cols.astype(F32) + 1.0) / ncol - 1.0
        for part in range(rows_dev // LANES):
            total = 0.0
            for k in range(2):
                both = jnp.concatenate(
                    [a[part * LANES : part * LANES + LANES + 2 * HALO, k * LANES : (k + 1) * LANES] for a in across],
                    axis=1,
                )
                hi, lo = split(both)
                wide = dot(band_ref[k], hi)
                done = wide[:LANES] + (wide[LANES:] + dot(band_ref[k, pl.ds(0, LANES), :], lo))
                place = pl.ds(part * LANES, LANES)
                one = jnp.concatenate([row_s[k, 0, place, :]] * 2, axis=1)
                two = jnp.concatenate([row_s[k, 1, place, :]] * 2, axis=1)
                coeff = one + v * (two + poly_ref[me, k, 5] * v)
                total = total + coeff * done
            columns = pl.ds(pair * width, width)
            low = min(max(EDGE - part * LANES, 0), LANES)
            high = min(max(rows_dev - EDGE - part * LANES, 0), LANES)
            for begin, end, final in ((0, low, False), (low, high, True), (high, LANES, False)):
                if begin == end:
                    continue
                piece = total[begin:end]
                if final:
                    own = pl.ds(part * LANES + begin - EDGE, end - begin)
                    piece = sci_ref[0, own, columns] - piece
                out_ref[pl.ds(part * LANES + begin, end - begin), columns] = piece


def subtract_kernel(sci_ref, matched_ref, out_ref):
    i = pl.program_id(0)
    blocks, _, width = sci_ref.shape
    rows = out_ref.shape[1]
    for b in range(blocks):
        columns = pl.ds(b * width, width)
        science = sci_ref[b, pl.ds(pl.multiple_of(i * rows, rows), rows), :]
        out_ref[0, :, columns] = science - matched_ref[0, :, columns]


def swap(value, axis, bit):
    count = lax.axis_size(axis)
    return lax.ppermute(value, axis, [(i, i ^ (1 << bit)) for i in range(count)])


def shards(
    raw_tiles, tile_kind, tile_invvar, tile_heights, row_interp, col_interp, psf_profiles, psf_poly
):
    strips, epochs = lax.axis_size("strip"), lax.axis_size("epoch")
    _, tiles, tile_rows, tile_cols = raw_tiles.shape
    _, blocks, _ = tile_heights.shape
    ncol, nrow = blocks * tile_cols, ROWS_DEV * strips
    sources = strips // blocks
    share = tile_cols // epochs
    bits = epochs.bit_length() - 1
    orders = (tuple(range(bits)), tuple(reversed(range(bits))))
    wrows = nrow // share
    rows_b = 2 * EDGE
    rows_a = ROWS_DEV - rows_b
    long_half = strips // 2 * rows_b + wrows // 2
    smem = pl.BlockSpec(memory_space=pltpu.SMEM)
    hbm = pl.BlockSpec(memory_space=pl.ANY)
    vmem = pl.BlockSpec(memory_space=pltpu.VMEM)
    kinds = col_interp.shape[0]

    sci_shapes = [jax.ShapeDtypeStruct((strips, rows, tile_cols), F32) for rows in (rows_a, rows_b)]
    send_shape = jax.ShapeDtypeStruct((epochs // 2, long_half, share), F32)
    together = 2 if tiles % 2 == 0 else 1
    sci_a, sci_b, keep_a, send_a, keep_b, send_b = pl.pallas_call(
        functools.partial(warp_kernel, (epochs, nrow, share, orders, tiles)),
        grid=(tiles // together,),
        in_specs=[
            smem,
            smem,
            smem,
            pl.BlockSpec((together, tile_rows, tile_cols), lambda t: (t, 0, 0)),
            hbm,
            hbm,
        ],
        out_specs=[hbm] * 6,
        out_shape=sci_shapes + [send_shape] * 4,
        scratch_shapes=[
            pltpu.VMEM((nrow, tile_cols), F32),
            pltpu.VMEM((epochs, nrow, share), F32),
            pltpu.VMEM((wrows, share), F32),
            pltpu.VMEM((kinds, tile_rows, tile_rows), F32),
            pltpu.VMEM((kinds, tile_cols, tile_cols), F32),
            pltpu.VMEM((kinds, tile_cols, tile_cols), BF16),
            pltpu.VMEM((kinds, tile_cols, tile_cols), BF16),
            pltpu.SMEM((2,), jnp.int32),
            pltpu.SMEM((kinds,), jnp.int32),
            pltpu.SemaphoreType.DMA((kinds, 2)),
            pltpu.SemaphoreType.DMA((strips, 3 + 2 * epochs)),
            pltpu.SemaphoreType.DMA((2 * epochs,)),
        ],
        name="warp",
        cost_estimate=pl.CostEstimate(flops=8_000_000_000, bytes_accessed=20_000_000, transcendentals=0),
    )(tile_kind, tile_heights, tile_invvar, raw_tiles[0], row_interp, col_interp)

    got_a = lax.all_to_all(sci_a, "strip", split_axis=0, concat_axis=0, tiled=True)
    invvars = tile_invvar
    for bit in range(strips.bit_length() - 1):
        invvars = jnp.concatenate([invvars, swap(invvars, "strip", bit)], axis=0)

    basis, _, _ = psf_profiles.shape
    build_bands = pl.pallas_call(
        bands_kernel,
        in_specs=[smem, smem],
        out_specs=[vmem] * 3,
        out_shape=[
            jax.ShapeDtypeStruct((2 * LANES, 2 * LANES), BF16),
            jax.ShapeDtypeStruct((2 * LANES, 2 * LANES), BF16),
            jax.ShapeDtypeStruct((basis, 2 * LANES, LANES + 2 * HALO), BF16),
        ],
        name="bands",
        cost_estimate=pl.CostEstimate(flops=10_000_000, bytes_accessed=500_000, transcendentals=0),
    )
    toep_hi, toep_lo, band = build_bands(psf_profiles, invvars)

    def reduced(keeps, sends):
        terms = [[keep] for keep in keeps]
        for i in range(bits):
            for part in range(2):
                terms[part].append(swap(sends[part], "epoch", orders[part][i]))
            left = epochs >> (i + 1)
            if left > 1:
                sends = [
                    functools.reduce(lambda a, b: a + b, [t[left // 2 : left] for t in own]) for own in terms
                ]
        return terms

    terms = reduced([keep_a, keep_b], [send_a, send_b])
    if sources > 1:
        fixed = []
        for own in terms:
            total = functools.reduce(lambda a, b: a + b, [t[:1] for t in own])
            around = total
            for k in range(1, sources):
                ring = [(i, i // sources * sources + (i + k) % sources) for i in range(strips)]
                around = around + lax.ppermute(total, "strip", ring)
            fixed.append([around])
        terms = fixed

    long = ROWS_DEV + 2 * HALO
    long_b = rows_b + 2 * HALO
    parts = pl.pallas_call(
        functools.partial(template_kernel, len(terms[0])),
        in_specs=[vmem] * (2 * len(terms[0])),
        out_specs=[vmem] * strips,
        out_shape=[jax.ShapeDtypeStruct((long_b, share), F32)] * strips,
        scratch_shapes=[pltpu.VMEM((strips * rows_b + 2 * HALO, share), F32)],
        name="template",
        cost_estimate=pl.CostEstimate(flops=2_000_000, bytes_accessed=5_000_000, transcendentals=0),
    )(*terms[0], *terms[1])
    came = [None] * strips
    came[0] = parts[0]
    for k in reversed(range(1, strips)):
        came[k] = lax.ppermute(parts[k], "strip", [(i, i ^ k) for i in range(strips)])
    side_a = got_a
    if sources > 1:
        side_a = jnp.sum(got_a.reshape((blocks, sources) + got_a.shape[1:]), axis=1)
    long_a = blocks // 2 * rows_a + 8 * pl.cdiv(blocks // 2 * rows_a, 8 * share)
    weighted_shape = jax.ShapeDtypeStruct((epochs // 2, long_a, share), F32)
    weigh = pl.pallas_call(
        functools.partial(weigh_kernel, (epochs, orders, share)),
        in_specs=[smem, smem, vmem],
        out_specs=[vmem] * 4,
        out_shape=[weighted_shape] * 4,
        scratch_shapes=[pltpu.VMEM((epochs, long_a, share), F32)],
        name="weigh",
        cost_estimate=pl.CostEstimate(flops=2_000_000, bytes_accessed=2_500_000, transcendentals=0),
    )
    weighted = weigh(tile_heights, invvars, side_a)
    middle_terms = reduced(weighted[0::2], weighted[1::2])
    outer = came[::sources]
    mine = pl.pallas_call(
        functools.partial(middle_kernel, len(middle_terms[0])),
        in_specs=[vmem] * (2 * len(middle_terms[0]) + blocks),
        out_specs=vmem,
        out_shape=jax.ShapeDtypeStruct((blocks, long, share), F32),
        name="middle",
        cost_estimate=pl.CostEstimate(flops=500_000, bytes_accessed=4_000_000, transcendentals=0),
    )(*middle_terms[0], *middle_terms[1], *outer)
    sci_b, got_a, mine = lax.optimization_barrier((sci_b, got_a, mine))
    got_b = lax.all_to_all(sci_b, "strip", split_axis=0, concat_axis=0, tiled=True)
    got_a = got_a if sources == 1 else side_a
    if sources > 1:
        got_b = jnp.sum(got_b.reshape((blocks, sources) + got_b.shape[1:]), axis=1)

    per_block = tile_cols // LANES
    if epochs == 4 and share == LANES:
        near = []
        for b in range(2):
            near.append(swap(mine, "epoch", b))
        cut = blocks // 2
        far_low = swap(near[1][:cut], "epoch", 0)
        far_high = swap(near[0][cut:], "epoch", 1)
        arrays = [mine, near[0], near[1], far_low, far_high]
        held = (0, 1, 2, 3)
    else:
        slots = [mine]
        for b in range(bits):
            slots = slots + [swap(s, "epoch", b) for s in slots]
        me = lax.axis_index("epoch")
        every = jnp.take(jnp.stack(slots), jnp.bitwise_xor(jnp.arange(epochs), me), axis=0)
        home = lax.axis_index("strip") // sources
        every = jnp.take(every, jnp.bitwise_xor(jnp.arange(blocks), home), axis=1)
        flat = jnp.transpose(every, (1, 2, 0, 3)).reshape(blocks, long, per_block, LANES)
        arrays = [jnp.transpose(flat, (0, 2, 1, 3)).reshape(blocks * per_block, long, LANES)]
        held = ()

    const = lambda b: (0, 0)
    convolve = pl.pallas_call(
        functools.partial(match_kernel, (held, nrow, ncol)),
        grid=(blocks,),
        in_specs=[hbm] * len(arrays)
        + [
            smem,
            pl.BlockSpec(toep_hi.shape, const),
            pl.BlockSpec(toep_lo.shape, const),
            pl.BlockSpec(band.shape, lambda b: (0, 0, 0)),
            pl.BlockSpec((1,) + got_a.shape[1:], lambda b: (b, 0, 0)),
        ],
        out_specs=pl.BlockSpec((ROWS_DEV, tile_cols), lambda b: (0, b)),
        out_shape=jax.ShapeDtypeStruct((ROWS_DEV, ncol), F32),
        scratch_shapes=[
            pltpu.VMEM((blocks * per_block + 2, long, LANES), F32),
            pltpu.VMEM((2, 2, ROWS_DEV, LANES), F32),
            pltpu.SemaphoreType.DMA((blocks, per_block)),
        ],
        name="convolve",
        compiler_params=pltpu.CompilerParams(vmem_limit_bytes=32 << 20),
        cost_estimate=pl.CostEstimate(flops=15_000_000_000, bytes_accessed=10_000_000, transcendentals=0),
    )
    matched = convolve(*arrays, psf_poly, toep_hi, toep_lo, band, got_a)
    unit = ROWS_DEV // 8
    outside = EDGE // unit
    rest = pl.BlockSpec(
        (1, unit, ncol), lambda i: (0, jnp.where(i < outside, i, i + rows_a // unit), 0)
    )
    return pl.pallas_call(
        subtract_kernel,
        grid=(2 * outside,),
        in_specs=[vmem, rest],
        out_specs=rest,
        out_shape=jax.ShapeDtypeStruct((1, ROWS_DEV, ncol), F32),
        input_output_aliases={1: 0},
        name="subtract",
        compiler_params=pltpu.CompilerParams(vmem_limit_bytes=16 << 20),
        cost_estimate=pl.CostEstimate(flops=1_000_000, bytes_accessed=6_000_000, transcendentals=0),
    )(pltpu.with_memory_space_constraint(got_b, pltpu.VMEM), matched[None])


def solution(mesh):
    in_specs = (
        P("epoch", "strip", None, None),
        P("epoch", "strip"),
        P("epoch", "strip"),
        P("epoch", None, None),
        P(),
        P(),
        P(),
        P(),
    )
    out_specs = P("epoch", "strip", None)

    return jax.shard_map(shards, mesh=mesh, in_specs=in_specs, out_specs=out_specs, check_vma=False)
```

```python
import functools

import jax
import jax.numpy as jnp
from jax import lax
from jax.experimental import pallas as pl
from jax.experimental.pallas import tpu as pltpu
from jax.sharding import PartitionSpec as P


ROWS_DEV = 256
HALO = 16
EDGE = 80
LANES = 128
F32 = jnp.float32
BF16 = jnp.bfloat16


def split(x):
    hi = x.astype(BF16)
    lo = (x - hi.astype(F32)).astype(BF16)
    return hi, lo


def dot(a, b, trans_b=False):
    dims = (((1,), (1 if trans_b else 0,)), ((), ()))
    return lax.dot_general(a, b, dims, preferred_element_type=F32)


def dot3(a, b, trans_b=False):
    a_hi, a_lo = a
    b_hi, b_lo = b
    both = dot(jnp.concatenate([a_hi, a_lo], axis=0), b_hi, trans_b)
    rows = a_hi.shape[0]
    return both[:rows] + (both[rows:] + dot(a_hi, b_lo, trans_b))


def start_and_wait(copies):
    for copy in copies:
        copy.start()
    for copy in copies:
        copy.wait()


def slot_order(count, order):
    bits = len(order)
    key = lambda j: sum(((j >> order[i]) & 1) << (bits - 1 - i) for i in range(bits))
    slots = sorted(range(count), key=key)
    return slots[: count // 2], slots[count // 2 :]


def warp_kernel(
    geom, kind_ref, heights_ref, invvar_ref, raw_ref, rmat_ref, cmat_ref,
    sci_a, sci_b, keep_a, send_a, keep_b, send_b,
    sci_s, num_s, wt_s, rmat_s, cmat_s, chi_s, clo_s, top_s, ready_s, fetch_sems, sems, wt_sems,
):
    epochs, nrow, share, orders, tiles = geom
    step = pl.program_id(0)
    together, tile_rows, tile_cols = raw_ref.shape
    last = pl.num_programs(0) - 1
    per_col = heights_ref.shape[2]
    span = tile_rows + 8
    me = lax.axis_index("epoch")
    first_tile = lax.axis_index("strip") * tiles
    block = lax.div(first_tile, per_col)
    offset_in = lax.rem(first_tile, per_col)
    kinds = cmat_ref.shape[0]
    strips, rows_a, _ = sci_a.shape
    rows_b = sci_b.shape[1]
    edge = rows_b // 2
    rows_dev = rows_a + rows_b
    nhalf = nrow // 2
    bhalf = strips // 2 * rows_b
    outs = (keep_a, send_a), (keep_b, send_b)

    def fetches(k):
        return [
            pltpu.make_async_copy(cmat_ref.at[k], cmat_s.at[k], fetch_sems.at[k, 0]),
            pltpu.make_async_copy(rmat_ref.at[k], rmat_s.at[k], fetch_sems.at[k, 1]),
        ]

    def strip_copies(s):
        base = s * rows_dev
        part = base // nhalf
        pairs = [(sci_s.at[pl.ds(base + edge, rows_a)], sci_a.at[s])]
        for i in range(2):
            source = pl.ds(base + i * (rows_dev - edge), edge)
            pairs.append((sci_s.at[source], sci_b.at[s, pl.ds(i * edge, edge)]))
            target = pl.ds((s - part * (strips // 2)) * rows_b + i * edge, edge)
            for slots, out in zip(slot_order(epochs, orders[part]), outs[part]):
                for place, j in enumerate(slots):
                    pairs.append((num_s.at[j, source], out.at[place, target]))
        return [pltpu.make_async_copy(a, b, sems.at[s, n]) for n, (a, b) in enumerate(pairs)]

    @pl.when(step == 0)
    def _():
        top_s[0] = lax.fori_loop(
            0, offset_in, lambda i, total: total + heights_ref[0, block, i], jnp.int32(0)
        )
        top_s[1] = 0
        first = kind_ref[0, 0]
        for i in range(kinds):
            ready_s[i] = 0
            for copy in fetches(lax.rem(first + i, kinds)):
                copy.start()
        if tiles != per_col:
            sci_s[...] = jnp.zeros_like(sci_s)
            num_s[...] = jnp.zeros_like(num_s)
            wt_s[...] = jnp.zeros_like(wt_s)

    def warped(i, top):
        t = step * together + i
        kind = kind_ref[0, t]
        height = heights_ref[0, block, offset_in + t]
        start = pl.multiple_of(jnp.minimum(lax.div(top, 8) * 8, nrow - span), 8)
        off = top - start
        across = dot3(split(raw_ref[i]), (chi_s[kind], clo_s[kind]), trans_b=True)
        live = lax.broadcasted_iota(jnp.int32, (tile_rows, tile_rows), 1) < height
        rows = jnp.concatenate(
            [jnp.where(live, rmat_s[kind], 0.0), jnp.zeros((8, tile_rows), F32)], axis=0
        )
        return t, height, start, off, dot3(split(pltpu.roll(rows, off, 0)), split(across))

    for i in range(together):
        kind = kind_ref[0, step * together + i]

        @pl.when(ready_s[kind] == 0)
        def _():
            for copy in fetches(kind):
                copy.wait()
            ready_s[kind] = 1

            def divide(n, carry):
                here = pl.ds(pl.multiple_of(n * (tile_cols // 8), tile_cols // 8), tile_cols // 8)
                chi_s[kind, here, :], clo_s[kind, here, :] = split(cmat_s[kind, here, :])
                return carry

            lax.fori_loop(0, 8, divide, 0)

    top = top_s[0]
    results = []
    for i in range(together):
        results.append((top, warped(i, top)))
        top = top + results[-1][1][1]
    top_s[0] = top
    after = top

    for top, (t, height, start, off, placed) in results:
        weight = invvar_ref[0, t]
        local = lax.broadcasted_iota(jnp.int32, (span, share), 0) - off
        own = (local >= 0) & (local < height)
        here = pl.ds(start, span)
        for q in range(epochs):
            columns = pl.ds(q * share, share)
            piece = placed[:, q * share : (q + 1) * share]
            slot = jnp.bitwise_xor(me, q)
            sci_s[here, columns] = jnp.where(own, piece, sci_s[here, columns])
            num_s[slot, here, :] = jnp.where(own, weight * piece, num_s[slot, here, :])
        flat = lax.broadcasted_iota(jnp.int32, wt_s.shape, 0) * share + lax.broadcasted_iota(
            jnp.int32, wt_s.shape, 1
        )
        wt_s[...] = jnp.where((flat >= top) & (flat < top + height), weight, wt_s[...])

    before = top_s[1]
    final = jnp.where(step == last, nrow, jnp.minimum(lax.div(after, 8) * 8, nrow - span))
    top_s[1] = final
    for s in range(strips):
        end = (s + 1) * rows_dev

        @pl.when((before < end) & (end <= final))
        def _():
            for copy in strip_copies(s):
                copy.start()

    @pl.when(step == last)
    def _():
        whalf = wt_s.shape[0] // 2
        copies = []
        for part, order in enumerate(orders):
            for slots, out in zip(slot_order(epochs, order), outs[part]):
                for place in range(len(slots)):
                    copies.append(
                        pltpu.make_async_copy(
                            wt_s.at[pl.ds(part * whalf, whalf)],
                            out.at[place, pl.ds(bhalf, whalf)],
                            wt_sems.at[len(copies)],
                        )
                    )
        start_and_wait(copies)
        for s in range(strips):
            for copy in strip_copies(s):
                copy.wait()
        for k in range(kinds):

            @pl.when(ready_s[k] == 0)
            def _():
                for copy in fetches(k):
                    copy.wait()


def added(refs, place):
    return functools.reduce(lambda a, b: a + b, [ref[0, place, :] for ref in refs])


def upright(row, width):
    return jnp.transpose(jnp.broadcast_to(row, (width, width)))


def template_kernel(terms, *refs):
    term_refs, out_refs, pad_s = refs[: 2 * terms], refs[2 * terms : -1], refs[-1]
    strips = len(out_refs)
    long, share = out_refs[0].shape
    rows_b = long - 2 * HALO
    edge = rows_b // 2
    half = strips // 2
    total = strips * rows_b
    blank = jnp.zeros((HALO, share), F32)
    pad_s[pl.ds(0, HALO), :] = blank
    pad_s[pl.ds(HALO + total, HALO), :] = blank
    per_strip = ROWS_DEV // share
    for part in range(2):
        own = term_refs[part * terms : (part + 1) * terms]
        weights = added(own, pl.ds(half * rows_b, half * per_strip))
        for s in range(half):
            below = jnp.concatenate(
                [upright(weights[s * per_strip + i : s * per_strip + i + 1, :], share) for i in range(per_strip)],
                axis=0,
            )
            for i in range(2):
                first = s * rows_b + i * edge
                under = below[i * (ROWS_DEV - edge) : i * (ROWS_DEV - edge) + edge]
                pad_s[pl.ds(HALO + part * half * rows_b + first, edge), :] = added(own, pl.ds(first, edge)) / under
    for k in range(strips):
        strip = jnp.bitwise_xor(lax.axis_index("strip"), k)
        out_refs[k][...] = pad_s[pl.ds(pl.multiple_of(strip * rows_b, 8), long), :]


def weigh_kernel(geom, heights_ref, invvar_ref, sci_ref, *refs):
    epochs, orders, share = geom
    outs, num_s = refs[:4], refs[4]
    blocks, rows_a, _ = sci_ref.shape
    per_col = heights_ref.shape[2]
    tiles = invvar_ref.shape[1]
    sources = per_col // tiles
    me, strip = lax.axis_index("epoch"), lax.axis_index("strip")
    first = strip * ROWS_DEV + EDGE
    half = blocks // 2
    long = outs[0].shape[1]
    flat_shape = (long - half * rows_a, share)
    pitch = pl.cdiv(rows_a, share) * share
    flat = lax.broadcasted_iota(jnp.int32, flat_shape, 0) * share + lax.broadcasted_iota(jnp.int32, flat_shape, 1)
    row = lax.broadcasted_iota(jnp.int32, (rows_a, share), 0) + first
    for part in range(2):
        wide = jnp.zeros(flat_shape, F32)
        for b in range(half):
            block = part * half + b
            sky = flat - b * pitch
            mine = (sky >= 0) & (sky < rows_a)
            sky = sky + first
            weight = jnp.zeros((rows_a, share), F32)
            top = jnp.int32(0)
            for t in range(per_col):
                height = heights_ref[0, block, t]
                value = invvar_ref[jnp.bitwise_xor(block * sources + t // tiles, strip), t % tiles]
                weight = jnp.where((row >= top) & (row < top + height), value, weight)
                wide = jnp.where(mine & (sky >= top) & (sky < top + height), value, wide)
                top = top + height
            for q in range(epochs):
                piece = sci_ref[block, :, pl.ds(q * share, share)]
                num_s[jnp.bitwise_xor(me, q), pl.ds(b * rows_a, rows_a), :] = weight * piece
        for j in range(epochs):
            num_s[j, pl.ds(half * rows_a, flat_shape[0]), :] = wide
        for slots, out in zip(slot_order(epochs, orders[part]), outs[2 * part : 2 * part + 2]):
            for place, j in enumerate(slots):
                out[place] = num_s[j]


def middle_kernel(terms, *refs):
    term_refs, outer_refs, out_ref = refs[: 2 * terms], refs[2 * terms : -1], refs[-1]
    blocks, long, share = out_ref.shape
    above = EDGE + HALO
    rows_a = long - 2 * above
    home = lax.div(lax.axis_index("strip"), lax.axis_size("strip") // blocks)
    half = blocks // 2
    for k, ref in enumerate(outer_refs):
        out_ref[k, pl.ds(0, above), :] = ref[pl.ds(0, above), :]
        out_ref[k, pl.ds(above + rows_a, above), :] = ref[pl.ds(above, above), :]
    for part in range(2):
        own = term_refs[part * terms : (part + 1) * terms]
        weights = added(own, pl.ds(half * rows_a, own[0].shape[1] - half * rows_a))
        lines = pl.cdiv(rows_a, share)
        for b in range(half):
            below = jnp.concatenate(
                [upright(weights[b * lines + i : b * lines + i + 1, :], share) for i in range(lines)], axis=0
            )
            value = added(own, pl.ds(b * rows_a, rows_a)) / below[:rows_a]
            out_ref[jnp.bitwise_xor(home, part * half + b), pl.ds(above, rows_a), :] = value


def bands_kernel(psf_ref, toep_hi, toep_lo, band_ref):
    basis, _, ksize = psf_ref.shape
    margin = ksize // 2
    for k in range(basis):
        shape = (2 * LANES, LANES)
        tap = lax.broadcasted_iota(jnp.int32, shape, 0) - lax.broadcasted_iota(jnp.int32, shape, 1)
        tap = tap - (LANES // 2 - margin)
        value = jnp.zeros(shape, F32)
        for j in range(ksize):
            value = jnp.where(tap == j, psf_ref[k, 1, j], value)
        toep_hi[:, pl.ds(k * LANES, LANES)], toep_lo[:, pl.ds(k * LANES, LANES)] = split(value)
        shape = (LANES, LANES + 2 * HALO)
        tap = lax.broadcasted_iota(jnp.int32, shape, 1) - lax.broadcasted_iota(jnp.int32, shape, 0)
        tap = tap - (HALO - margin)
        value = jnp.zeros(shape, F32)
        for j in range(ksize):
            value = jnp.where(tap == j, psf_ref[k, 0, j], value)
        band_ref[k, pl.ds(0, LANES), :], band_ref[k, pl.ds(LANES, LANES), :] = split(value)


def match_kernel(geom, *refs):
    slots, nrow, ncol = geom
    count = max(len(slots), 1) + (len(slots) > 1)
    tile_refs = refs[:count]
    poly_ref, toep_hi, toep_lo, band_ref, sci_ref, out_ref, pad_s, row_s, sems = refs[count:]
    step = pl.program_id(0)
    blocks = pl.num_programs(0)
    tiles = pad_s.shape[0] - 2
    rows_dev = pad_s.shape[1] - 2 * HALO
    me = lax.axis_index("epoch")
    strip = lax.axis_index("strip")
    per_step = out_ref.shape[1] // LANES

    def bring(b):
        if not slots:
            for i in range(per_step):
                place = b * per_step + i
                pltpu.make_async_copy(tile_refs[0].at[place], pad_s.at[1 + place], sems.at[b, i]).start()
            return
        at = jnp.bitwise_xor(strip, b)
        for n, slot in enumerate(slots):
            target = pad_s.at[1 + b * per_step + jnp.bitwise_xor(me, slot)]
            if n < len(slots) - 1:
                pltpu.make_async_copy(tile_refs[n].at[at], target, sems.at[b, n]).start()
                continue
            cut = tile_refs[n].shape[0]

            @pl.when(at < cut)
            def _():
                pltpu.make_async_copy(tile_refs[n].at[at], target, sems.at[b, n]).start()

            @pl.when(at >= cut)
            def _():
                pltpu.make_async_copy(tile_refs[n + 1].at[at - cut], target, sems.at[b, n]).start()

    def await_block(b):
        for i in range(per_step):
            pltpu.make_async_copy(tile_refs[0].at[0], pad_s.at[1], sems.at[b, i]).wait()

    @pl.when(step == 0)
    def _():
        for b in range(tiles // per_step):
            bring(b)
        pad_s[0] = jnp.zeros(pad_s.shape[1:], F32)
        pad_s[tiles + 1] = jnp.zeros(pad_s.shape[1:], F32)
        shape = (rows_dev, LANES)
        counter = (strip * rows_dev + lax.broadcasted_iota(jnp.int32, shape, 0)).astype(F32)
        u = (2.0 * counter + 1.0) / nrow - 1.0
        for k in range(2):
            p = [poly_ref[me, k, i] for i in range(6)]
            row_s[k, 0] = p[0] + u * (p[1] + p[3] * u)
            row_s[k, 1] = p[2] + p[4] * u
        await_block(0)

    @pl.when(step < blocks - 1)
    def _():
        await_block(step + 1)

    lane = lax.broadcasted_iota(jnp.int32, pad_s.shape[1:], 1)
    base = step * per_step
    shifted = []
    for m in range(per_step + 1):
        mixed = jnp.where(lane < LANES // 2, pad_s[base + m + 1], pad_s[base + m])
        shifted.append(split(pltpu.roll(mixed, LANES // 2, 1)))
    toep = (toep_hi[...], toep_lo[...])
    for pair in range(per_step // 2):
        across = []
        for c in (2 * pair, 2 * pair + 1):
            window = tuple(
                jnp.concatenate([shifted[c][i], shifted[c + 1][i]], axis=1) for i in range(2)
            )
            across.append(dot3(window, toep))
        width = 2 * LANES
        cols = lax.broadcasted_iota(jnp.int32, (1, width), 1) + (base + 2 * pair) * LANES
        v = (2.0 * cols.astype(F32) + 1.0) / ncol - 1.0
        for part in range(rows_dev // LANES):
            total = 0.0
            for k in range(2):
                both = jnp.concatenate(
                    [a[part * LANES : part * LANES + LANES + 2 * HALO, k * LANES : (k + 1) * LANES] for a in across],
                    axis=1,
                )
                hi, lo = split(both)
                wide = dot(band_ref[k], hi)
                done = wide[:LANES] + (wide[LANES:] + dot(band_ref[k, pl.ds(0, LANES), :], lo))
                place = pl.ds(part * LANES, LANES)
                one = jnp.concatenate([row_s[k, 0, place, :]] * 2, axis=1)
                two = jnp.concatenate([row_s[k, 1, place, :]] * 2, axis=1)
                coeff = one + v * (two + poly_ref[me, k, 5] * v)
                total = total + coeff * done
            columns = pl.ds(pair * width, width)
            low = min(max(EDGE - part * LANES, 0), LANES)
            high = min(max(rows_dev - EDGE - part * LANES, 0), LANES)
            for begin, end, final in ((0, low, False), (low, high, True), (high, LANES, False)):
                if begin == end:
                    continue
                piece = total[begin:end]
                if final:
                    own = pl.ds(part * LANES + begin - EDGE, end - begin)
                    piece = sci_ref[0, own, columns] - piece
                out_ref[pl.ds(part * LANES + begin, end - begin), columns] = piece


def subtract_kernel(sci_ref, matched_ref, out_ref):
    i = pl.program_id(0)
    blocks, _, width = sci_ref.shape
    rows = out_ref.shape[1]
    for b in range(blocks):
        columns = pl.ds(b * width, width)
        science = sci_ref[b, pl.ds(pl.multiple_of(i * rows, rows), rows), :]
        out_ref[0, :, columns] = science - matched_ref[0, :, columns]


def swap(value, axis, bit):
    count = lax.axis_size(axis)
    return lax.ppermute(value, axis, [(i, i ^ (1 << bit)) for i in range(count)])


def shards(
    raw_tiles, tile_kind, tile_invvar, tile_heights, row_interp, col_interp, psf_profiles, psf_poly
):
    strips, epochs = lax.axis_size("strip"), lax.axis_size("epoch")
    _, tiles, tile_rows, tile_cols = raw_tiles.shape
    _, blocks, _ = tile_heights.shape
    ncol, nrow = blocks * tile_cols, ROWS_DEV * strips
    sources = strips // blocks
    share = tile_cols // epochs
    bits = epochs.bit_length() - 1
    orders = (tuple(range(bits)), tuple(reversed(range(bits))))
    wrows = nrow // share
    rows_b = 2 * EDGE
    rows_a = ROWS_DEV - rows_b
    long_half = strips // 2 * rows_b + wrows // 2
    smem = pl.BlockSpec(memory_space=pltpu.SMEM)
    hbm = pl.BlockSpec(memory_space=pl.ANY)
    vmem = pl.BlockSpec(memory_space=pltpu.VMEM)
    kinds = col_interp.shape[0]

    sci_shapes = [jax.ShapeDtypeStruct((strips, rows, tile_cols), F32) for rows in (rows_a, rows_b)]
    send_shape = jax.ShapeDtypeStruct((epochs // 2, long_half, share), F32)
    together = 2 if tiles % 2 == 0 else 1
    sci_a, sci_b, keep_a, send_a, keep_b, send_b = pl.pallas_call(
        functools.partial(warp_kernel, (epochs, nrow, share, orders, tiles)),
        grid=(tiles // together,),
        in_specs=[
            smem,
            smem,
            smem,
            pl.BlockSpec((together, tile_rows, tile_cols), lambda t: (t, 0, 0)),
            hbm,
            hbm,
        ],
        out_specs=[hbm] * 6,
        out_shape=sci_shapes + [send_shape] * 4,
        scratch_shapes=[
            pltpu.VMEM((nrow, tile_cols), F32),
            pltpu.VMEM((epochs, nrow, share), F32),
            pltpu.VMEM((wrows, share), F32),
            pltpu.VMEM((kinds, tile_rows, tile_rows), F32),
            pltpu.VMEM((kinds, tile_cols, tile_cols), F32),
            pltpu.VMEM((kinds, tile_cols, tile_cols), BF16),
            pltpu.VMEM((kinds, tile_cols, tile_cols), BF16),
            pltpu.SMEM((2,), jnp.int32),
            pltpu.SMEM((kinds,), jnp.int32),
            pltpu.SemaphoreType.DMA((kinds, 2)),
            pltpu.SemaphoreType.DMA((strips, 3 + 2 * epochs)),
            pltpu.SemaphoreType.DMA((2 * epochs,)),
        ],
        name="warp",
        cost_estimate=pl.CostEstimate(flops=8_000_000_000, bytes_accessed=20_000_000, transcendentals=0),
    )(tile_kind, tile_heights, tile_invvar, raw_tiles[0], row_interp, col_interp)

    got_a = lax.all_to_all(sci_a, "strip", split_axis=0, concat_axis=0, tiled=True)
    invvars = [tile_invvar]
    for k in range(1, strips):
        invvars.append(lax.ppermute(tile_invvar, "strip", [(i, i ^ k) for i in range(strips)]))
    invvars = jnp.concatenate(invvars, axis=0)

    basis, _, _ = psf_profiles.shape
    build_bands = pl.pallas_call(
        bands_kernel,
        in_specs=[smem],
        out_specs=[vmem] * 3,
        out_shape=[
            jax.ShapeDtypeStruct((2 * LANES, 2 * LANES), BF16),
            jax.ShapeDtypeStruct((2 * LANES, 2 * LANES), BF16),
            jax.ShapeDtypeStruct((basis, 2 * LANES, LANES + 2 * HALO), BF16),
        ],
        name="bands",
        cost_estimate=pl.CostEstimate(flops=10_000_000, bytes_accessed=500_000, transcendentals=0),
    )
    toep_hi, toep_lo, band = build_bands(psf_profiles)

    def reduced(keeps, sends):
        terms = [[keep] for keep in keeps]
        sends = list(sends)
        for i in range(bits):
            for part in range(2):
                terms[part].append(swap(sends[part], "epoch", orders[part][i]))
            left = epochs >> (i + 1)
            if left > 1:
                for part, own in enumerate(terms):
                    sends[part] = functools.reduce(lambda a, b: a + b, [t[left // 2 : left] for t in own])
        return terms

    terms = reduced([keep_a, keep_b], [send_a, send_b])
    if sources > 1:
        fixed = []
        for own in terms:
            total = functools.reduce(lambda a, b: a + b, [t[:1] for t in own])
            around = total
            for k in range(1, sources):
                ring = [(i, i // sources * sources + (i + k) % sources) for i in range(strips)]
                around = around + lax.ppermute(total, "strip", ring)
            fixed.append([around])
        terms = fixed

    long = ROWS_DEV + 2 * HALO
    long_b = rows_b + 2 * HALO
    parts = pl.pallas_call(
        functools.partial(template_kernel, len(terms[0])),
        in_specs=[vmem] * (2 * len(terms[0])),
        out_specs=[vmem] * strips,
        out_shape=[jax.ShapeDtypeStruct((long_b, share), F32)] * strips,
        scratch_shapes=[pltpu.VMEM((strips * rows_b + 2 * HALO, share), F32)],
        name="template",
        cost_estimate=pl.CostEstimate(flops=2_000_000, bytes_accessed=5_000_000, transcendentals=0),
    )(*terms[0], *terms[1])
    came = [None] * strips
    came[0] = parts[0]
    for k in reversed(range(1, strips)):
        came[k] = lax.ppermute(parts[k], "strip", [(i, i ^ k) for i in range(strips)])
    side_a = got_a
    if sources > 1:
        side_a = jnp.sum(got_a.reshape((blocks, sources) + got_a.shape[1:]), axis=1)
    long_a = blocks // 2 * rows_a + 8 * pl.cdiv(blocks // 2 * pl.cdiv(rows_a, share), 8)
    weighted_shape = jax.ShapeDtypeStruct((epochs // 2, long_a, share), F32)
    weigh = pl.pallas_call(
        functools.partial(weigh_kernel, (epochs, orders, share)),
        in_specs=[smem, smem, vmem],
        out_specs=[vmem] * 4,
        out_shape=[weighted_shape] * 4,
        scratch_shapes=[pltpu.VMEM((epochs, long_a, share), F32)],
        name="weigh",
        cost_estimate=pl.CostEstimate(flops=2_000_000, bytes_accessed=2_500_000, transcendentals=0),
    )
    weighted = weigh(tile_heights, invvars, side_a)
    middle_terms = reduced(weighted[0::2], weighted[1::2])
    outer = came[::sources]
    for part in range(2):
        sci_b, middle_terms[part][-1] = lax.optimization_barrier((sci_b, middle_terms[part][-1]))
    sci_b, got_a, *outer = lax.optimization_barrier((sci_b, got_a, *outer))
    merge = pl.pallas_call(
        functools.partial(middle_kernel, len(middle_terms[0])),
        in_specs=[vmem] * (2 * len(middle_terms[0]) + blocks),
        out_specs=vmem,
        out_shape=jax.ShapeDtypeStruct((blocks, long, share), F32),
        name="middle",
        cost_estimate=pl.CostEstimate(flops=500_000, bytes_accessed=4_000_000, transcendentals=0),
    )
    mine = merge(*middle_terms[0], *middle_terms[1], *outer)
    got_b = lax.all_to_all(sci_b, "strip", split_axis=0, concat_axis=0, tiled=True)
    got_a = got_a if sources == 1 else side_a
    if sources > 1:
        got_b = jnp.sum(got_b.reshape((blocks, sources) + got_b.shape[1:]), axis=1)

    per_block = tile_cols // LANES
    if epochs == 4 and share == LANES:
        near = []
        for b in range(2):
            near.append(swap(mine, "epoch", b))
        cut = blocks // 2
        far_low = swap(near[1][:cut], "epoch", 0)
        far_high = swap(near[0][cut:], "epoch", 1)
        arrays = [mine, near[0], near[1], far_low, far_high]
        held = (0, 1, 2, 3)
    else:
        slots = [mine]
        for b in range(bits):
            slots = slots + [swap(s, "epoch", b) for s in slots]
        me = lax.axis_index("epoch")
        every = jnp.take(jnp.stack(slots), jnp.bitwise_xor(jnp.arange(epochs), me), axis=0)
        home = lax.axis_index("strip") // sources
        every = jnp.take(every, jnp.bitwise_xor(jnp.arange(blocks), home), axis=1)
        flat = jnp.transpose(every, (1, 2, 0, 3)).reshape(blocks, long, per_block, LANES)
        arrays = [jnp.transpose(flat, (0, 2, 1, 3)).reshape(blocks * per_block, long, LANES)]
        held = ()

    const = lambda b: (0, 0)
    convolve = pl.pallas_call(
        functools.partial(match_kernel, (held, nrow, ncol)),
        grid=(blocks,),
        in_specs=[hbm] * len(arrays)
        + [
            smem,
            pl.BlockSpec(toep_hi.shape, const),
            pl.BlockSpec(toep_lo.shape, const),
            pl.BlockSpec(band.shape, lambda b: (0, 0, 0)),
            pl.BlockSpec((1,) + got_a.shape[1:], lambda b: (b, 0, 0)),
        ],
        out_specs=pl.BlockSpec((ROWS_DEV, tile_cols), lambda b: (0, b)),
        out_shape=jax.ShapeDtypeStruct((ROWS_DEV, ncol), F32),
        scratch_shapes=[
            pltpu.VMEM((blocks * per_block + 2, long, LANES), F32),
            pltpu.VMEM((2, 2, ROWS_DEV, LANES), F32),
            pltpu.SemaphoreType.DMA((blocks, per_block)),
        ],
        name="convolve",
        compiler_params=pltpu.CompilerParams(vmem_limit_bytes=32 << 20),
        cost_estimate=pl.CostEstimate(flops=15_000_000_000, bytes_accessed=10_000_000, transcendentals=0),
    )
    matched = convolve(*arrays, psf_poly, toep_hi, toep_lo, band, got_a)
    unit = ROWS_DEV // 16
    outside = EDGE // unit
    rest = pl.BlockSpec(
        (1, unit, ncol), lambda i: (0, jnp.where(i < outside, i, i + rows_a // unit), 0)
    )
    return pl.pallas_call(
        subtract_kernel,
        grid=(2 * outside,),
        in_specs=[vmem, rest],
        out_specs=rest,
        out_shape=jax.ShapeDtypeStruct((1, ROWS_DEV, ncol), F32),
        input_output_aliases={1: 0},
        name="subtract",
        compiler_params=pltpu.CompilerParams(vmem_limit_bytes=16 << 20),
        cost_estimate=pl.CostEstimate(flops=1_000_000, bytes_accessed=6_000_000, transcendentals=0),
    )(pltpu.with_memory_space_constraint(got_b, pltpu.VMEM), matched[None])


def solution(mesh):
    in_specs = (
        P("epoch", "strip", None, None),
        P("epoch", "strip"),
        P("epoch", "strip"),
        P("epoch", None, None),
        P(),
        P(),
        P(),
        P(),
    )
    out_specs = P("epoch", "strip", None)

    return jax.shard_map(shards, mesh=mesh, in_specs=in_specs, out_specs=out_specs, check_vma=False)
```

```python
import functools

import jax
import jax.numpy as jnp
from jax import lax
from jax.experimental import pallas as pl
from jax.experimental.pallas import tpu as pltpu
from jax.sharding import PartitionSpec as P


ROWS_DEV = 256
HALO = 16
FIRST_PART = 3
LANES = 128
F32 = jnp.float32
BF16 = jnp.bfloat16
F8 = jnp.float8_e4m3fn


def split(x):
    hi = x.astype(BF16)
    lo = (x - hi.astype(F32)).astype(BF16)
    return hi, lo


def dot(a, b, trans_b=False):
    dims = (((1,), (1 if trans_b else 0,)), ((), ()))
    return lax.dot_general(a, b, dims, preferred_element_type=F32)


def dot3(a, b, trans_b=False):
    a_hi, a_lo = a
    b_hi, b_lo = b
    both = dot(jnp.concatenate([a_hi, a_lo], axis=0), b_hi, trans_b)
    rows = a_hi.shape[0]
    return both[:rows] + (both[rows:] + dot(a_hi, b_lo, trans_b))


def split8(x, own, rest, swapped=False):
    hi = x.astype(BF16)
    wide = hi.astype(F32)
    high, low = (wide * own).astype(F8), ((x - wide) * rest).astype(F8)
    return hi, jnp.concatenate([high, low] if swapped else [low, high], axis=-1)


def start_and_wait(copies):
    for copy in copies:
        copy.start()
    for copy in copies:
        copy.wait()


def slot_order(count, order):
    bits = len(order)
    key = lambda j: sum(((j >> order[i]) & 1) << (bits - 1 - i) for i in range(bits))
    slots = sorted(range(count), key=key)
    return slots[: count // 2], slots[count // 2 :]


def warp_kernel(
    geom, kind_ref, heights_ref, invvar_ref, raw_ref, rmat_ref, cmat_ref,
    sci_a, sci_b, keep_a, send_a, keep_b, send_b,
    sci_s, num_s, wt_s, rmat_s, cmat_s, chi_s, clo_s, top_s, ready_s, fetch_sems, sems, wt_sems,
):
    epochs, nrow, share, orders, tiles = geom
    step = pl.program_id(0)
    together, tile_rows, tile_cols = raw_ref.shape
    last = pl.num_programs(0) - 1
    per_col = heights_ref.shape[2]
    span = tile_rows + 8
    me = lax.axis_index("epoch")
    first_tile = lax.axis_index("strip") * tiles
    block = lax.div(first_tile, per_col)
    offset_in = lax.rem(first_tile, per_col)
    kinds = cmat_ref.shape[0]
    strips, rows_a, _ = sci_a.shape
    rows_dev = rows_a + sci_b.shape[1]
    nhalf = nrow // 2
    outs = (keep_a, send_a), (keep_b, send_b)

    def fetches(k):
        return [
            pltpu.make_async_copy(cmat_ref.at[k], cmat_s.at[k], fetch_sems.at[k, 0]),
            pltpu.make_async_copy(rmat_ref.at[k], rmat_s.at[k], fetch_sems.at[k, 1]),
        ]

    def strip_copies(s):
        base = s * rows_dev
        part = base // nhalf
        pairs = [
            (sci_s.at[pl.ds(base, rows_a)], sci_a.at[s]),
            (sci_s.at[pl.ds(base + rows_a, rows_dev - rows_a)], sci_b.at[s]),
        ]
        for slots, out in zip(slot_order(epochs, orders[part]), outs[part]):
            for place, j in enumerate(slots):
                pairs.append(
                    (num_s.at[j, pl.ds(base, rows_dev)], out.at[place, pl.ds(base - part * nhalf, rows_dev)])
                )
        return [pltpu.make_async_copy(a, b, sems.at[s, n]) for n, (a, b) in enumerate(pairs)]

    @pl.when(step == 0)
    def _():
        top_s[0] = lax.fori_loop(
            0, offset_in, lambda i, total: total + heights_ref[0, block, i], jnp.int32(0)
        )
        top_s[1] = 0
        first = kind_ref[0, 0]
        for i in range(kinds):
            ready_s[i] = 0
            for copy in fetches(lax.rem(first + i, kinds)):
                copy.start()
        if tiles != per_col:
            sci_s[...] = jnp.zeros_like(sci_s)
            num_s[...] = jnp.zeros_like(num_s)
            wt_s[...] = jnp.zeros_like(wt_s)

    def warped(i, top):
        t = step * together + i
        kind = kind_ref[0, t]
        height = heights_ref[0, block, offset_in + t]
        start = pl.multiple_of(jnp.minimum(lax.div(top, 8) * 8, nrow - span), 8)
        off = top - start
        main, fine = split8(raw_ref[i], 1.0, 256.0)
        across = dot(main, chi_s[kind], True) + dot(fine, clo_s[kind], True) * (1.0 / 4096.0)
        live = lax.broadcasted_iota(jnp.int32, (tile_rows, tile_rows), 1) < height
        rows = jnp.concatenate(
            [jnp.where(live, rmat_s[kind], 0.0), jnp.zeros((8, tile_rows), F32)], axis=0
        )
        return t, height, start, off, dot3(split(pltpu.roll(rows, off, 0)), split(across))

    for i in range(together):
        kind = kind_ref[0, step * together + i]

        @pl.when(ready_s[kind] == 0)
        def _():
            for copy in fetches(kind):
                copy.wait()
            ready_s[kind] = 1

            def divide(n, carry):
                here = pl.ds(pl.multiple_of(n * (tile_cols // 8), tile_cols // 8), tile_cols // 8)
                chi_s[kind, here, :], clo_s[kind, here, :] = split8(cmat_s[kind, here, :], 16.0, 4096.0, True)
                return carry

            lax.fori_loop(0, 8, divide, 0)

    top = top_s[0]
    results = []
    for i in range(together):
        results.append((top, warped(i, top)))
        top = top + results[-1][1][1]
    top_s[0] = top
    after = top

    for top, (t, height, start, off, placed) in results:
        weight = invvar_ref[0, t]
        local = lax.broadcasted_iota(jnp.int32, (span, share), 0) - off
        own = (local >= 0) & (local < height)
        here = pl.ds(start, span)
        for q in range(epochs):
            columns = pl.ds(q * share, share)
            piece = placed[:, q * share : (q + 1) * share]
            slot = jnp.bitwise_xor(me, q)
            sci_s[here, columns] = jnp.where(own, piece, sci_s[here, columns])
            num_s[slot, here, :] = jnp.where(own, weight * piece, num_s[slot, here, :])
        flat = lax.broadcasted_iota(jnp.int32, wt_s.shape, 0) * share + lax.broadcasted_iota(
            jnp.int32, wt_s.shape, 1
        )
        wt_s[...] = jnp.where((flat >= top) & (flat < top + height), weight, wt_s[...])

    before = top_s[1]
    final = jnp.where(step == last, nrow, jnp.minimum(lax.div(after, 8) * 8, nrow - span))
    top_s[1] = final
    for s in range(strips):
        end = (s + 1) * rows_dev

        @pl.when((before < end) & (end <= final))
        def _():
            for copy in strip_copies(s):
                copy.start()

    @pl.when(step == last)
    def _():
        whalf = wt_s.shape[0] // 2
        copies = []
        for part, order in enumerate(orders):
            for slots, out in zip(slot_order(epochs, order), outs[part]):
                for place in range(len(slots)):
                    copies.append(
                        pltpu.make_async_copy(
                            wt_s.at[pl.ds(part * whalf, whalf)],
                            out.at[place, pl.ds(nhalf, whalf)],
                            wt_sems.at[len(copies)],
                        )
                    )
        start_and_wait(copies)
        for s in range(strips):
            for copy in strip_copies(s):
                copy.wait()
        for k in range(kinds):

            @pl.when(ready_s[k] == 0)
            def _():
                for copy in fetches(k):
                    copy.wait()


def template_kernel(terms, *refs):
    term_refs, out_refs, pad_s = refs[: 2 * terms], refs[2 * terms : -1], refs[-1]
    strips = len(out_refs)
    long, share = out_refs[0].shape
    rows_dev = long - 2 * HALO
    nrow = strips * rows_dev
    nhalf = nrow // 2
    whalf = nhalf // share
    edge = jnp.zeros((HALO, share), F32)
    pad_s[pl.ds(0, HALO), :] = edge
    pad_s[pl.ds(HALO + nrow, HALO), :] = edge
    for part in range(2):
        own = term_refs[part * terms : (part + 1) * terms]
        add = lambda place: functools.reduce(lambda a, b: a + b, [ref[0, place, :] for ref in own])
        weights = add(pl.ds(nhalf, whalf))
        for i in range(whalf):
            below = jnp.transpose(jnp.broadcast_to(weights[i : i + 1, :], (share, share)))
            pad_s[pl.ds(HALO + part * nhalf + i * share, share), :] = add(pl.ds(i * share, share)) / below
    for k in range(strips):
        strip = jnp.bitwise_xor(lax.axis_index("strip"), k)
        out_refs[k][...] = pad_s[pl.ds(pl.multiple_of(strip * rows_dev, rows_dev), long), :]


def bands_kernel(psf_ref, toep_hi, toep_lo, band_ref):
    basis, _, ksize = psf_ref.shape
    margin = ksize // 2
    for k in range(basis):
        shape = (2 * LANES, LANES)
        tap = lax.broadcasted_iota(jnp.int32, shape, 0) - lax.broadcasted_iota(jnp.int32, shape, 1)
        tap = tap - (LANES // 2 - margin)
        value = jnp.zeros(shape, F32)
        for j in range(ksize):
            value = jnp.where(tap == j, psf_ref[k, 1, j], value)
        toep_hi[:, pl.ds(k * LANES, LANES)], toep_lo[:, pl.ds(k * LANES, LANES)] = split(value)
        shape = (LANES, LANES + 2 * HALO)
        tap = lax.broadcasted_iota(jnp.int32, shape, 1) - lax.broadcasted_iota(jnp.int32, shape, 0)
        tap = tap - (HALO - margin)
        value = jnp.zeros(shape, F32)
        for j in range(ksize):
            value = jnp.where(tap == j, psf_ref[k, 0, j], value)
        band_ref[k, pl.ds(0, LANES), :], band_ref[k, pl.ds(LANES, LANES), :] = split(value)


def match_kernel(geom, *refs):
    slots, nrow, ncol = geom
    count = max(len(slots), 1) + (len(slots) > 1)
    tile_refs = refs[:count]
    poly_ref, toep_hi, toep_lo, band_ref, sci_ref, out_ref, pad_s, row_s, sems = refs[count:]
    step = pl.program_id(0)
    blocks = pl.num_programs(0)
    tiles = pad_s.shape[0] - 2
    rows_dev = pad_s.shape[1] - 2 * HALO
    me = lax.axis_index("epoch")
    strip = lax.axis_index("strip")
    per_step = out_ref.shape[1] // LANES

    def bring(b):
        if not slots:
            for i in range(per_step):
                place = b * per_step + i
                pltpu.make_async_copy(tile_refs[0].at[place], pad_s.at[1 + place], sems.at[b, i]).start()
            return
        at = jnp.bitwise_xor(strip, b)
        for n, slot in enumerate(slots):
            target = pad_s.at[1 + b * per_step + jnp.bitwise_xor(me, slot)]
            if n < len(slots) - 1:
                pltpu.make_async_copy(tile_refs[n].at[at], target, sems.at[b, n]).start()
                continue
            cut = tile_refs[n].shape[0]

            @pl.when(at < cut)
            def _():
                pltpu.make_async_copy(tile_refs[n].at[at], target, sems.at[b, n]).start()

            @pl.when(at >= cut)
            def _():
                pltpu.make_async_copy(tile_refs[n + 1].at[at - cut], target, sems.at[b, n]).start()

    def await_block(b):
        for i in range(per_step):
            pltpu.make_async_copy(tile_refs[0].at[0], pad_s.at[1], sems.at[b, i]).wait()

    @pl.when(step == 0)
    def _():
        for b in range(tiles // per_step):
            bring(b)
        pad_s[0] = jnp.zeros(pad_s.shape[1:], F32)
        pad_s[tiles + 1] = jnp.zeros(pad_s.shape[1:], F32)
        shape = (rows_dev, LANES)
        counter = (strip * rows_dev + lax.broadcasted_iota(jnp.int32, shape, 0)).astype(F32)
        u = (2.0 * counter + 1.0) / nrow - 1.0
        for k in range(2):
            p = [poly_ref[me, k, i] for i in range(6)]
            row_s[k, 0] = p[0] + u * (p[1] + p[3] * u)
            row_s[k, 1] = p[2] + p[4] * u
        await_block(0)

    @pl.when(step < blocks - 1)
    def _():
        await_block(step + 1)

    lane = lax.broadcasted_iota(jnp.int32, pad_s.shape[1:], 1)
    base = step * per_step
    shifted = []
    for m in range(per_step + 1):
        mixed = jnp.where(lane < LANES // 2, pad_s[base + m + 1], pad_s[base + m])
        shifted.append(split(pltpu.roll(mixed, LANES // 2, 1)))
    toep = (toep_hi[...], toep_lo[...])
    for pair in range(per_step // 2):
        across = []
        for c in (2 * pair, 2 * pair + 1):
            window = tuple(
                jnp.concatenate([shifted[c][i], shifted[c + 1][i]], axis=1) for i in range(2)
            )
            across.append(dot3(window, toep))
        width = 2 * LANES
        cols = lax.broadcasted_iota(jnp.int32, (1, width), 1) + (base + 2 * pair) * LANES
        v = (2.0 * cols.astype(F32) + 1.0) / ncol - 1.0
        for part in range(rows_dev // LANES):
            total = 0.0
            for k in range(2):
                both = jnp.concatenate(
                    [a[part * LANES : part * LANES + LANES + 2 * HALO, k * LANES : (k + 1) * LANES] for a in across],
                    axis=1,
                )
                hi, lo = split(both)
                wide = dot(band_ref[k], hi)
                done = wide[:LANES] + (wide[LANES:] + dot(band_ref[k, pl.ds(0, LANES), :], lo))
                place = pl.ds(part * LANES, LANES)
                one = jnp.concatenate([row_s[k, 0, place, :]] * 2, axis=1)
                two = jnp.concatenate([row_s[k, 1, place, :]] * 2, axis=1)
                coeff = one + v * (two + poly_ref[me, k, 5] * v)
                total = total + coeff * done
            columns = pl.ds(pair * width, width)
            ready = min(max(sci_ref.shape[1] - part * LANES, 0), LANES)
            if ready:
                here = pl.ds(part * LANES, ready)
                out_ref[here, columns] = sci_ref[0, here, columns] - total[:ready]
            if ready < LANES:
                out_ref[pl.ds(part * LANES + ready, LANES - ready), columns] = total[ready:]


def subtract_kernel(sci_ref, matched_ref, out_ref):
    i = pl.program_id(0)
    blocks, _, width = sci_ref.shape
    rows = out_ref.shape[1]
    for b in range(blocks):
        columns = pl.ds(b * width, width)
        science = sci_ref[b, pl.ds(pl.multiple_of(i * rows, rows), rows), :]
        out_ref[0, :, columns] = science - matched_ref[0, :, columns]


def swap(value, axis, bit):
    count = lax.axis_size(axis)
    return lax.ppermute(value, axis, [(i, i ^ (1 << bit)) for i in range(count)])


def shards(
    raw_tiles, tile_kind, tile_invvar, tile_heights, row_interp, col_interp, psf_profiles, psf_poly
):
    strips, epochs = lax.axis_size("strip"), lax.axis_size("epoch")
    _, tiles, tile_rows, tile_cols = raw_tiles.shape
    _, blocks, _ = tile_heights.shape
    ncol, nrow = blocks * tile_cols, ROWS_DEV * strips
    sources = strips // blocks
    share = tile_cols // epochs
    bits = epochs.bit_length() - 1
    orders = (tuple(range(bits)), tuple(reversed(range(bits))))
    nhalf = nrow // 2
    wrows = nrow // share
    long_half = nhalf + wrows // 2
    smem = pl.BlockSpec(memory_space=pltpu.SMEM)
    hbm = pl.BlockSpec(memory_space=pl.ANY)
    vmem = pl.BlockSpec(memory_space=pltpu.VMEM)
    kinds = col_interp.shape[0]

    first_rows = ROWS_DEV * FIRST_PART // 8
    sci_shapes = [
        jax.ShapeDtypeStruct((strips, rows, tile_cols), F32) for rows in (first_rows, ROWS_DEV - first_rows)
    ]
    send_shape = jax.ShapeDtypeStruct((epochs // 2, long_half, share), F32)
    together = 2 if tiles % 2 == 0 else 1
    sci_a, sci_b, keep_a, send_a, keep_b, send_b = pl.pallas_call(
        functools.partial(warp_kernel, (epochs, nrow, share, orders, tiles)),
        grid=(tiles // together,),
        in_specs=[
            smem,
            smem,
            smem,
            pl.BlockSpec((together, tile_rows, tile_cols), lambda t: (t, 0, 0)),
            hbm,
            hbm,
        ],
        out_specs=[hbm] * 6,
        out_shape=sci_shapes + [send_shape] * 4,
        scratch_shapes=[
            pltpu.VMEM((nrow, tile_cols), F32),
            pltpu.VMEM((epochs, nrow, share), F32),
            pltpu.VMEM((wrows, share), F32),
            pltpu.VMEM((kinds, tile_rows, tile_rows), F32),
            pltpu.VMEM((kinds, tile_cols, tile_cols), F32),
            pltpu.VMEM((kinds, tile_cols, tile_cols), BF16),
            pltpu.VMEM((kinds, tile_cols, 2 * tile_cols), F8),
            pltpu.SMEM((2,), jnp.int32),
            pltpu.SMEM((kinds,), jnp.int32),
            pltpu.SemaphoreType.DMA((kinds, 2)),
            pltpu.SemaphoreType.DMA((strips, 2 + epochs)),
            pltpu.SemaphoreType.DMA((2 * epochs,)),
        ],
        name="warp",
        cost_estimate=pl.CostEstimate(flops=8_000_000_000, bytes_accessed=20_000_000, transcendentals=0),
    )(tile_kind, tile_heights, tile_invvar, raw_tiles[0], row_interp, col_interp)

    got_a = lax.all_to_all(sci_a, "strip", split_axis=0, concat_axis=0, tiled=True)

    basis, _, _ = psf_profiles.shape
    build_bands = pl.pallas_call(
        bands_kernel,
        in_specs=[smem],
        out_specs=[vmem] * 3,
        out_shape=[
            jax.ShapeDtypeStruct((2 * LANES, 2 * LANES), BF16),
            jax.ShapeDtypeStruct((2 * LANES, 2 * LANES), BF16),
            jax.ShapeDtypeStruct((basis, 2 * LANES, LANES + 2 * HALO), BF16),
        ],
        name="bands",
        cost_estimate=pl.CostEstimate(flops=10_000_000, bytes_accessed=500_000, transcendentals=0),
    )
    toep_hi, toep_lo, band = build_bands(psf_profiles)

    terms = [[keep_a], [keep_b]]
    sends = [send_a, send_b]
    for i in range(bits):
        for part in range(2):
            terms[part].append(swap(sends[part], "epoch", orders[part][i]))
        left = epochs >> (i + 1)
        if left > 1:
            sends = [
                functools.reduce(lambda a, b: a + b, [t[left // 2 : left] for t in own]) for own in terms
            ]
    if sources > 1:
        fixed = []
        for own in terms:
            total = functools.reduce(lambda a, b: a + b, [t[:1] for t in own])
            around = total
            for k in range(1, sources):
                ring = [(i, i // sources * sources + (i + k) % sources) for i in range(strips)]
                around = around + lax.ppermute(total, "strip", ring)
            fixed.append([around])
        terms = fixed

    long = ROWS_DEV + 2 * HALO
    parts = pl.pallas_call(
        functools.partial(template_kernel, len(terms[0])),
        in_specs=[vmem] * (2 * len(terms[0])),
        out_specs=[vmem] * strips,
        out_shape=[jax.ShapeDtypeStruct((long, share), F32)] * strips,
        scratch_shapes=[pltpu.VMEM((nrow + 2 * HALO, share), F32)],
        name="template",
        cost_estimate=pl.CostEstimate(flops=2_000_000, bytes_accessed=5_000_000, transcendentals=0),
    )(*terms[0], *terms[1])
    came = [None] * strips
    came[0] = parts[0]
    for k in reversed(range(1, strips)):
        came[k] = lax.ppermute(parts[k], "strip", [(i, i ^ k) for i in range(strips)])
    mine = jnp.stack(came[:: sources])
    sci_b, got_a, mine = lax.optimization_barrier((sci_b, got_a, mine))
    got_b = lax.all_to_all(sci_b, "strip", split_axis=0, concat_axis=0, tiled=True)
    if sources > 1:
        got_a = jnp.sum(got_a.reshape((blocks, sources) + got_a.shape[1:]), axis=1)
        got_b = jnp.sum(got_b.reshape((blocks, sources) + got_b.shape[1:]), axis=1)

    per_block = tile_cols // LANES
    if epochs == 4 and share == LANES:
        near = []
        for b in range(2):
            near.append(swap(mine, "epoch", b))
        cut = blocks // 2
        far_low = swap(near[1][:cut], "epoch", 0)
        far_high = swap(near[0][cut:], "epoch", 1)
        arrays = [mine, near[0], near[1], far_low, far_high]
        held = (0, 1, 2, 3)
    else:
        slots = [mine]
        for b in range(bits):
            slots = slots + [swap(s, "epoch", b) for s in slots]
        me = lax.axis_index("epoch")
        every = jnp.take(jnp.stack(slots), jnp.bitwise_xor(jnp.arange(epochs), me), axis=0)
        home = lax.axis_index("strip") // sources
        every = jnp.take(every, jnp.bitwise_xor(jnp.arange(blocks), home), axis=1)
        flat = jnp.transpose(every, (1, 2, 0, 3)).reshape(blocks, long, per_block, LANES)
        arrays = [jnp.transpose(flat, (0, 2, 1, 3)).reshape(blocks * per_block, long, LANES)]
        held = ()

    const = lambda b: (0, 0)
    convolve = pl.pallas_call(
        functools.partial(match_kernel, (held, nrow, ncol)),
        grid=(blocks,),
        in_specs=[hbm] * len(arrays)
        + [
            smem,
            pl.BlockSpec(toep_hi.shape, const),
            pl.BlockSpec(toep_lo.shape, const),
            pl.BlockSpec(band.shape, lambda b: (0, 0, 0)),
            pl.BlockSpec((1,) + got_a.shape[1:], lambda b: (b, 0, 0)),
        ],
        out_specs=pl.BlockSpec((ROWS_DEV, tile_cols), lambda b: (0, b)),
        out_shape=jax.ShapeDtypeStruct((ROWS_DEV, ncol), F32),
        scratch_shapes=[
            pltpu.VMEM((blocks * per_block + 2, long, LANES), F32),
            pltpu.VMEM((2, 2, ROWS_DEV, LANES), F32),
            pltpu.SemaphoreType.DMA((blocks, per_block)),
        ],
        name="convolve",
        compiler_params=pltpu.CompilerParams(vmem_limit_bytes=32 << 20),
        cost_estimate=pl.CostEstimate(flops=15_000_000_000, bytes_accessed=10_000_000, transcendentals=0),
    )
    matched = convolve(*arrays, psf_poly, toep_hi, toep_lo, band, got_a)
    unit = ROWS_DEV // 8
    rest = pl.BlockSpec((1, unit, ncol), lambda i: (0, FIRST_PART + i, 0))
    return pl.pallas_call(
        subtract_kernel,
        grid=(8 - FIRST_PART,),
        in_specs=[vmem, rest],
        out_specs=rest,
        out_shape=jax.ShapeDtypeStruct((1, ROWS_DEV, ncol), F32),
        input_output_aliases={1: 0},
        name="subtract",
        compiler_params=pltpu.CompilerParams(vmem_limit_bytes=16 << 20),
        cost_estimate=pl.CostEstimate(flops=1_000_000, bytes_accessed=6_000_000, transcendentals=0),
    )(pltpu.with_memory_space_constraint(got_b, pltpu.VMEM), matched[None])


def solution(mesh):
    in_specs = (
        P("epoch", "strip", None, None),
        P("epoch", "strip"),
        P("epoch", "strip"),
        P("epoch", None, None),
        P(),
        P(),
        P(),
        P(),
    )
    out_specs = P("epoch", "strip", None)

    return jax.shard_map(shards, mesh=mesh, in_specs=in_specs, out_specs=out_specs, check_vma=False)
```

```python
import functools

import jax
import jax.numpy as jnp
from jax import lax
from jax.experimental import pallas as pl
from jax.experimental.pallas import tpu as pltpu
from jax.sharding import PartitionSpec as P


ROWS_DEV = 256
HALO = 16
EDGE = 80
LANES = 128
F32 = jnp.float32
BF16 = jnp.bfloat16


def split(x):
    hi = x.astype(BF16)
    lo = (x - hi.astype(F32)).astype(BF16)
    return hi, lo


def dot(a, b, trans_b=False):
    dims = (((1,), (1 if trans_b else 0,)), ((), ()))
    return lax.dot_general(a, b, dims, preferred_element_type=F32)


def dot3(a, b, trans_b=False):
    a_hi, a_lo = a
    b_hi, b_lo = b
    both = dot(jnp.concatenate([a_hi, a_lo], axis=0), b_hi, trans_b)
    rows = a_hi.shape[0]
    return both[:rows] + (both[rows:] + dot(a_hi, b_lo, trans_b))


def start_and_wait(copies):
    for copy in copies:
        copy.start()
    for copy in copies:
        copy.wait()


def slot_order(count, order):
    bits = len(order)
    key = lambda j: sum(((j >> order[i]) & 1) << (bits - 1 - i) for i in range(bits))
    slots = sorted(range(count), key=key)
    return slots[: count // 2], slots[count // 2 :]


def warp_kernel(
    geom, kind_ref, heights_ref, invvar_ref, raw_ref, rmat_ref, cmat_ref,
    sci_a, sci_b, keep_a, send_a, keep_b, send_b,
    sci_s, num_s, wt_s, wide_s, rmat_s, cmat_s, chi_s, clo_s, top_s, ready_s, fetch_sems, sems, wt_sems,
):
    epochs, nrow, share, orders, tiles = geom
    step = pl.program_id(0)
    together, tile_rows, tile_cols = raw_ref.shape
    last = pl.num_programs(0) - 1
    per_col = heights_ref.shape[2]
    span = tile_rows + 8
    me = lax.axis_index("epoch")
    first_tile = lax.axis_index("strip") * tiles
    block = lax.div(first_tile, per_col)
    offset_in = lax.rem(first_tile, per_col)
    kinds = cmat_ref.shape[0]
    strips = sci_a.shape[0]
    rows_dev = nrow // strips
    rows_b = sci_b.shape[1]
    rows_a = rows_dev - rows_b
    edge = rows_b // 2
    nhalf = nrow // 2
    bhalf = strips // 2 * rows_b
    outs = (keep_a, send_a), (keep_b, send_b)

    def fetches(k):
        return [
            pltpu.make_async_copy(cmat_ref.at[k], cmat_s.at[k], fetch_sems.at[k, 0]),
            pltpu.make_async_copy(rmat_ref.at[k], rmat_s.at[k], fetch_sems.at[k, 1]),
        ]

    def strip_copies(s):
        base = s * rows_dev
        part = base // nhalf
        pairs = [(sci_s.at[pl.ds(base + edge, rows_a)], sci_a.at[s, pl.ds(0, rows_a)])]
        for i in range(2):
            source = pl.ds(base + i * (rows_dev - edge), edge)
            pairs.append((sci_s.at[source], sci_b.at[s, pl.ds(i * edge, edge)]))
            target = pl.ds((s - part * (strips // 2)) * rows_b + i * edge, edge)
            for slots, out in zip(slot_order(epochs, orders[part]), outs[part]):
                for place, j in enumerate(slots):
                    pairs.append((num_s.at[j, source], out.at[place, target]))
        return [pltpu.make_async_copy(a, b, sems.at[s, n]) for n, (a, b) in enumerate(pairs)]

    @pl.when(step == 0)
    def _():
        top_s[0] = lax.fori_loop(
            0, offset_in, lambda i, total: total + heights_ref[0, block, i], jnp.int32(0)
        )
        top_s[1] = 0
        first = kind_ref[0, 0]
        for i in range(kinds):
            ready_s[i] = 0
            for copy in fetches(lax.rem(first + i, kinds)):
                copy.start()
        if tiles != per_col:
            sci_s[...] = jnp.zeros_like(sci_s)
            num_s[...] = jnp.zeros_like(num_s)
            wt_s[...] = jnp.zeros_like(wt_s)

    def warped(i, top):
        t = step * together + i
        kind = kind_ref[0, t]
        height = heights_ref[0, block, offset_in + t]
        start = pl.multiple_of(jnp.minimum(lax.div(top, 8) * 8, nrow - span), 8)
        off = top - start
        across = dot3(split(raw_ref[i]), (chi_s[kind], clo_s[kind]), trans_b=True)
        live = lax.broadcasted_iota(jnp.int32, (tile_rows, tile_rows), 1) < height
        rows = jnp.concatenate(
            [jnp.where(live, rmat_s[kind], 0.0), jnp.zeros((8, tile_rows), F32)], axis=0
        )
        return t, height, start, off, dot3(split(pltpu.roll(rows, off, 0)), split(across))

    for i in range(together):
        kind = kind_ref[0, step * together + i]

        @pl.when(ready_s[kind] == 0)
        def _():
            for copy in fetches(kind):
                copy.wait()
            ready_s[kind] = 1

            def divide(n, carry):
                here = pl.ds(pl.multiple_of(n * (tile_cols // 8), tile_cols // 8), tile_cols // 8)
                chi_s[kind, here, :], clo_s[kind, here, :] = split(cmat_s[kind, here, :])
                return carry

            lax.fori_loop(0, 8, divide, 0)

    top = top_s[0]
    results = []
    for i in range(together):
        results.append((top, warped(i, top)))
        top = top + results[-1][1][1]
    top_s[0] = top
    after = top

    for top, (t, height, start, off, placed) in results:
        weight = invvar_ref[0, t]
        local = lax.broadcasted_iota(jnp.int32, (span, share), 0) - off
        own = (local >= 0) & (local < height)
        here = pl.ds(start, span)
        for q in range(epochs):
            columns = pl.ds(q * share, share)
            piece = placed[:, q * share : (q + 1) * share]
            slot = jnp.bitwise_xor(me, q)
            sci_s[here, columns] = jnp.where(own, piece, sci_s[here, columns])
            num_s[slot, here, :] = jnp.where(own, weight * piece, num_s[slot, here, :])
        flat = lax.broadcasted_iota(jnp.int32, wt_s.shape, 0) * share + lax.broadcasted_iota(
            jnp.int32, wt_s.shape, 1
        )
        wt_s[...] = jnp.where((flat >= top) & (flat < top + height), weight, wt_s[...])

    before = top_s[1]
    final = jnp.where(step == last, nrow, jnp.minimum(lax.div(after, 8) * 8, nrow - span))
    top_s[1] = final
    for s in range(strips):
        end = (s + 1) * rows_dev

        @pl.when((before < end) & (end <= final))
        def _():
            for copy in strip_copies(s):
                copy.start()

    @pl.when(step == last)
    def _():
        whalf = wt_s.shape[0] // 2
        copies = []
        for part, order in enumerate(orders):
            for slots, out in zip(slot_order(epochs, order), outs[part]):
                for place in range(len(slots)):
                    copies.append(
                        pltpu.make_async_copy(
                            wt_s.at[pl.ds(part * whalf, whalf)],
                            out.at[place, pl.ds(bhalf, whalf)],
                            wt_sems.at[len(copies)],
                        )
                    )
        per_strip = rows_dev // share
        wide_s[...] = jnp.zeros_like(wide_s)
        for s in range(strips):
            wide_s[s, pl.ds(0, per_strip), pl.ds(0, share)] = wt_s[pl.ds(s * per_strip, per_strip), :]
            copies.append(
                pltpu.make_async_copy(
                    wide_s.at[s], sci_a.at[s, pl.ds(rows_a, wide_s.shape[1])], wt_sems.at[len(copies)]
                )
            )
        start_and_wait(copies)
        for s in range(strips):
            for copy in strip_copies(s):
                copy.wait()
        for k in range(kinds):

            @pl.when(ready_s[k] == 0)
            def _():
                for copy in fetches(k):
                    copy.wait()


def added(refs, place):
    return functools.reduce(lambda a, b: a + b, [ref[0, place, :] for ref in refs])


def upright(row, width):
    return jnp.transpose(jnp.broadcast_to(row, (width, width)))


def template_kernel(terms, *refs):
    term_refs, out_refs, pad_s = refs[: 2 * terms], refs[2 * terms : -1], refs[-1]
    strips = len(out_refs)
    long, share = out_refs[0].shape
    rows_b = long - 2 * HALO
    edge = rows_b // 2
    half = strips // 2
    total = strips * rows_b
    blank = jnp.zeros((HALO, share), F32)
    pad_s[pl.ds(0, HALO), :] = blank
    pad_s[pl.ds(HALO + total, HALO), :] = blank
    per_strip = ROWS_DEV // share
    for part in range(2):
        own = term_refs[part * terms : (part + 1) * terms]
        weights = added(own, pl.ds(half * rows_b, half * per_strip))
        for s in range(half):
            below = jnp.concatenate(
                [upright(weights[s * per_strip + i : s * per_strip + i + 1, :], share) for i in range(per_strip)],
                axis=0,
            )
            for i in range(2):
                first = s * rows_b + i * edge
                under = below[i * (ROWS_DEV - edge) : i * (ROWS_DEV - edge) + edge]
                pad_s[pl.ds(HALO + part * half * rows_b + first, edge), :] = added(own, pl.ds(first, edge)) / under
    for k in range(strips):
        strip = jnp.bitwise_xor(lax.axis_index("strip"), k)
        out_refs[k][...] = pad_s[pl.ds(pl.multiple_of(strip * rows_b, 8), long), :]


def weigh_kernel(geom, sci_ref, *refs):
    epochs, orders, share = geom
    outs, num_s = refs[:4], refs[4]
    blocks = sci_ref.shape[0]
    rows_a = ROWS_DEV - 2 * EDGE
    per_strip = ROWS_DEV // share
    me = lax.axis_index("epoch")
    half = blocks // 2
    for part in range(2):
        for b in range(half):
            block = part * half + b
            lines = sci_ref[block, pl.ds(rows_a, 8), pl.ds(0, share)][:per_strip]
            below = jnp.concatenate([upright(lines[i : i + 1], share) for i in range(per_strip)], axis=0)
            weight = below[EDGE : EDGE + rows_a]
            for q in range(epochs):
                piece = sci_ref[block, pl.ds(0, rows_a), pl.ds(q * share, share)]
                num_s[jnp.bitwise_xor(me, q), pl.ds(b * rows_a, rows_a), :] = weight * piece
            for j in range(epochs):
                num_s[j, pl.ds(half * rows_a + b * per_strip, per_strip), :] = lines
        for slots, out in zip(slot_order(epochs, orders[part]), outs[2 * part : 2 * part + 2]):
            for place, j in enumerate(slots):
                out[place] = num_s[j]


def middle_kernel(terms, *refs):
    term_refs, outer_refs, out_ref = refs[: 2 * terms], refs[2 * terms : -1], refs[-1]
    blocks, long, share = out_ref.shape
    above = EDGE + HALO
    rows_a = long - 2 * above
    home = lax.div(lax.axis_index("strip"), lax.axis_size("strip") // blocks)
    half = blocks // 2
    for k, ref in enumerate(outer_refs):
        out_ref[k, pl.ds(0, above), :] = ref[pl.ds(0, above), :]
        out_ref[k, pl.ds(above + rows_a, above), :] = ref[pl.ds(above, above), :]
    for part in range(2):
        own = term_refs[part * terms : (part + 1) * terms]
        weights = added(own, pl.ds(half * rows_a, own[0].shape[1] - half * rows_a))
        per_strip = ROWS_DEV // share
        for b in range(half):
            below = jnp.concatenate(
                [upright(weights[b * per_strip + i : b * per_strip + i + 1, :], share) for i in range(per_strip)],
                axis=0,
            )
            value = added(own, pl.ds(b * rows_a, rows_a)) / below[EDGE : EDGE + rows_a]
            out_ref[jnp.bitwise_xor(home, part * half + b), pl.ds(above, rows_a), :] = value


def bands_kernel(psf_ref, toep_hi, toep_lo, band_ref):
    basis, _, ksize = psf_ref.shape
    margin = ksize // 2
    for k in range(basis):
        shape = (2 * LANES, LANES)
        tap = lax.broadcasted_iota(jnp.int32, shape, 0) - lax.broadcasted_iota(jnp.int32, shape, 1)
        tap = tap - (LANES // 2 - margin)
        value = jnp.zeros(shape, F32)
        for j in range(ksize):
            value = jnp.where(tap == j, psf_ref[k, 1, j], value)
        toep_hi[:, pl.ds(k * LANES, LANES)], toep_lo[:, pl.ds(k * LANES, LANES)] = split(value)
        shape = (LANES, LANES + 2 * HALO)
        tap = lax.broadcasted_iota(jnp.int32, shape, 1) - lax.broadcasted_iota(jnp.int32, shape, 0)
        tap = tap - (HALO - margin)
        value = jnp.zeros(shape, F32)
        for j in range(ksize):
            value = jnp.where(tap == j, psf_ref[k, 0, j], value)
        band_ref[k, pl.ds(0, LANES), :], band_ref[k, pl.ds(LANES, LANES), :] = split(value)


def match_kernel(geom, *refs):
    slots, nrow, ncol = geom
    count = max(len(slots), 1) + (len(slots) > 1)
    tile_refs = refs[:count]
    poly_ref, toep_hi, toep_lo, band_ref, sci_ref, out_ref, pad_s, row_s, sems = refs[count:]
    step = pl.program_id(0)
    blocks = pl.num_programs(0)
    tiles = pad_s.shape[0] - 2
    rows_dev = pad_s.shape[1] - 2 * HALO
    me = lax.axis_index("epoch")
    strip = lax.axis_index("strip")
    per_step = out_ref.shape[1] // LANES

    def bring(b):
        if not slots:
            for i in range(per_step):
                place = b * per_step + i
                pltpu.make_async_copy(tile_refs[0].at[place], pad_s.at[1 + place], sems.at[b, i]).start()
            return
        at = jnp.bitwise_xor(strip, b)
        for n, slot in enumerate(slots):
            target = pad_s.at[1 + b * per_step + jnp.bitwise_xor(me, slot)]
            if n < len(slots) - 1:
                pltpu.make_async_copy(tile_refs[n].at[at], target, sems.at[b, n]).start()
                continue
            cut = tile_refs[n].shape[0]

            @pl.when(at < cut)
            def _():
                pltpu.make_async_copy(tile_refs[n].at[at], target, sems.at[b, n]).start()

            @pl.when(at >= cut)
            def _():
                pltpu.make_async_copy(tile_refs[n + 1].at[at - cut], target, sems.at[b, n]).start()

    def await_block(b):
        for i in range(per_step):
            pltpu.make_async_copy(tile_refs[0].at[0], pad_s.at[1], sems.at[b, i]).wait()

    @pl.when(step == 0)
    def _():
        for b in range(tiles // per_step):
            bring(b)
        pad_s[0] = jnp.zeros(pad_s.shape[1:], F32)
        pad_s[tiles + 1] = jnp.zeros(pad_s.shape[1:], F32)
        shape = (rows_dev, LANES)
        counter = (strip * rows_dev + lax.broadcasted_iota(jnp.int32, shape, 0)).astype(F32)
        u = (2.0 * counter + 1.0) / nrow - 1.0
        for k in range(2):
            p = [poly_ref[me, k, i] for i in range(6)]
            row_s[k, 0] = p[0] + u * (p[1] + p[3] * u)
            row_s[k, 1] = p[2] + p[4] * u
        await_block(0)

    @pl.when(step < blocks - 1)
    def _():
        await_block(step + 1)

    lane = lax.broadcasted_iota(jnp.int32, pad_s.shape[1:], 1)
    base = step * per_step
    shifted = []
    for m in range(per_step + 1):
        mixed = jnp.where(lane < LANES // 2, pad_s[base + m + 1], pad_s[base + m])
        shifted.append(split(pltpu.roll(mixed, LANES // 2, 1)))
    toep = (toep_hi[...], toep_lo[...])
    for pair in range(per_step // 2):
        across = []
        for c in (2 * pair, 2 * pair + 1):
            window = tuple(
                jnp.concatenate([shifted[c][i], shifted[c + 1][i]], axis=1) for i in range(2)
            )
            across.append(dot3(window, toep))
        width = 2 * LANES
        cols = lax.broadcasted_iota(jnp.int32, (1, width), 1) + (base + 2 * pair) * LANES
        v = (2.0 * cols.astype(F32) + 1.0) / ncol - 1.0
        for part in range(rows_dev // LANES):
            total = 0.0
            for k in range(2):
                both = jnp.concatenate(
                    [a[part * LANES : part * LANES + LANES + 2 * HALO, k * LANES : (k + 1) * LANES] for a in across],
                    axis=1,
                )
                hi, lo = split(both)
                wide = dot(band_ref[k], hi)
                done = wide[:LANES] + (wide[LANES:] + dot(band_ref[k, pl.ds(0, LANES), :], lo))
                place = pl.ds(part * LANES, LANES)
                one = jnp.concatenate([row_s[k, 0, place, :]] * 2, axis=1)
                two = jnp.concatenate([row_s[k, 1, place, :]] * 2, axis=1)
                coeff = one + v * (two + poly_ref[me, k, 5] * v)
                total = total + coeff * done
            columns = pl.ds(pair * width, width)
            low = min(max(EDGE - part * LANES, 0), LANES)
            high = min(max(rows_dev - EDGE - part * LANES, 0), LANES)
            for begin, end, final in ((0, low, False), (low, high, True), (high, LANES, False)):
                if begin == end:
                    continue
                piece = total[begin:end]
                if final:
                    own = pl.ds(part * LANES + begin - EDGE, end - begin)
                    piece = sci_ref[0, own, columns] - piece
                out_ref[pl.ds(part * LANES + begin, end - begin), columns] = piece


def subtract_kernel(sci_ref, matched_ref, out_ref):
    i = pl.program_id(0)
    blocks, _, width = sci_ref.shape
    rows = out_ref.shape[1]
    for b in range(blocks):
        columns = pl.ds(b * width, width)
        science = sci_ref[b, pl.ds(pl.multiple_of(i * rows, rows), rows), :]
        out_ref[0, :, columns] = science - matched_ref[0, :, columns]


def swap(value, axis, bit):
    count = lax.axis_size(axis)
    return lax.ppermute(value, axis, [(i, i ^ (1 << bit)) for i in range(count)])


def shards(
    raw_tiles, tile_kind, tile_invvar, tile_heights, row_interp, col_interp, psf_profiles, psf_poly
):
    strips, epochs = lax.axis_size("strip"), lax.axis_size("epoch")
    _, tiles, tile_rows, tile_cols = raw_tiles.shape
    _, blocks, _ = tile_heights.shape
    ncol, nrow = blocks * tile_cols, ROWS_DEV * strips
    sources = strips // blocks
    share = tile_cols // epochs
    bits = epochs.bit_length() - 1
    orders = (tuple(range(bits)), tuple(reversed(range(bits))))
    wrows = nrow // share
    rows_b = 2 * EDGE
    rows_a = ROWS_DEV - rows_b
    long_half = strips // 2 * rows_b + wrows // 2
    smem = pl.BlockSpec(memory_space=pltpu.SMEM)
    hbm = pl.BlockSpec(memory_space=pl.ANY)
    vmem = pl.BlockSpec(memory_space=pltpu.VMEM)
    kinds = col_interp.shape[0]

    sci_shapes = [jax.ShapeDtypeStruct((strips, rows, tile_cols), F32) for rows in (rows_a + 8, rows_b)]
    send_shape = jax.ShapeDtypeStruct((epochs // 2, long_half, share), F32)
    together = 2 if tiles % 2 == 0 else 1
    sci_a, sci_b, keep_a, send_a, keep_b, send_b = pl.pallas_call(
        functools.partial(warp_kernel, (epochs, nrow, share, orders, tiles)),
        grid=(tiles // together,),
        in_specs=[
            smem,
            smem,
            smem,
            pl.BlockSpec((together, tile_rows, tile_cols), lambda t: (t, 0, 0)),
            hbm,
            hbm,
        ],
        out_specs=[hbm] * 6,
        out_shape=sci_shapes + [send_shape] * 4,
        scratch_shapes=[
            pltpu.VMEM((nrow, tile_cols), F32),
            pltpu.VMEM((epochs, nrow, share), F32),
            pltpu.VMEM((wrows, share), F32),
            pltpu.VMEM((strips, 8, tile_cols), F32),
            pltpu.VMEM((kinds, tile_rows, tile_rows), F32),
            pltpu.VMEM((kinds, tile_cols, tile_cols), F32),
            pltpu.VMEM((kinds, tile_cols, tile_cols), BF16),
            pltpu.VMEM((kinds, tile_cols, tile_cols), BF16),
            pltpu.SMEM((2,), jnp.int32),
            pltpu.SMEM((kinds,), jnp.int32),
            pltpu.SemaphoreType.DMA((kinds, 2)),
            pltpu.SemaphoreType.DMA((strips, 3 + 2 * epochs)),
            pltpu.SemaphoreType.DMA((2 * epochs + strips,)),
        ],
        name="warp",
        cost_estimate=pl.CostEstimate(flops=8_000_000_000, bytes_accessed=20_000_000, transcendentals=0),
    )(tile_kind, tile_heights, tile_invvar, raw_tiles[0], row_interp, col_interp)

    got_a = lax.all_to_all(sci_a, "strip", split_axis=0, concat_axis=0, tiled=True)
    basis, _, _ = psf_profiles.shape
    build_bands = pl.pallas_call(
        bands_kernel,
        in_specs=[smem],
        out_specs=[vmem] * 3,
        out_shape=[
            jax.ShapeDtypeStruct((2 * LANES, 2 * LANES), BF16),
            jax.ShapeDtypeStruct((2 * LANES, 2 * LANES), BF16),
            jax.ShapeDtypeStruct((basis, 2 * LANES, LANES + 2 * HALO), BF16),
        ],
        name="bands",
        cost_estimate=pl.CostEstimate(flops=10_000_000, bytes_accessed=500_000, transcendentals=0),
    )
    toep_hi, toep_lo, band = build_bands(psf_profiles)

    def reduced(keeps, sends):
        terms = [[keep] for keep in keeps]
        sends = list(sends)
        for i in range(bits):
            for part in range(2):
                terms[part].append(swap(sends[part], "epoch", orders[part][i]))
            left = epochs >> (i + 1)
            if left > 1:
                for part, own in enumerate(terms):
                    sends[part] = functools.reduce(lambda a, b: a + b, [t[left // 2 : left] for t in own])
        return terms

    terms = reduced([keep_a, keep_b], [send_a, send_b])
    if sources > 1:
        fixed = []
        for own in terms:
            total = functools.reduce(lambda a, b: a + b, [t[:1] for t in own])
            around = total
            for k in range(1, sources):
                ring = [(i, i // sources * sources + (i + k) % sources) for i in range(strips)]
                around = around + lax.ppermute(total, "strip", ring)
            fixed.append([around])
        terms = fixed

    long = ROWS_DEV + 2 * HALO
    long_b = rows_b + 2 * HALO
    parts = pl.pallas_call(
        functools.partial(template_kernel, len(terms[0])),
        in_specs=[vmem] * (2 * len(terms[0])),
        out_specs=[vmem] * strips,
        out_shape=[jax.ShapeDtypeStruct((long_b, share), F32)] * strips,
        scratch_shapes=[pltpu.VMEM((strips * rows_b + 2 * HALO, share), F32)],
        name="template",
        cost_estimate=pl.CostEstimate(flops=2_000_000, bytes_accessed=5_000_000, transcendentals=0),
    )(*terms[0], *terms[1])
    came = [None] * strips
    came[0] = parts[0]
    for k in reversed(range(1, strips)):
        came[k] = lax.ppermute(parts[k], "strip", [(i, i ^ k) for i in range(strips)])
    side_a = got_a
    if sources > 1:
        side_a = jnp.sum(got_a.reshape((blocks, sources) + got_a.shape[1:]), axis=1)
    long_a = blocks // 2 * (rows_a + ROWS_DEV // share)
    weighted_shape = jax.ShapeDtypeStruct((epochs // 2, long_a, share), F32)
    weigh = pl.pallas_call(
        functools.partial(weigh_kernel, (epochs, orders, share)),
        in_specs=[vmem],
        out_specs=[vmem] * 4,
        out_shape=[weighted_shape] * 4,
        scratch_shapes=[pltpu.VMEM((epochs, long_a, share), F32)],
        name="weigh",
        cost_estimate=pl.CostEstimate(flops=2_000_000, bytes_accessed=2_500_000, transcendentals=0),
    )
    weighted = weigh(side_a)
    middle_terms = reduced(weighted[0::2], weighted[1::2])
    outer = came[::sources]
    sci_b, got_a, *outer = lax.optimization_barrier((sci_b, got_a, *outer))
    merge = pl.pallas_call(
        functools.partial(middle_kernel, len(middle_terms[0])),
        in_specs=[vmem] * (2 * len(middle_terms[0]) + blocks),
        out_specs=vmem,
        out_shape=jax.ShapeDtypeStruct((blocks, long, share), F32),
        name="middle",
        cost_estimate=pl.CostEstimate(flops=500_000, bytes_accessed=4_000_000, transcendentals=0),
    )
    mine = merge(*middle_terms[0], *middle_terms[1], *outer)
    got_b = lax.all_to_all(sci_b, "strip", split_axis=0, concat_axis=0, tiled=True)
    got_a = got_a if sources == 1 else side_a
    if sources > 1:
        got_b = jnp.sum(got_b.reshape((blocks, sources) + got_b.shape[1:]), axis=1)

    per_block = tile_cols // LANES
    if epochs == 4 and share == LANES:
        near = []
        for b in range(2):
            near.append(swap(mine, "epoch", b))
        cut = blocks // 2
        far_low = swap(near[1][:cut], "epoch", 0)
        far_high = swap(near[0][cut:], "epoch", 1)
        arrays = [mine, near[0], near[1], far_low, far_high]
        held = (0, 1, 2, 3)
    else:
        slots = [mine]
        for b in range(bits):
            slots = slots + [swap(s, "epoch", b) for s in slots]
        me = lax.axis_index("epoch")
        every = jnp.take(jnp.stack(slots), jnp.bitwise_xor(jnp.arange(epochs), me), axis=0)
        home = lax.axis_index("strip") // sources
        every = jnp.take(every, jnp.bitwise_xor(jnp.arange(blocks), home), axis=1)
        flat = jnp.transpose(every, (1, 2, 0, 3)).reshape(blocks, long, per_block, LANES)
        arrays = [jnp.transpose(flat, (0, 2, 1, 3)).reshape(blocks * per_block, long, LANES)]
        held = ()

    const = lambda b: (0, 0)
    convolve = pl.pallas_call(
        functools.partial(match_kernel, (held, nrow, ncol)),
        grid=(blocks,),
        in_specs=[hbm] * len(arrays)
        + [
            smem,
            pl.BlockSpec(toep_hi.shape, const),
            pl.BlockSpec(toep_lo.shape, const),
            pl.BlockSpec(band.shape, lambda b: (0, 0, 0)),
            pl.BlockSpec((1,) + got_a.shape[1:], lambda b: (b, 0, 0)),
        ],
        out_specs=pl.BlockSpec((ROWS_DEV, tile_cols), lambda b: (0, b)),
        out_shape=jax.ShapeDtypeStruct((ROWS_DEV, ncol), F32),
        scratch_shapes=[
            pltpu.VMEM((blocks * per_block + 2, long, LANES), F32),
            pltpu.VMEM((2, 2, ROWS_DEV, LANES), F32),
            pltpu.SemaphoreType.DMA((blocks, per_block)),
        ],
        name="convolve",
        compiler_params=pltpu.CompilerParams(vmem_limit_bytes=32 << 20),
        cost_estimate=pl.CostEstimate(flops=15_000_000_000, bytes_accessed=10_000_000, transcendentals=0),
    )
    matched = convolve(*arrays, psf_poly, toep_hi, toep_lo, band, got_a)
    unit = ROWS_DEV // 16
    outside = EDGE // unit
    rest = pl.BlockSpec(
        (1, unit, ncol), lambda i: (0, jnp.where(i < outside, i, i + rows_a // unit), 0)
    )
    return pl.pallas_call(
        subtract_kernel,
        grid=(2 * outside,),
        in_specs=[vmem, rest],
        out_specs=rest,
        out_shape=jax.ShapeDtypeStruct((1, ROWS_DEV, ncol), F32),
        input_output_aliases={1: 0},
        name="subtract",
        compiler_params=pltpu.CompilerParams(vmem_limit_bytes=16 << 20),
        cost_estimate=pl.CostEstimate(flops=1_000_000, bytes_accessed=6_000_000, transcendentals=0),
    )(pltpu.with_memory_space_constraint(got_b, pltpu.VMEM), matched[None])


def solution(mesh):
    in_specs = (
        P("epoch", "strip", None, None),
        P("epoch", "strip"),
        P("epoch", "strip"),
        P("epoch", None, None),
        P(),
        P(),
        P(),
        P(),
    )
    out_specs = P("epoch", "strip", None)

    return jax.shard_map(shards, mesh=mesh, in_specs=in_specs, out_specs=out_specs, check_vma=False)
```

```python
import functools

import jax
import jax.numpy as jnp
from jax import lax
from jax.experimental import pallas as pl
from jax.experimental.pallas import tpu as pltpu
from jax.sharding import PartitionSpec as P


ROWS_DEV = 256
HALO = 16
FIRST_PART = 3
LANES = 128
F32 = jnp.float32
BF16 = jnp.bfloat16


def split(x):
    hi = x.astype(BF16)
    lo = (x - hi.astype(F32)).astype(BF16)
    return hi, lo


def dot(a, b, trans_b=False):
    dims = (((1,), (1 if trans_b else 0,)), ((), ()))
    return lax.dot_general(a, b, dims, preferred_element_type=F32)


def dot3(a, b, trans_b=False):
    a_hi, a_lo = a
    b_hi, b_lo = b
    both = dot(jnp.concatenate([a_hi, a_lo], axis=0), b_hi, trans_b)
    rows = a_hi.shape[0]
    return both[:rows] + (both[rows:] + dot(a_hi, b_lo, trans_b))


def start_and_wait(copies):
    for copy in copies:
        copy.start()
    for copy in copies:
        copy.wait()


def slot_order(count, order):
    bits = len(order)
    key = lambda j: sum(((j >> order[i]) & 1) << (bits - 1 - i) for i in range(bits))
    slots = sorted(range(count), key=key)
    return slots[: count // 2], slots[count // 2 :]


def warp_kernel(
    geom, kind_ref, heights_ref, invvar_ref, raw_ref, rmat_ref, cmat_ref,
    sci_a, sci_b, keep_a, send_a, keep_b, send_b,
    sci_s, num_s, wt_s, rmat_s, cmat_s, chi_s, clo_s, top_s, ready_s, fetch_sems, sems, wt_sems,
):
    epochs, nrow, share, orders, tiles = geom
    step = pl.program_id(0)
    together, tile_rows, tile_cols = raw_ref.shape
    last = pl.num_programs(0) - 1
    per_col = heights_ref.shape[2]
    span = tile_rows + 8
    me = lax.axis_index("epoch")
    first_tile = lax.axis_index("strip") * tiles
    block = lax.div(first_tile, per_col)
    offset_in = lax.rem(first_tile, per_col)
    kinds = cmat_ref.shape[0]
    strips, rows_a, _ = sci_a.shape
    rows_dev = rows_a + sci_b.shape[1]
    nhalf = nrow // 2
    outs = (keep_a, send_a), (keep_b, send_b)

    def fetches(k):
        return [
            pltpu.make_async_copy(cmat_ref.at[k], cmat_s.at[k], fetch_sems.at[k, 0]),
            pltpu.make_async_copy(rmat_ref.at[k], rmat_s.at[k], fetch_sems.at[k, 1]),
        ]

    def strip_copies(s):
        base = s * rows_dev
        part = base // nhalf
        pairs = [
            (sci_s.at[pl.ds(base, rows_a)], sci_a.at[s]),
            (sci_s.at[pl.ds(base + rows_a, rows_dev - rows_a)], sci_b.at[s]),
        ]
        for slots, out in zip(slot_order(epochs, orders[part]), outs[part]):
            for place, j in enumerate(slots):
                pairs.append(
                    (num_s.at[j, pl.ds(base, rows_dev)], out.at[place, pl.ds(base - part * nhalf, rows_dev)])
                )
        return [pltpu.make_async_copy(a, b, sems.at[s, n]) for n, (a, b) in enumerate(pairs)]

    @pl.when(step == 0)
    def _():
        top_s[0] = lax.fori_loop(
            0, offset_in, lambda i, total: total + heights_ref[0, block, i], jnp.int32(0)
        )
        top_s[1] = 0
        first = kind_ref[0, 0]
        for i in range(kinds):
            ready_s[i] = 0
            for copy in fetches(lax.rem(first + i, kinds)):
                copy.start()
        if tiles != per_col:
            sci_s[...] = jnp.zeros_like(sci_s)
            num_s[...] = jnp.zeros_like(num_s)
            wt_s[...] = jnp.zeros_like(wt_s)

    def warped(i, top):
        t = step * together + i
        kind = kind_ref[0, t]
        height = heights_ref[0, block, offset_in + t]
        start = pl.multiple_of(jnp.minimum(lax.div(top, 8) * 8, nrow - span), 8)
        off = top - start
        across = dot3(split(raw_ref[i]), (chi_s[kind], clo_s[kind]), trans_b=True)
        live = lax.broadcasted_iota(jnp.int32, (tile_rows, tile_rows), 1) < height
        rows = jnp.concatenate(
            [jnp.where(live, rmat_s[kind], 0.0), jnp.zeros((8, tile_rows), F32)], axis=0
        )
        return t, height, start, off, dot3(split(pltpu.roll(rows, off, 0)), split(across))

    for i in range(together):
        kind = kind_ref[0, step * together + i]

        @pl.when(ready_s[kind] == 0)
        def _():
            for copy in fetches(kind):
                copy.wait()
            ready_s[kind] = 1

            def divide(n, carry):
                here = pl.ds(pl.multiple_of(n * (tile_cols // 8), tile_cols // 8), tile_cols // 8)
                chi_s[kind, here, :], clo_s[kind, here, :] = split(cmat_s[kind, here, :])
                return carry

            lax.fori_loop(0, 8, divide, 0)

    top = top_s[0]
    results = []
    for i in range(together):
        results.append((top, warped(i, top)))
        top = top + results[-1][1][1]
    top_s[0] = top
    after = top

    for top, (t, height, start, off, placed) in results:
        weight = invvar_ref[0, t]
        local = lax.broadcasted_iota(jnp.int32, (span, share), 0) - off
        own = (local >= 0) & (local < height)
        here = pl.ds(start, span)
        for q in range(epochs):
            columns = pl.ds(q * share, share)
            piece = placed[:, q * share : (q + 1) * share]
            slot = jnp.bitwise_xor(me, q)
            sci_s[here, columns] = jnp.where(own, piece, sci_s[here, columns])
            num_s[slot, here, :] = jnp.where(own, weight * piece, num_s[slot, here, :])
        flat = lax.broadcasted_iota(jnp.int32, wt_s.shape, 0) * share + lax.broadcasted_iota(
            jnp.int32, wt_s.shape, 1
        )
        wt_s[...] = jnp.where((flat >= top) & (flat < top + height), weight, wt_s[...])

    before = top_s[1]
    final = jnp.where(step == last, nrow, jnp.minimum(lax.div(after, 8) * 8, nrow - span))
    top_s[1] = final
    for s in range(strips):
        end = (s + 1) * rows_dev

        @pl.when((before < end) & (end <= final))
        def _():
            for copy in strip_copies(s):
                copy.start()

    @pl.when(step == last)
    def _():
        whalf = wt_s.shape[0] // 2
        copies = []
        for part, order in enumerate(orders):
            for slots, out in zip(slot_order(epochs, order), outs[part]):
                for place in range(len(slots)):
                    copies.append(
                        pltpu.make_async_copy(
                            wt_s.at[pl.ds(part * whalf, whalf)],
                            out.at[place, pl.ds(nhalf, whalf)],
                            wt_sems.at[len(copies)],
                        )
                    )
        start_and_wait(copies)
        for s in range(strips):
            for copy in strip_copies(s):
                copy.wait()
        for k in range(kinds):

            @pl.when(ready_s[k] == 0)
            def _():
                for copy in fetches(k):
                    copy.wait()


def template_kernel(terms, *refs):
    term_refs, out_refs, pad_s = refs[: 2 * terms], refs[2 * terms : -1], refs[-1]
    strips = len(out_refs)
    long, share = out_refs[0].shape
    rows_dev = long - 2 * HALO
    nrow = strips * rows_dev
    nhalf = nrow // 2
    whalf = nhalf // share
    edge = jnp.zeros((HALO, share), F32)
    pad_s[pl.ds(0, HALO), :] = edge
    pad_s[pl.ds(HALO + nrow, HALO), :] = edge
    for part in range(2):
        own = term_refs[part * terms : (part + 1) * terms]
        add = lambda place: functools.reduce(lambda a, b: a + b, [ref[0, place, :] for ref in own])
        weights = add(pl.ds(nhalf, whalf))
        for i in range(whalf):
            below = jnp.transpose(jnp.broadcast_to(weights[i : i + 1, :], (share, share)))
            pad_s[pl.ds(HALO + part * nhalf + i * share, share), :] = add(pl.ds(i * share, share)) / below
    for k in range(strips):
        strip = jnp.bitwise_xor(lax.axis_index("strip"), k)
        out_refs[k][...] = pad_s[pl.ds(pl.multiple_of(strip * rows_dev, rows_dev), long), :]


def bands_kernel(psf_ref, toep_hi, toep_lo, band_ref):
    basis, _, ksize = psf_ref.shape
    margin = ksize // 2
    for k in range(basis):
        shape = (2 * LANES, LANES)
        tap = lax.broadcasted_iota(jnp.int32, shape, 0) - lax.broadcasted_iota(jnp.int32, shape, 1)
        tap = tap - (LANES // 2 - margin)
        value = jnp.zeros(shape, F32)
        for j in range(ksize):
            value = jnp.where(tap == j, psf_ref[k, 1, j], value)
        toep_hi[:, pl.ds(k * LANES, LANES)], toep_lo[:, pl.ds(k * LANES, LANES)] = split(value)
        shape = (LANES, LANES + 2 * HALO)
        tap = lax.broadcasted_iota(jnp.int32, shape, 1) - lax.broadcasted_iota(jnp.int32, shape, 0)
        tap = tap - (HALO - margin)
        value = jnp.zeros(shape, F32)
        for j in range(ksize):
            value = jnp.where(tap == j, psf_ref[k, 0, j], value)
        band_ref[k, pl.ds(0, LANES), :], band_ref[k, pl.ds(LANES, LANES), :] = split(value)


def match_kernel(geom, *refs):
    slots, nrow, ncol = geom
    count = max(len(slots), 1) + (len(slots) > 1)
    tile_refs = refs[:count]
    poly_ref, toep_hi, toep_lo, band_ref, sci_ref, out_ref, pad_s, row_s = refs[count:]
    step = pl.program_id(0)
    blocks = pl.num_programs(0)
    tiles = pad_s.shape[0] - 2
    rows_dev = pad_s.shape[1] - 2 * HALO
    me = lax.axis_index("epoch")
    strip = lax.axis_index("strip")
    per_step = out_ref.shape[1] // LANES

    def bring(b):
        if not slots:
            for i in range(per_step):
                place = b * per_step + i
                pad_s[1 + place] = tile_refs[0][place]
            return
        at = jnp.bitwise_xor(strip, b)
        for n, slot in enumerate(slots[:-1]):
            pad_s[1 + b * per_step + jnp.bitwise_xor(me, slot)] = tile_refs[n][at]
        place = 1 + b * per_step + jnp.bitwise_xor(me, slots[-1])
        cut = tile_refs[-1].shape[0]

        @pl.when(at < cut)
        def _():
            pad_s[place] = tile_refs[-2][at]

        @pl.when(at >= cut)
        def _():
            pad_s[place] = tile_refs[-1][at - cut]

    @pl.when(step == 0)
    def _():
        bring(0)
        pad_s[0] = jnp.zeros(pad_s.shape[1:], F32)
        pad_s[tiles + 1] = jnp.zeros(pad_s.shape[1:], F32)
        shape = (rows_dev, LANES)
        counter = (strip * rows_dev + lax.broadcasted_iota(jnp.int32, shape, 0)).astype(F32)
        u = (2.0 * counter + 1.0) / nrow - 1.0
        for k in range(2):
            p = [poly_ref[me, k, i] for i in range(6)]
            row_s[k, 0] = p[0] + u * (p[1] + p[3] * u)
            row_s[k, 1] = p[2] + p[4] * u

    @pl.when(step < blocks - 1)
    def _():
        bring(step + 1)

    lane = lax.broadcasted_iota(jnp.int32, pad_s.shape[1:], 1)
    base = step * per_step
    shifted = []
    for m in range(per_step + 1):
        mixed = jnp.where(lane < LANES // 2, pad_s[base + m + 1], pad_s[base + m])
        shifted.append(split(pltpu.roll(mixed, LANES // 2, 1)))
    toep = (toep_hi[...], toep_lo[...])
    for pair in range(per_step // 2):
        across = []
        for c in (2 * pair, 2 * pair + 1):
            window = tuple(
                jnp.concatenate([shifted[c][i], shifted[c + 1][i]], axis=1) for i in range(2)
            )
            across.append(dot3(window, toep))
        width = 2 * LANES
        cols = lax.broadcasted_iota(jnp.int32, (1, width), 1) + (base + 2 * pair) * LANES
        v = (2.0 * cols.astype(F32) + 1.0) / ncol - 1.0
        for part in range(rows_dev // LANES):
            total = 0.0
            for k in range(2):
                both = jnp.concatenate(
                    [a[part * LANES : part * LANES + LANES + 2 * HALO, k * LANES : (k + 1) * LANES] for a in across],
                    axis=1,
                )
                hi, lo = split(both)
                wide = dot(band_ref[k], hi)
                done = wide[:LANES] + (wide[LANES:] + dot(band_ref[k, pl.ds(0, LANES), :], lo))
                place = pl.ds(part * LANES, LANES)
                one = jnp.concatenate([row_s[k, 0, place, :]] * 2, axis=1)
                two = jnp.concatenate([row_s[k, 1, place, :]] * 2, axis=1)
                coeff = one + v * (two + poly_ref[me, k, 5] * v)
                total = total + coeff * done
            columns = pl.ds(pair * width, width)
            ready = min(max(sci_ref.shape[1] - part * LANES, 0), LANES)
            if ready:
                here = pl.ds(part * LANES, ready)
                out_ref[here, columns] = sci_ref[0, here, columns] - total[:ready]
            if ready < LANES:
                out_ref[pl.ds(part * LANES + ready, LANES - ready), columns] = total[ready:]


def subtract_kernel(sci_ref, matched_ref, out_ref):
    i = pl.program_id(0)
    blocks, _, width = sci_ref.shape
    rows = out_ref.shape[1]
    for b in range(blocks):
        columns = pl.ds(b * width, width)
        science = sci_ref[b, pl.ds(pl.multiple_of(i * rows, rows), rows), :]
        out_ref[0, :, columns] = science - matched_ref[0, :, columns]


def swap(value, axis, bit):
    count = lax.axis_size(axis)
    return lax.ppermute(value, axis, [(i, i ^ (1 << bit)) for i in range(count)])


def shards(
    raw_tiles, tile_kind, tile_invvar, tile_heights, row_interp, col_interp, psf_profiles, psf_poly
):
    strips, epochs = lax.axis_size("strip"), lax.axis_size("epoch")
    _, tiles, tile_rows, tile_cols = raw_tiles.shape
    _, blocks, _ = tile_heights.shape
    ncol, nrow = blocks * tile_cols, ROWS_DEV * strips
    sources = strips // blocks
    share = tile_cols // epochs
    bits = epochs.bit_length() - 1
    orders = (tuple(range(bits)), tuple(reversed(range(bits))))
    nhalf = nrow // 2
    wrows = nrow // share
    long_half = nhalf + wrows // 2
    smem = pl.BlockSpec(memory_space=pltpu.SMEM)
    hbm = pl.BlockSpec(memory_space=pl.ANY)
    vmem = pl.BlockSpec(memory_space=pltpu.VMEM)
    kinds = col_interp.shape[0]

    first_rows = ROWS_DEV * FIRST_PART // 8
    sci_shapes = [
        jax.ShapeDtypeStruct((strips, rows, tile_cols), F32) for rows in (first_rows, ROWS_DEV - first_rows)
    ]
    send_shape = jax.ShapeDtypeStruct((epochs // 2, long_half, share), F32)
    together = 2 if tiles % 2 == 0 else 1
    sci_a, sci_b, keep_a, send_a, keep_b, send_b = pl.pallas_call(
        functools.partial(warp_kernel, (epochs, nrow, share, orders, tiles)),
        grid=(tiles // together,),
        in_specs=[
            smem,
            smem,
            smem,
            pl.BlockSpec((together, tile_rows, tile_cols), lambda t: (t, 0, 0)),
            hbm,
            hbm,
        ],
        out_specs=[hbm] * 6,
        out_shape=sci_shapes + [send_shape] * 4,
        scratch_shapes=[
            pltpu.VMEM((nrow, tile_cols), F32),
            pltpu.VMEM((epochs, nrow, share), F32),
            pltpu.VMEM((wrows, share), F32),
            pltpu.VMEM((kinds, tile_rows, tile_rows), F32),
            pltpu.VMEM((kinds, tile_cols, tile_cols), F32),
            pltpu.VMEM((kinds, tile_cols, tile_cols), BF16),
            pltpu.VMEM((kinds, tile_cols, tile_cols), BF16),
            pltpu.SMEM((2,), jnp.int32),
            pltpu.SMEM((kinds,), jnp.int32),
            pltpu.SemaphoreType.DMA((kinds, 2)),
            pltpu.SemaphoreType.DMA((strips, 2 + epochs)),
            pltpu.SemaphoreType.DMA((2 * epochs,)),
        ],
        name="warp",
        cost_estimate=pl.CostEstimate(flops=8_000_000_000, bytes_accessed=20_000_000, transcendentals=0),
    )(tile_kind, tile_heights, tile_invvar, raw_tiles[0], row_interp, col_interp)

    got_a = lax.all_to_all(sci_a, "strip", split_axis=0, concat_axis=0, tiled=True)

    basis, _, _ = psf_profiles.shape
    build_bands = pl.pallas_call(
        bands_kernel,
        in_specs=[smem],
        out_specs=[vmem] * 3,
        out_shape=[
            jax.ShapeDtypeStruct((2 * LANES, 2 * LANES), BF16),
            jax.ShapeDtypeStruct((2 * LANES, 2 * LANES), BF16),
            jax.ShapeDtypeStruct((basis, 2 * LANES, LANES + 2 * HALO), BF16),
        ],
        name="bands",
        cost_estimate=pl.CostEstimate(flops=10_000_000, bytes_accessed=500_000, transcendentals=0),
    )
    toep_hi, toep_lo, band = build_bands(psf_profiles)

    terms = [[keep_a], [keep_b]]
    sends = [send_a, send_b]
    for i in range(bits):
        for part in range(2):
            terms[part].append(swap(sends[part], "epoch", orders[part][i]))
        left = epochs >> (i + 1)
        if left > 1:
            sends = [
                functools.reduce(lambda a, b: a + b, [t[left // 2 : left] for t in own]) for own in terms
            ]
    if sources > 1:
        fixed = []
        for own in terms:
            total = functools.reduce(lambda a, b: a + b, [t[:1] for t in own])
            around = total
            for k in range(1, sources):
                ring = [(i, i // sources * sources + (i + k) % sources) for i in range(strips)]
                around = around + lax.ppermute(total, "strip", ring)
            fixed.append([around])
        terms = fixed

    long = ROWS_DEV + 2 * HALO
    parts = pl.pallas_call(
        functools.partial(template_kernel, len(terms[0])),
        in_specs=[vmem] * (2 * len(terms[0])),
        out_specs=[vmem] * strips,
        out_shape=[jax.ShapeDtypeStruct((long, share), F32)] * strips,
        scratch_shapes=[pltpu.VMEM((nrow + 2 * HALO, share), F32)],
        name="template",
        cost_estimate=pl.CostEstimate(flops=2_000_000, bytes_accessed=5_000_000, transcendentals=0),
    )(*terms[0], *terms[1])
    came = [None] * strips
    came[0] = parts[0]
    for k in reversed(range(1, strips)):
        came[k] = lax.ppermute(parts[k], "strip", [(i, i ^ k) for i in range(strips)])
    mine = jnp.stack(came[:: sources])
    sci_b, got_a, mine = lax.optimization_barrier((sci_b, got_a, mine))
    got_b = lax.all_to_all(sci_b, "strip", split_axis=0, concat_axis=0, tiled=True)
    if sources > 1:
        got_a = jnp.sum(got_a.reshape((blocks, sources) + got_a.shape[1:]), axis=1)
        got_b = jnp.sum(got_b.reshape((blocks, sources) + got_b.shape[1:]), axis=1)

    per_block = tile_cols // LANES
    if epochs == 4 and share == LANES:
        near = []
        for b in range(2):
            near.append(swap(mine, "epoch", b))
        cut = blocks // 2
        far_low = swap(near[1][:cut], "epoch", 0)
        far_high = swap(near[0][cut:], "epoch", 1)
        arrays = [mine, near[0], near[1], far_low, far_high]
        held = (0, 1, 2, 3)
    else:
        slots = [mine]
        for b in range(bits):
            slots = slots + [swap(s, "epoch", b) for s in slots]
        me = lax.axis_index("epoch")
        every = jnp.take(jnp.stack(slots), jnp.bitwise_xor(jnp.arange(epochs), me), axis=0)
        home = lax.axis_index("strip") // sources
        every = jnp.take(every, jnp.bitwise_xor(jnp.arange(blocks), home), axis=1)
        flat = jnp.transpose(every, (1, 2, 0, 3)).reshape(blocks, long, per_block, LANES)
        arrays = [jnp.transpose(flat, (0, 2, 1, 3)).reshape(blocks * per_block, long, LANES)]
        held = ()

    const = lambda b: (0, 0)
    convolve = pl.pallas_call(
        functools.partial(match_kernel, (held, nrow, ncol)),
        grid=(blocks,),
        in_specs=[vmem] * len(arrays)
        + [
            smem,
            pl.BlockSpec(toep_hi.shape, const),
            pl.BlockSpec(toep_lo.shape, const),
            pl.BlockSpec(band.shape, lambda b: (0, 0, 0)),
            pl.BlockSpec((1,) + got_a.shape[1:], lambda b: (b, 0, 0)),
        ],
        out_specs=pl.BlockSpec((ROWS_DEV, tile_cols), lambda b: (0, b)),
        out_shape=jax.ShapeDtypeStruct((ROWS_DEV, ncol), F32),
        scratch_shapes=[
            pltpu.VMEM((blocks * per_block + 2, long, LANES), F32),
            pltpu.VMEM((2, 2, ROWS_DEV, LANES), F32),
        ],
        name="convolve",
        compiler_params=pltpu.CompilerParams(vmem_limit_bytes=28 << 20),
        cost_estimate=pl.CostEstimate(flops=15_000_000_000, bytes_accessed=10_000_000, transcendentals=0),
    )
    arrays = [pltpu.with_memory_space_constraint(x, pltpu.VMEM) for x in arrays]
    matched = convolve(*arrays, psf_poly, toep_hi, toep_lo, band, got_a)
    unit = ROWS_DEV // 8
    rest = pl.BlockSpec((1, unit, ncol), lambda i: (0, FIRST_PART + i, 0))
    return pl.pallas_call(
        subtract_kernel,
        grid=(8 - FIRST_PART,),
        in_specs=[vmem, rest],
        out_specs=rest,
        out_shape=jax.ShapeDtypeStruct((1, ROWS_DEV, ncol), F32),
        input_output_aliases={1: 0},
        name="subtract",
        compiler_params=pltpu.CompilerParams(vmem_limit_bytes=16 << 20),
        cost_estimate=pl.CostEstimate(flops=1_000_000, bytes_accessed=6_000_000, transcendentals=0),
    )(pltpu.with_memory_space_constraint(got_b, pltpu.VMEM), matched[None])


def solution(mesh):
    in_specs = (
        P("epoch", "strip", None, None),
        P("epoch", "strip"),
        P("epoch", "strip"),
        P("epoch", None, None),
        P(),
        P(),
        P(),
        P(),
    )
    out_specs = P("epoch", "strip", None)

    return jax.shard_map(shards, mesh=mesh, in_specs=in_specs, out_specs=out_specs, check_vma=False)
```

```python
import functools

import jax
import jax.numpy as jnp
from jax import lax
from jax.experimental import pallas as pl
from jax.experimental.pallas import tpu as pltpu
from jax.sharding import PartitionSpec as P


ROWS_DEV = 256
HALO = 16
FIRST_PART = 3
LANES = 128
F32 = jnp.float32
BF16 = jnp.bfloat16


def split(x):
    hi = x.astype(BF16)
    lo = (x - hi.astype(F32)).astype(BF16)
    return hi, lo


def dot(a, b, trans_b=False):
    dims = (((1,), (1 if trans_b else 0,)), ((), ()))
    return lax.dot_general(a, b, dims, preferred_element_type=F32)


def dot3(a, b, trans_b=False):
    a_hi, a_lo = a
    b_hi, b_lo = b
    both = dot(jnp.concatenate([a_hi, a_lo], axis=0), b_hi, trans_b)
    rows = a_hi.shape[0]
    return both[:rows] + (both[rows:] + dot(a_hi, b_lo, trans_b))


def start_and_wait(copies):
    for copy in copies:
        copy.start()
    for copy in copies:
        copy.wait()


def slot_order(count, order):
    bits = len(order)
    key = lambda j: sum(((j >> order[i]) & 1) << (bits - 1 - i) for i in range(bits))
    slots = sorted(range(count), key=key)
    return slots[: count // 2], slots[count // 2 :]


def warp_kernel(
    geom, kind_ref, heights_ref, invvar_ref, raw_ref, rmat_ref, cmat_ref, *refs
):
    strips = lax.axis_size("strip")
    sci_a, sci_b = refs[:strips], refs[strips : 2 * strips]
    keep_a, send_a, keep_b, send_b = refs[2 * strips : 2 * strips + 4]
    (
        sci_s, num_s, wt_s, rmat_s, cmat_s, chi_s, clo_s, top_s, ready_s, fetch_sems, sems, sci_sems, wt_sems
    ) = refs[2 * strips + 4 :]
    epochs, nrow, share, orders, tiles = geom
    step = pl.program_id(0)
    together, tile_rows, tile_cols = raw_ref.shape
    last = pl.num_programs(0) - 1
    per_col = heights_ref.shape[2]
    span = tile_rows + 8
    me = lax.axis_index("epoch")
    first_tile = lax.axis_index("strip") * tiles
    block = lax.div(first_tile, per_col)
    offset_in = lax.rem(first_tile, per_col)
    kinds = cmat_ref.shape[0]
    rows_a, rows_b = sci_a[0].shape[0], sci_b[0].shape[0]
    rows_dev = rows_a + rows_b
    nhalf = nrow // 2
    outs = (keep_a, send_a), (keep_b, send_b)

    def fetches(k):
        return [
            pltpu.make_async_copy(cmat_ref.at[k], cmat_s.at[k], fetch_sems.at[k, 0]),
            pltpu.make_async_copy(rmat_ref.at[k], rmat_s.at[k], fetch_sems.at[k, 1]),
        ]

    def strip_copies(s):
        base = s * rows_dev
        part = base // nhalf
        pairs = []
        for slots, out in zip(slot_order(epochs, orders[part]), outs[part]):
            for place, j in enumerate(slots):
                pairs.append(
                    (num_s.at[j, pl.ds(base, rows_dev)], out.at[place, pl.ds(base - part * nhalf, rows_dev)])
                )
        return [pltpu.make_async_copy(a, b, sems.at[s, n]) for n, (a, b) in enumerate(pairs)]

    def partner(k):
        return jnp.bitwise_xor(lax.axis_index("strip"), k)

    def sci_copies(k):
        base = pl.multiple_of(partner(k) * rows_dev, rows_dev)
        return [
            pltpu.make_async_copy(sci_s.at[pl.ds(base, rows_a)], sci_a[k], sci_sems.at[k, 0]),
            pltpu.make_async_copy(sci_s.at[pl.ds(base + rows_a, rows_b)], sci_b[k], sci_sems.at[k, 1]),
        ]

    @pl.when(step == 0)
    def _():
        top_s[0] = lax.fori_loop(
            0, offset_in, lambda i, total: total + heights_ref[0, block, i], jnp.int32(0)
        )
        top_s[1] = 0
        first = kind_ref[0, 0]
        for i in range(kinds):
            ready_s[i] = 0
            for copy in fetches(lax.rem(first + i, kinds)):
                copy.start()
        if tiles != per_col:
            sci_s[...] = jnp.zeros_like(sci_s)
            num_s[...] = jnp.zeros_like(num_s)
            wt_s[...] = jnp.zeros_like(wt_s)

    def warped(i, top):
        t = step * together + i
        kind = kind_ref[0, t]
        height = heights_ref[0, block, offset_in + t]
        start = pl.multiple_of(jnp.minimum(lax.div(top, 8) * 8, nrow - span), 8)
        off = top - start
        across = dot3(split(raw_ref[i]), (chi_s[kind], clo_s[kind]), trans_b=True)
        live = lax.broadcasted_iota(jnp.int32, (tile_rows, tile_rows), 1) < height
        rows = jnp.concatenate(
            [jnp.where(live, rmat_s[kind], 0.0), jnp.zeros((8, tile_rows), F32)], axis=0
        )
        return t, height, start, off, dot3(split(pltpu.roll(rows, off, 0)), split(across))

    for i in range(together):
        kind = kind_ref[0, step * together + i]

        @pl.when(ready_s[kind] == 0)
        def _():
            for copy in fetches(kind):
                copy.wait()
            ready_s[kind] = 1

            def divide(n, carry):
                here = pl.ds(pl.multiple_of(n * (tile_cols // 8), tile_cols // 8), tile_cols // 8)
                chi_s[kind, here, :], clo_s[kind, here, :] = split(cmat_s[kind, here, :])
                return carry

            lax.fori_loop(0, 8, divide, 0)

    top = top_s[0]
    results = []
    for i in range(together):
        results.append((top, warped(i, top)))
        top = top + results[-1][1][1]
    top_s[0] = top
    after = top

    for top, (t, height, start, off, placed) in results:
        weight = invvar_ref[0, t]
        local = lax.broadcasted_iota(jnp.int32, (span, share), 0) - off
        own = (local >= 0) & (local < height)
        here = pl.ds(start, span)
        for q in range(epochs):
            columns = pl.ds(q * share, share)
            piece = placed[:, q * share : (q + 1) * share]
            slot = jnp.bitwise_xor(me, q)
            sci_s[here, columns] = jnp.where(own, piece, sci_s[here, columns])
            num_s[slot, here, :] = jnp.where(own, weight * piece, num_s[slot, here, :])
        flat = lax.broadcasted_iota(jnp.int32, wt_s.shape, 0) * share + lax.broadcasted_iota(
            jnp.int32, wt_s.shape, 1
        )
        wt_s[...] = jnp.where((flat >= top) & (flat < top + height), weight, wt_s[...])

    before = top_s[1]
    final = jnp.where(step == last, nrow, jnp.minimum(lax.div(after, 8) * 8, nrow - span))
    top_s[1] = final
    for s in range(strips):
        end = (s + 1) * rows_dev

        @pl.when((before < end) & (end <= final))
        def _():
            for copy in strip_copies(s):
                copy.start()

    for k in range(strips):
        edge = (partner(k) + 1) * rows_dev

        @pl.when((before < edge) & (edge <= final))
        def _():
            for copy in sci_copies(k):
                copy.start()

    @pl.when(step == last)
    def _():
        whalf = wt_s.shape[0] // 2
        copies = []
        for part, order in enumerate(orders):
            for slots, out in zip(slot_order(epochs, order), outs[part]):
                for place in range(len(slots)):
                    copies.append(
                        pltpu.make_async_copy(
                            wt_s.at[pl.ds(part * whalf, whalf)],
                            out.at[place, pl.ds(nhalf, whalf)],
                            wt_sems.at[len(copies)],
                        )
                    )
        start_and_wait(copies)
        for s in range(strips):
            for copy in strip_copies(s) + sci_copies(s):
                copy.wait()
        for k in range(kinds):

            @pl.when(ready_s[k] == 0)
            def _():
                for copy in fetches(k):
                    copy.wait()


def template_kernel(terms, *refs):
    term_refs, out_refs, pad_s = refs[: 2 * terms], refs[2 * terms : -1], refs[-1]
    strips = len(out_refs)
    long, share = out_refs[0].shape
    rows_dev = long - 2 * HALO
    nrow = strips * rows_dev
    nhalf = nrow // 2
    whalf = nhalf // share
    edge = jnp.zeros((HALO, share), F32)
    pad_s[pl.ds(0, HALO), :] = edge
    pad_s[pl.ds(HALO + nrow, HALO), :] = edge
    for part in range(2):
        own = term_refs[part * terms : (part + 1) * terms]
        add = lambda place: functools.reduce(lambda a, b: a + b, [ref[0, place, :] for ref in own])
        weights = add(pl.ds(nhalf, whalf))
        for i in range(whalf):
            below = jnp.transpose(jnp.broadcast_to(weights[i : i + 1, :], (share, share)))
            pad_s[pl.ds(HALO + part * nhalf + i * share, share), :] = add(pl.ds(i * share, share)) / below
    for k in range(strips):
        strip = jnp.bitwise_xor(lax.axis_index("strip"), k)
        out_refs[k][...] = pad_s[pl.ds(pl.multiple_of(strip * rows_dev, rows_dev), long), :]


def bands_kernel(psf_ref, toep_hi, toep_lo, band_ref):
    basis, _, ksize = psf_ref.shape
    margin = ksize // 2
    for k in range(basis):
        shape = (2 * LANES, LANES)
        tap = lax.broadcasted_iota(jnp.int32, shape, 0) - lax.broadcasted_iota(jnp.int32, shape, 1)
        tap = tap - (LANES // 2 - margin)
        value = jnp.zeros(shape, F32)
        for j in range(ksize):
            value = jnp.where(tap == j, psf_ref[k, 1, j], value)
        toep_hi[:, pl.ds(k * LANES, LANES)], toep_lo[:, pl.ds(k * LANES, LANES)] = split(value)
        shape = (LANES, LANES + 2 * HALO)
        tap = lax.broadcasted_iota(jnp.int32, shape, 1) - lax.broadcasted_iota(jnp.int32, shape, 0)
        tap = tap - (HALO - margin)
        value = jnp.zeros(shape, F32)
        for j in range(ksize):
            value = jnp.where(tap == j, psf_ref[k, 0, j], value)
        band_ref[k, pl.ds(0, LANES), :], band_ref[k, pl.ds(LANES, LANES), :] = split(value)


def match_kernel(geom, *refs):
    slots, nrow, ncol = geom
    count = max(len(slots), 1) + (len(slots) > 1)
    tile_refs = refs[:count]
    poly_ref, toep_hi, toep_lo, band_ref, *sci_refs, out_ref, pad_s, row_s = refs[count:]
    step = pl.program_id(0)
    blocks = pl.num_programs(0)
    tiles = pad_s.shape[0] - 2
    rows_dev = pad_s.shape[1] - 2 * HALO
    me = lax.axis_index("epoch")
    strip = lax.axis_index("strip")
    per_step = out_ref.shape[1] // LANES

    def bring(b):
        if not slots:
            for i in range(per_step):
                place = b * per_step + i
                pad_s[1 + place] = tile_refs[0][place]
            return
        at = jnp.bitwise_xor(strip, b)
        for n, slot in enumerate(slots[:-1]):
            pad_s[1 + b * per_step + jnp.bitwise_xor(me, slot)] = tile_refs[n][at]
        place = 1 + b * per_step + jnp.bitwise_xor(me, slots[-1])
        cut = tile_refs[-1].shape[0]

        @pl.when(at < cut)
        def _():
            pad_s[place] = tile_refs[-2][at]

        @pl.when(at >= cut)
        def _():
            pad_s[place] = tile_refs[-1][at - cut]

    @pl.when(step == 0)
    def _():
        bring(0)
        pad_s[0] = jnp.zeros(pad_s.shape[1:], F32)
        pad_s[tiles + 1] = jnp.zeros(pad_s.shape[1:], F32)
        shape = (rows_dev, LANES)
        counter = (strip * rows_dev + lax.broadcasted_iota(jnp.int32, shape, 0)).astype(F32)
        u = (2.0 * counter + 1.0) / nrow - 1.0
        for k in range(2):
            p = [poly_ref[me, k, i] for i in range(6)]
            row_s[k, 0] = p[0] + u * (p[1] + p[3] * u)
            row_s[k, 1] = p[2] + p[4] * u

    @pl.when(step < blocks - 1)
    def _():
        bring(step + 1)

    lane = lax.broadcasted_iota(jnp.int32, pad_s.shape[1:], 1)
    base = step * per_step
    shifted = []
    for m in range(per_step + 1):
        mixed = jnp.where(lane < LANES // 2, pad_s[base + m + 1], pad_s[base + m])
        shifted.append(split(pltpu.roll(mixed, LANES // 2, 1)))
    toep = (toep_hi[...], toep_lo[...])
    for pair in range(per_step // 2):
        across = []
        for c in (2 * pair, 2 * pair + 1):
            window = tuple(
                jnp.concatenate([shifted[c][i], shifted[c + 1][i]], axis=1) for i in range(2)
            )
            across.append(dot3(window, toep))
        width = 2 * LANES
        cols = lax.broadcasted_iota(jnp.int32, (1, width), 1) + (base + 2 * pair) * LANES
        v = (2.0 * cols.astype(F32) + 1.0) / ncol - 1.0
        for part in range(rows_dev // LANES):
            total = 0.0
            for k in range(2):
                both = jnp.concatenate(
                    [a[part * LANES : part * LANES + LANES + 2 * HALO, k * LANES : (k + 1) * LANES] for a in across],
                    axis=1,
                )
                hi, lo = split(both)
                wide = dot(band_ref[k], hi)
                done = wide[:LANES] + (wide[LANES:] + dot(band_ref[k, pl.ds(0, LANES), :], lo))
                place = pl.ds(part * LANES, LANES)
                one = jnp.concatenate([row_s[k, 0, place, :]] * 2, axis=1)
                two = jnp.concatenate([row_s[k, 1, place, :]] * 2, axis=1)
                coeff = one + v * (two + poly_ref[me, k, 5] * v)
                total = total + coeff * done
            out_ref[pl.ds(part * LANES, LANES), pl.ds(pair * width, width)] = total

    home = lax.div(strip, lax.axis_size("strip") // blocks)
    for k, ref in enumerate(sci_refs):

        @pl.when(jnp.bitwise_xor(home, step) == k)
        def _():
            ready = pl.ds(0, ref.shape[0])
            out_ref[ready, :] = ref[...] - out_ref[ready, :]


def subtract_kernel(*refs):
    *sci_refs, matched_ref, out_ref = refs
    i = pl.program_id(0)
    rows, width = out_ref.shape[1], sci_refs[0].shape[1]
    home = lax.div(lax.axis_index("strip"), lax.axis_size("strip") // len(sci_refs))
    for k, ref in enumerate(sci_refs):
        columns = pl.ds(pl.multiple_of(jnp.bitwise_xor(home, k) * width, width), width)
        science = ref[pl.ds(pl.multiple_of(i * rows, rows), rows), :]
        out_ref[0, :, columns] = science - matched_ref[0, :, columns]


def swap(value, axis, bit):
    count = lax.axis_size(axis)
    return lax.ppermute(value, axis, [(i, i ^ (1 << bit)) for i in range(count)])


def shards(
    raw_tiles, tile_kind, tile_invvar, tile_heights, row_interp, col_interp, psf_profiles, psf_poly
):
    strips, epochs = lax.axis_size("strip"), lax.axis_size("epoch")
    _, tiles, tile_rows, tile_cols = raw_tiles.shape
    _, blocks, _ = tile_heights.shape
    ncol, nrow = blocks * tile_cols, ROWS_DEV * strips
    sources = strips // blocks
    share = tile_cols // epochs
    bits = epochs.bit_length() - 1
    orders = (tuple(range(bits)), tuple(reversed(range(bits))))
    nhalf = nrow // 2
    wrows = nrow // share
    long_half = nhalf + wrows // 2
    smem = pl.BlockSpec(memory_space=pltpu.SMEM)
    hbm = pl.BlockSpec(memory_space=pl.ANY)
    vmem = pl.BlockSpec(memory_space=pltpu.VMEM)
    kinds = col_interp.shape[0]

    first_rows = ROWS_DEV * FIRST_PART // 8
    sci_shapes = [
        jax.ShapeDtypeStruct((rows, tile_cols), F32) for rows in (first_rows, ROWS_DEV - first_rows)
    ]
    send_shape = jax.ShapeDtypeStruct((epochs // 2, long_half, share), F32)
    together = 2 if tiles % 2 == 0 else 1
    warped = pl.pallas_call(
        functools.partial(warp_kernel, (epochs, nrow, share, orders, tiles)),
        grid=(tiles // together,),
        in_specs=[
            smem,
            smem,
            smem,
            pl.BlockSpec((together, tile_rows, tile_cols), lambda t: (t, 0, 0)),
            hbm,
            hbm,
        ],
        out_specs=[hbm] * (2 * strips + 4),
        out_shape=[sci_shapes[0]] * strips + [sci_shapes[1]] * strips + [send_shape] * 4,
        scratch_shapes=[
            pltpu.VMEM((nrow, tile_cols), F32),
            pltpu.VMEM((epochs, nrow, share), F32),
            pltpu.VMEM((wrows, share), F32),
            pltpu.VMEM((kinds, tile_rows, tile_rows), F32),
            pltpu.VMEM((kinds, tile_cols, tile_cols), F32),
            pltpu.VMEM((kinds, tile_cols, tile_cols), BF16),
            pltpu.VMEM((kinds, tile_cols, tile_cols), BF16),
            pltpu.SMEM((2,), jnp.int32),
            pltpu.SMEM((kinds,), jnp.int32),
            pltpu.SemaphoreType.DMA((kinds, 2)),
            pltpu.SemaphoreType.DMA((strips, epochs)),
            pltpu.SemaphoreType.DMA((strips, 2)),
            pltpu.SemaphoreType.DMA((2 * epochs,)),
        ],
        name="warp",
        cost_estimate=pl.CostEstimate(flops=8_000_000_000, bytes_accessed=20_000_000, transcendentals=0),
    )(tile_kind, tile_heights, tile_invvar, raw_tiles[0], row_interp, col_interp)

    sci_a, sci_b = warped[:strips], warped[strips : 2 * strips]
    keep_a, send_a, keep_b, send_b = warped[2 * strips :]

    def exchanged(arrays):
        got = [arrays[0]] + [None] * (strips - 1)
        for k in reversed(range(1, strips)):
            got[k] = lax.ppermute(arrays[k], "strip", [(i, i ^ k) for i in range(strips)])
        return got

    def merged(got):
        return [
            functools.reduce(lambda a, b: a + b, got[k : k + sources]) for k in range(0, strips, sources)
        ]

    got_a = exchanged(sci_a)

    basis, _, _ = psf_profiles.shape
    build_bands = pl.pallas_call(
        bands_kernel,
        in_specs=[smem],
        out_specs=[vmem] * 3,
        out_shape=[
            jax.ShapeDtypeStruct((2 * LANES, 2 * LANES), BF16),
            jax.ShapeDtypeStruct((2 * LANES, 2 * LANES), BF16),
            jax.ShapeDtypeStruct((basis, 2 * LANES, LANES + 2 * HALO), BF16),
        ],
        name="bands",
        cost_estimate=pl.CostEstimate(flops=10_000_000, bytes_accessed=500_000, transcendentals=0),
    )
    toep_hi, toep_lo, band = build_bands(psf_profiles)

    terms = [[keep_a], [keep_b]]
    sends = [send_a, send_b]
    for i in range(bits):
        for part in range(2):
            terms[part].append(swap(sends[part], "epoch", orders[part][i]))
        left = epochs >> (i + 1)
        if left > 1:
            sends = [
                functools.reduce(lambda a, b: a + b, [t[left // 2 : left] for t in own]) for own in terms
            ]
    if sources > 1:
        fixed = []
        for own in terms:
            total = functools.reduce(lambda a, b: a + b, [t[:1] for t in own])
            around = total
            for k in range(1, sources):
                ring = [(i, i // sources * sources + (i + k) % sources) for i in range(strips)]
                around = around + lax.ppermute(total, "strip", ring)
            fixed.append([around])
        terms = fixed

    long = ROWS_DEV + 2 * HALO
    build_strips = pl.pallas_call(
        functools.partial(template_kernel, len(terms[0])),
        in_specs=[vmem] * (2 * len(terms[0])),
        out_specs=[vmem] * strips,
        out_shape=[jax.ShapeDtypeStruct((long, share), F32)] * strips,
        scratch_shapes=[pltpu.VMEM((nrow + 2 * HALO, share), F32)],
        name="template",
        cost_estimate=pl.CostEstimate(flops=2_000_000, bytes_accessed=5_000_000, transcendentals=0),
    )
    parts = build_strips(*terms[0], *terms[1])
    came = exchanged(parts)
    mine = jnp.stack(came[:: sources])
    mine, *sci_b = lax.optimization_barrier((mine, *sci_b))
    got_b = merged(exchanged(sci_b))
    got_a = merged(got_a)

    per_block = tile_cols // LANES
    if epochs == 4 and share == LANES:
        near = []
        for b in range(2):
            near.append(swap(mine, "epoch", b))
        cut = blocks // 2
        far_low = swap(near[1][:cut], "epoch", 0)
        far_high = swap(near[0][cut:], "epoch", 1)
        arrays = [mine, near[0], near[1], far_low, far_high]
        held = (0, 1, 2, 3)
    else:
        slots = [mine]
        for b in range(bits):
            slots = slots + [swap(s, "epoch", b) for s in slots]
        me = lax.axis_index("epoch")
        every = jnp.take(jnp.stack(slots), jnp.bitwise_xor(jnp.arange(epochs), me), axis=0)
        home = lax.axis_index("strip") // sources
        every = jnp.take(every, jnp.bitwise_xor(jnp.arange(blocks), home), axis=1)
        flat = jnp.transpose(every, (1, 2, 0, 3)).reshape(blocks, long, per_block, LANES)
        arrays = [jnp.transpose(flat, (0, 2, 1, 3)).reshape(blocks * per_block, long, LANES)]
        held = ()

    const = lambda b: (0, 0)
    convolve = pl.pallas_call(
        functools.partial(match_kernel, (held, nrow, ncol)),
        grid=(blocks,),
        in_specs=[vmem] * len(arrays)
        + [
            smem,
            pl.BlockSpec(toep_hi.shape, const),
            pl.BlockSpec(toep_lo.shape, const),
            pl.BlockSpec(band.shape, lambda b: (0, 0, 0)),
        ]
        + [vmem] * blocks,
        out_specs=pl.BlockSpec((ROWS_DEV, tile_cols), lambda b: (0, b)),
        out_shape=jax.ShapeDtypeStruct((ROWS_DEV, ncol), F32),
        scratch_shapes=[
            pltpu.VMEM((blocks * per_block + 2, long, LANES), F32),
            pltpu.VMEM((2, 2, ROWS_DEV, LANES), F32),
        ],
        name="convolve",
        compiler_params=pltpu.CompilerParams(vmem_limit_bytes=28 << 20),
        cost_estimate=pl.CostEstimate(flops=15_000_000_000, bytes_accessed=10_000_000, transcendentals=0),
    )
    arrays = [pltpu.with_memory_space_constraint(x, pltpu.VMEM) for x in arrays]
    matched = convolve(*arrays, psf_poly, toep_hi, toep_lo, band, *got_a)
    unit = ROWS_DEV // 8
    rest = pl.BlockSpec((1, unit, ncol), lambda i: (0, FIRST_PART + i, 0))
    return pl.pallas_call(
        subtract_kernel,
        grid=(8 - FIRST_PART,),
        in_specs=[vmem] * blocks + [rest],
        out_specs=rest,
        out_shape=jax.ShapeDtypeStruct((1, ROWS_DEV, ncol), F32),
        input_output_aliases={blocks: 0},
        name="subtract",
        compiler_params=pltpu.CompilerParams(vmem_limit_bytes=16 << 20),
        cost_estimate=pl.CostEstimate(flops=1_000_000, bytes_accessed=6_000_000, transcendentals=0),
    )(*[pltpu.with_memory_space_constraint(x, pltpu.VMEM) for x in got_b], matched[None])


def solution(mesh):
    in_specs = (
        P("epoch", "strip", None, None),
        P("epoch", "strip"),
        P("epoch", "strip"),
        P("epoch", None, None),
        P(),
        P(),
        P(),
        P(),
    )
    out_specs = P("epoch", "strip", None)

    return jax.shard_map(shards, mesh=mesh, in_specs=in_specs, out_specs=out_specs, check_vma=False)
```

```python
import functools

import jax
import jax.numpy as jnp
from jax import lax
from jax.experimental import pallas as pl
from jax.experimental.pallas import tpu as pltpu
from jax.sharding import PartitionSpec as P


ROWS_DEV = 256
HALO = 16
FIRST_PART = 3
LANES = 128
F32 = jnp.float32
BF16 = jnp.bfloat16


def split(x):
    hi = x.astype(BF16)
    lo = (x - hi.astype(F32)).astype(BF16)
    return hi, lo


def dot(a, b, trans_b=False):
    dims = (((1,), (1 if trans_b else 0,)), ((), ()))
    return lax.dot_general(a, b, dims, preferred_element_type=F32)


def dot3(a, b, trans_b=False):
    a_hi, a_lo = a
    b_hi, b_lo = b
    both = dot(jnp.concatenate([a_hi, a_lo], axis=0), b_hi, trans_b)
    rows = a_hi.shape[0]
    return both[:rows] + (both[rows:] + dot(a_hi, b_lo, trans_b))


def start_and_wait(copies):
    for copy in copies:
        copy.start()
    for copy in copies:
        copy.wait()


def slot_order(count, order):
    bits = len(order)
    key = lambda j: sum(((j >> order[i]) & 1) << (bits - 1 - i) for i in range(bits))
    slots = sorted(range(count), key=key)
    return slots[: count // 2], slots[count // 2 :]


def warp_kernel(
    geom, kind_ref, heights_ref, invvar_ref, raw_ref, rmat_ref, cmat_ref,
    sci_a, sci_b, keep_a, send_a, keep_b, send_b,
    sci_s, num_s, wt_s, rmat_s, cmat_s, chi_s, clo_s, top_s, ready_s, fetch_sems, sems, wt_sems,
):
    epochs, nrow, share, orders, tiles = geom
    step = pl.program_id(0)
    together, tile_rows, tile_cols = raw_ref.shape
    last = pl.num_programs(0) - 1
    per_col = heights_ref.shape[2]
    span = tile_rows + 8
    me = lax.axis_index("epoch")
    first_tile = lax.axis_index("strip") * tiles
    block = lax.div(first_tile, per_col)
    offset_in = lax.rem(first_tile, per_col)
    kinds = cmat_ref.shape[0]
    strips, rows_a, _ = sci_a.shape
    rows_dev = rows_a + sci_b.shape[1]
    nhalf = nrow // 2
    outs = (keep_a, send_a), (keep_b, send_b)

    def fetches(k):
        return [
            pltpu.make_async_copy(cmat_ref.at[k], cmat_s.at[k], fetch_sems.at[k, 0]),
            pltpu.make_async_copy(rmat_ref.at[k], rmat_s.at[k], fetch_sems.at[k, 1]),
        ]

    def strip_copies(s):
        base = s * rows_dev
        part = base // nhalf
        pairs = [
            (sci_s.at[pl.ds(base, rows_a)], sci_a.at[s]),
            (sci_s.at[pl.ds(base + rows_a, rows_dev - rows_a)], sci_b.at[s]),
        ]
        for slots, out in zip(slot_order(epochs, orders[part]), outs[part]):
            for place, j in enumerate(slots):
                pairs.append(
                    (num_s.at[j, pl.ds(base, rows_dev)], out.at[place, pl.ds(base - part * nhalf, rows_dev)])
                )
        return [pltpu.make_async_copy(a, b, sems.at[s, n]) for n, (a, b) in enumerate(pairs)]

    @pl.when(step == 0)
    def _():
        top_s[0] = lax.fori_loop(
            0, offset_in, lambda i, total: total + heights_ref[0, block, i], jnp.int32(0)
        )
        top_s[1] = 0
        first = kind_ref[0, 0]
        for i in range(kinds):
            ready_s[i] = 0
            for copy in fetches(lax.rem(first + i, kinds)):
                copy.start()
        if tiles != per_col:
            sci_s[...] = jnp.zeros_like(sci_s)
            num_s[...] = jnp.zeros_like(num_s)
            wt_s[...] = jnp.zeros_like(wt_s)

    def warped(i, top):
        t = step * together + i
        kind = kind_ref[0, t]
        height = heights_ref[0, block, offset_in + t]
        start = pl.multiple_of(jnp.minimum(lax.div(top, 8) * 8, nrow - span), 8)
        off = top - start
        across = dot3(split(raw_ref[i]), (chi_s[kind], clo_s[kind]), trans_b=True)
        live = lax.broadcasted_iota(jnp.int32, (tile_rows, tile_rows), 1) < height
        rows = jnp.concatenate(
            [jnp.where(live, rmat_s[kind], 0.0), jnp.zeros((8, tile_rows), F32)], axis=0
        )
        return t, height, start, off, dot3(split(pltpu.roll(rows, off, 0)), split(across))

    for i in range(together):
        kind = kind_ref[0, step * together + i]

        @pl.when(ready_s[kind] == 0)
        def _():
            for copy in fetches(kind):
                copy.wait()
            ready_s[kind] = 1

            def divide(n, carry):
                here = pl.ds(pl.multiple_of(n * (tile_cols // 8), tile_cols // 8), tile_cols // 8)
                chi_s[kind, here, :], clo_s[kind, here, :] = split(cmat_s[kind, here, :])
                return carry

            lax.fori_loop(0, 8, divide, 0)

    top = top_s[0]
    results = []
    for i in range(together):
        results.append((top, warped(i, top)))
        top = top + results[-1][1][1]
    top_s[0] = top
    after = top

    for top, (t, height, start, off, placed) in results:
        weight = invvar_ref[0, t]
        local = lax.broadcasted_iota(jnp.int32, (span, share), 0) - off
        own = (local >= 0) & (local < height)
        here = pl.ds(start, span)
        for q in range(epochs):
            columns = pl.ds(q * share, share)
            piece = placed[:, q * share : (q + 1) * share]
            slot = jnp.bitwise_xor(me, q)
            sci_s[here, columns] = jnp.where(own, piece, sci_s[here, columns])
            num_s[slot, here, :] = jnp.where(own, weight * piece, num_s[slot, here, :])
        flat = lax.broadcasted_iota(jnp.int32, wt_s.shape, 0) * share + lax.broadcasted_iota(
            jnp.int32, wt_s.shape, 1
        )
        wt_s[...] = jnp.where((flat >= top) & (flat < top + height), weight, wt_s[...])

    before = top_s[1]
    final = jnp.where(step == last, nrow, jnp.minimum(lax.div(after, 8) * 8, nrow - span))
    top_s[1] = final
    for s in range(strips):
        end = (s + 1) * rows_dev

        @pl.when((before < end) & (end <= final))
        def _():
            for copy in strip_copies(s):
                copy.start()

    @pl.when(step == last)
    def _():
        whalf = wt_s.shape[0] // 2
        copies = []
        for part, order in enumerate(orders):
            for slots, out in zip(slot_order(epochs, order), outs[part]):
                for place in range(len(slots)):
                    copies.append(
                        pltpu.make_async_copy(
                            wt_s.at[pl.ds(part * whalf, whalf)],
                            out.at[place, pl.ds(nhalf, whalf)],
                            wt_sems.at[len(copies)],
                        )
                    )
        start_and_wait(copies)
        for s in range(strips):
            for copy in strip_copies(s):
                copy.wait()
        for k in range(kinds):

            @pl.when(ready_s[k] == 0)
            def _():
                for copy in fetches(k):
                    copy.wait()


def template_kernel(terms, *refs):
    term_refs, out_refs, pad_s = refs[: 2 * terms], refs[2 * terms : -1], refs[-1]
    strips = len(out_refs)
    long, share = out_refs[0].shape
    rows_dev = long - 2 * HALO
    nrow = strips * rows_dev
    nhalf = nrow // 2
    whalf = nhalf // share
    edge = jnp.zeros((HALO, share), F32)
    pad_s[pl.ds(0, HALO), :] = edge
    pad_s[pl.ds(HALO + nrow, HALO), :] = edge
    for part in range(2):
        own = term_refs[part * terms : (part + 1) * terms]
        add = lambda place: functools.reduce(lambda a, b: a + b, [ref[0, place, :] for ref in own])
        weights = add(pl.ds(nhalf, whalf))
        for i in range(whalf):
            below = jnp.transpose(jnp.broadcast_to(weights[i : i + 1, :], (share, share)))
            pad_s[pl.ds(HALO + part * nhalf + i * share, share), :] = add(pl.ds(i * share, share)) / below
    for k in range(strips):
        strip = jnp.bitwise_xor(lax.axis_index("strip"), k)
        out_refs[k][...] = pad_s[pl.ds(pl.multiple_of(strip * rows_dev, rows_dev), long), :]


def bands_kernel(psf_ref, toep_hi, toep_lo, band_ref):
    basis, _, ksize = psf_ref.shape
    margin = ksize // 2
    for k in range(basis):
        shape = (2 * LANES, LANES)
        tap = lax.broadcasted_iota(jnp.int32, shape, 0) - lax.broadcasted_iota(jnp.int32, shape, 1)
        tap = tap - (LANES // 2 - margin)
        value = jnp.zeros(shape, F32)
        for j in range(ksize):
            value = jnp.where(tap == j, psf_ref[k, 1, j], value)
        toep_hi[:, pl.ds(k * LANES, LANES)], toep_lo[:, pl.ds(k * LANES, LANES)] = split(value)
        shape = (LANES, LANES + 2 * HALO)
        tap = lax.broadcasted_iota(jnp.int32, shape, 1) - lax.broadcasted_iota(jnp.int32, shape, 0)
        tap = tap - (HALO - margin)
        value = jnp.zeros(shape, F32)
        for j in range(ksize):
            value = jnp.where(tap == j, psf_ref[k, 0, j], value)
        band_ref[k, pl.ds(0, LANES), :], band_ref[k, pl.ds(LANES, LANES), :] = split(value)


def match_kernel(geom, *refs):
    slots, nrow, ncol = geom
    count = max(len(slots), 1) + (len(slots) > 1)
    tile_refs = refs[:count]
    poly_ref, toep_hi, toep_lo, band_ref, sci_ref, out_ref, pad_s, row_s = refs[count:]
    step = pl.program_id(0)
    blocks = pl.num_programs(0)
    tiles = pad_s.shape[0] - 2
    rows_dev = pad_s.shape[1] - 2 * HALO
    me = lax.axis_index("epoch")
    strip = lax.axis_index("strip")
    per_step = out_ref.shape[1] // LANES

    def bring(b):
        if not slots:
            for i in range(per_step):
                place = b * per_step + i
                pad_s[1 + place] = tile_refs[0][place]
            return
        at = jnp.bitwise_xor(strip, b)
        for n, slot in enumerate(slots[:-1]):
            pad_s[1 + b * per_step + jnp.bitwise_xor(me, slot)] = tile_refs[n][at]
        place = 1 + b * per_step + jnp.bitwise_xor(me, slots[-1])
        cut = tile_refs[-1].shape[0]

        @pl.when(at < cut)
        def _():
            pad_s[place] = tile_refs[-2][at]

        @pl.when(at >= cut)
        def _():
            pad_s[place] = tile_refs[-1][at - cut]

    @pl.when(step == 0)
    def _():
        bring(0)
        pad_s[0] = jnp.zeros(pad_s.shape[1:], F32)
        pad_s[tiles + 1] = jnp.zeros(pad_s.shape[1:], F32)
        shape = (rows_dev, LANES)
        counter = (strip * rows_dev + lax.broadcasted_iota(jnp.int32, shape, 0)).astype(F32)
        u = (2.0 * counter + 1.0) / nrow - 1.0
        for k in range(2):
            p = [poly_ref[me, k, i] for i in range(6)]
            row_s[k, 0] = p[0] + u * (p[1] + p[3] * u)
            row_s[k, 1] = p[2] + p[4] * u

    @pl.when(step < blocks - 1)
    def _():
        bring(step + 1)

    lane = lax.broadcasted_iota(jnp.int32, pad_s.shape[1:], 1)
    base = step * per_step
    shifted = []
    for m in range(per_step + 1):
        mixed = jnp.where(lane < LANES // 2, pad_s[base + m + 1], pad_s[base + m])
        shifted.append(split(pltpu.roll(mixed, LANES // 2, 1)))
    toep = (toep_hi[...], toep_lo[...])
    for pair in range(per_step // 2):
        across = []
        for c in (2 * pair, 2 * pair + 1):
            window = tuple(
                jnp.concatenate([shifted[c][i], shifted[c + 1][i]], axis=1) for i in range(2)
            )
            across.append(dot3(window, toep))
        width = 2 * LANES
        cols = lax.broadcasted_iota(jnp.int32, (1, width), 1) + (base + 2 * pair) * LANES
        v = (2.0 * cols.astype(F32) + 1.0) / ncol - 1.0
        for part in range(rows_dev // LANES):
            total = 0.0
            for k in range(2):
                both = jnp.concatenate(
                    [a[part * LANES : part * LANES + LANES + 2 * HALO, k * LANES : (k + 1) * LANES] for a in across],
                    axis=1,
                )
                hi, lo = split(both)
                wide = dot(band_ref[k], hi)
                done = wide[:LANES] + (wide[LANES:] + dot(band_ref[k, pl.ds(0, LANES), :], lo))
                place = pl.ds(part * LANES, LANES)
                one = jnp.concatenate([row_s[k, 0, place, :]] * 2, axis=1)
                two = jnp.concatenate([row_s[k, 1, place, :]] * 2, axis=1)
                coeff = one + v * (two + poly_ref[me, k, 5] * v)
                total = total + coeff * done
            columns = pl.ds(pair * width, width)
            ready = min(max(sci_ref.shape[1] - part * LANES, 0), LANES)
            if ready:
                here = pl.ds(part * LANES, ready)
                out_ref[here, columns] = sci_ref[0, here, columns] - total[:ready]
            if ready < LANES:
                out_ref[pl.ds(part * LANES + ready, LANES - ready), columns] = total[ready:]


def subtract_kernel(sci_ref, matched_ref, out_ref):
    i = pl.program_id(0)
    blocks, _, width = sci_ref.shape
    rows = out_ref.shape[1]
    for b in range(blocks):
        columns = pl.ds(b * width, width)
        science = sci_ref[b, pl.ds(pl.multiple_of(i * rows, rows), rows), :]
        out_ref[0, :, columns] = science - matched_ref[0, :, columns]


def swap(value, axis, bit):
    count = lax.axis_size(axis)
    return lax.ppermute(value, axis, [(i, i ^ (1 << bit)) for i in range(count)])


def shards(
    raw_tiles, tile_kind, tile_invvar, tile_heights, row_interp, col_interp, psf_profiles, psf_poly
):
    strips, epochs = lax.axis_size("strip"), lax.axis_size("epoch")
    _, tiles, tile_rows, tile_cols = raw_tiles.shape
    _, blocks, _ = tile_heights.shape
    ncol, nrow = blocks * tile_cols, ROWS_DEV * strips
    sources = strips // blocks
    share = tile_cols // epochs
    bits = epochs.bit_length() - 1
    orders = (tuple(range(bits)), tuple(reversed(range(bits))))
    nhalf = nrow // 2
    wrows = nrow // share
    long_half = nhalf + wrows // 2
    smem = pl.BlockSpec(memory_space=pltpu.SMEM)
    hbm = pl.BlockSpec(memory_space=pl.ANY)
    vmem = pl.BlockSpec(memory_space=pltpu.VMEM)
    kinds = col_interp.shape[0]

    first_rows = ROWS_DEV * FIRST_PART // 8
    sci_shapes = [
        jax.ShapeDtypeStruct((strips, rows, tile_cols), F32) for rows in (first_rows, ROWS_DEV - first_rows)
    ]
    send_shape = jax.ShapeDtypeStruct((epochs // 2, long_half, share), F32)
    together = 2 if tiles % 2 == 0 else 1
    sci_a, sci_b, keep_a, send_a, keep_b, send_b = pl.pallas_call(
        functools.partial(warp_kernel, (epochs, nrow, share, orders, tiles)),
        grid=(tiles // together,),
        in_specs=[
            smem,
            smem,
            smem,
            pl.BlockSpec((together, tile_rows, tile_cols), lambda t: (t, 0, 0)),
            hbm,
            hbm,
        ],
        out_specs=[hbm] * 6,
        out_shape=sci_shapes + [send_shape] * 4,
        scratch_shapes=[
            pltpu.VMEM((nrow, tile_cols), F32),
            pltpu.VMEM((epochs, nrow, share), F32),
            pltpu.VMEM((wrows, share), F32),
            pltpu.VMEM((kinds, tile_rows, tile_rows), F32),
            pltpu.VMEM((kinds, tile_cols, tile_cols), F32),
            pltpu.VMEM((kinds, tile_cols, tile_cols), BF16),
            pltpu.VMEM((kinds, tile_cols, tile_cols), BF16),
            pltpu.SMEM((2,), jnp.int32),
            pltpu.SMEM((kinds,), jnp.int32),
            pltpu.SemaphoreType.DMA((kinds, 2)),
            pltpu.SemaphoreType.DMA((strips, 2 + epochs)),
            pltpu.SemaphoreType.DMA((2 * epochs,)),
        ],
        name="warp",
        cost_estimate=pl.CostEstimate(flops=8_000_000_000, bytes_accessed=20_000_000, transcendentals=0),
    )(tile_kind, tile_heights, tile_invvar, raw_tiles[0], row_interp, col_interp)

    got_a = lax.all_to_all(sci_a, "strip", split_axis=0, concat_axis=0, tiled=True)

    basis, _, _ = psf_profiles.shape
    build_bands = pl.pallas_call(
        bands_kernel,
        in_specs=[smem],
        out_specs=[vmem] * 3,
        out_shape=[
            jax.ShapeDtypeStruct((2 * LANES, 2 * LANES), BF16),
            jax.ShapeDtypeStruct((2 * LANES, 2 * LANES), BF16),
            jax.ShapeDtypeStruct((basis, 2 * LANES, LANES + 2 * HALO), BF16),
        ],
        name="bands",
        cost_estimate=pl.CostEstimate(flops=10_000_000, bytes_accessed=500_000, transcendentals=0),
    )
    toep_hi, toep_lo, band = build_bands(psf_profiles)

    terms = [[keep_a], [keep_b]]
    sends = [send_a, send_b]
    for i in range(bits):
        for part in range(2):
            terms[part].append(swap(sends[part], "epoch", orders[part][i]))
        left = epochs >> (i + 1)
        if left > 1:
            sends = [
                functools.reduce(lambda a, b: a + b, [t[left // 2 : left] for t in own]) for own in terms
            ]
    if sources > 1:
        fixed = []
        for own in terms:
            total = functools.reduce(lambda a, b: a + b, [t[:1] for t in own])
            around = total
            for k in range(1, sources):
                ring = [(i, i // sources * sources + (i + k) % sources) for i in range(strips)]
                around = around + lax.ppermute(total, "strip", ring)
            fixed.append([around])
        terms = fixed

    long = ROWS_DEV + 2 * HALO
    first_slot = pl.BlockSpec((1, long_half, share), lambda i: (0, 0, 0))
    kinds_of_term = [first_slot] * (len(terms[0]) - 1) + [vmem]
    for own in terms:
        own[-1] = pltpu.with_memory_space_constraint(own[-1], pltpu.VMEM)
    parts = pl.pallas_call(
        functools.partial(template_kernel, len(terms[0])),
        grid=(1,),
        in_specs=kinds_of_term * 2,
        out_specs=[pl.BlockSpec((long, share), lambda i: (0, 0))] * strips,
        out_shape=[jax.ShapeDtypeStruct((long, share), F32)] * strips,
        scratch_shapes=[pltpu.VMEM((nrow + 2 * HALO, share), F32)],
        name="template",
        cost_estimate=pl.CostEstimate(flops=2_000_000, bytes_accessed=5_000_000, transcendentals=0),
    )(*terms[0], *terms[1])
    came = [None] * strips
    came[0] = parts[0]
    for k in reversed(range(1, strips)):
        came[k] = lax.ppermute(parts[k], "strip", [(i, i ^ k) for i in range(strips)])
    came[strips // 2], got_a = lax.optimization_barrier((came[strips // 2], got_a))
    mine = jnp.stack(came[:: sources])
    sci_b, mine = lax.optimization_barrier((sci_b, mine))
    got_b = lax.all_to_all(sci_b, "strip", split_axis=0, concat_axis=0, tiled=True)
    if sources > 1:
        got_a = jnp.sum(got_a.reshape((blocks, sources) + got_a.shape[1:]), axis=1)
        got_b = jnp.sum(got_b.reshape((blocks, sources) + got_b.shape[1:]), axis=1)

    per_block = tile_cols // LANES
    if epochs == 4 and share == LANES:
        near = []
        for b in range(2):
            near.append(swap(mine, "epoch", b))
        cut = blocks // 2
        far_low = swap(near[1][:cut], "epoch", 0)
        far_high = swap(near[0][cut:], "epoch", 1)
        arrays = [mine, near[0], near[1], far_low, far_high]
        held = (0, 1, 2, 3)
    else:
        slots = [mine]
        for b in range(bits):
            slots = slots + [swap(s, "epoch", b) for s in slots]
        me = lax.axis_index("epoch")
        every = jnp.take(jnp.stack(slots), jnp.bitwise_xor(jnp.arange(epochs), me), axis=0)
        home = lax.axis_index("strip") // sources
        every = jnp.take(every, jnp.bitwise_xor(jnp.arange(blocks), home), axis=1)
        flat = jnp.transpose(every, (1, 2, 0, 3)).reshape(blocks, long, per_block, LANES)
        arrays = [jnp.transpose(flat, (0, 2, 1, 3)).reshape(blocks * per_block, long, LANES)]
        held = ()

    const = lambda b: (0, 0)
    convolve = pl.pallas_call(
        functools.partial(match_kernel, (held, nrow, ncol)),
        grid=(blocks,),
        in_specs=[vmem] * len(arrays)
        + [
            smem,
            pl.BlockSpec(toep_hi.shape, const),
            pl.BlockSpec(toep_lo.shape, const),
            pl.BlockSpec(band.shape, lambda b: (0, 0, 0)),
            pl.BlockSpec((1,) + got_a.shape[1:], lambda b: (b, 0, 0)),
        ],
        out_specs=pl.BlockSpec((ROWS_DEV, tile_cols), lambda b: (0, b)),
        out_shape=jax.ShapeDtypeStruct((ROWS_DEV, ncol), F32),
        scratch_shapes=[
            pltpu.VMEM((blocks * per_block + 2, long, LANES), F32),
            pltpu.VMEM((2, 2, ROWS_DEV, LANES), F32),
        ],
        name="convolve",
        compiler_params=pltpu.CompilerParams(vmem_limit_bytes=28 << 20),
        cost_estimate=pl.CostEstimate(flops=15_000_000_000, bytes_accessed=10_000_000, transcendentals=0),
    )
    arrays = [pltpu.with_memory_space_constraint(x, pltpu.VMEM) for x in arrays]
    matched = convolve(*arrays, psf_poly, toep_hi, toep_lo, band, got_a)
    unit = ROWS_DEV // 16
    rest = pl.BlockSpec((1, unit, ncol), lambda i: (0, 2 * FIRST_PART + i, 0))
    return pl.pallas_call(
        subtract_kernel,
        grid=(2 * (8 - FIRST_PART),),
        in_specs=[vmem, rest],
        out_specs=rest,
        out_shape=jax.ShapeDtypeStruct((1, ROWS_DEV, ncol), F32),
        input_output_aliases={1: 0},
        name="subtract",
        compiler_params=pltpu.CompilerParams(vmem_limit_bytes=16 << 20),
        cost_estimate=pl.CostEstimate(flops=1_000_000, bytes_accessed=6_000_000, transcendentals=0),
    )(pltpu.with_memory_space_constraint(got_b, pltpu.VMEM), matched[None])


def solution(mesh):
    in_specs = (
        P("epoch", "strip", None, None),
        P("epoch", "strip"),
        P("epoch", "strip"),
        P("epoch", None, None),
        P(),
        P(),
        P(),
        P(),
    )
    out_specs = P("epoch", "strip", None)

    return jax.shard_map(shards, mesh=mesh, in_specs=in_specs, out_specs=out_specs, check_vma=False)
```

```python
import functools

import jax
import jax.numpy as jnp
from jax import lax
from jax.experimental import pallas as pl
from jax.experimental.pallas import tpu as pltpu
from jax.sharding import PartitionSpec as P


ROWS_DEV = 256
HALO = 16
FIRST_PART = 3
LANES = 128
F32 = jnp.float32
BF16 = jnp.bfloat16


def split(x):
    hi = x.astype(BF16)
    lo = (x - hi.astype(F32)).astype(BF16)
    return hi, lo


def dot(a, b, trans_b=False):
    dims = (((1,), (1 if trans_b else 0,)), ((), ()))
    return lax.dot_general(a, b, dims, preferred_element_type=F32)


def dot3(a, b, trans_b=False):
    a_hi, a_lo = a
    b_hi, b_lo = b
    both = dot(jnp.concatenate([a_hi, a_lo], axis=0), b_hi, trans_b)
    rows = a_hi.shape[0]
    return both[:rows] + (both[rows:] + dot(a_hi, b_lo, trans_b))


def start_and_wait(copies):
    for copy in copies:
        copy.start()
    for copy in copies:
        copy.wait()


def slot_order(count, order):
    bits = len(order)
    key = lambda j: sum(((j >> order[i]) & 1) << (bits - 1 - i) for i in range(bits))
    slots = sorted(range(count), key=key)
    return slots[: count // 2], slots[count // 2 :]


def warp_kernel(
    geom, kind_ref, heights_ref, invvar_ref, raw_ref, rmat_ref, cmat_ref,
    sci_a, sci_b, keep_a, send_a, keep_b, send_b,
    sci_s, num_s, wt_s, rmat_s, cmat_s, chi_s, clo_s, top_s, ready_s, fetch_sems, sems, wt_sems,
):
    epochs, nrow, share, orders, tiles = geom
    step = pl.program_id(0)
    together, tile_rows, tile_cols = raw_ref.shape
    last = pl.num_programs(0) - 1
    per_col = heights_ref.shape[2]
    span = tile_rows + 8
    me = lax.axis_index("epoch")
    first_tile = lax.axis_index("strip") * tiles
    block = lax.div(first_tile, per_col)
    offset_in = lax.rem(first_tile, per_col)
    kinds = cmat_ref.shape[0]
    strips, rows_a, _ = sci_a.shape
    rows_dev = rows_a + sci_b.shape[1]
    nhalf = nrow // 2
    outs = (keep_a, send_a), (keep_b, send_b)

    def fetches(k):
        return [
            pltpu.make_async_copy(cmat_ref.at[k], cmat_s.at[k], fetch_sems.at[k, 0]),
            pltpu.make_async_copy(rmat_ref.at[k], rmat_s.at[k], fetch_sems.at[k, 1]),
        ]

    def strip_copies(s):
        base = s * rows_dev
        part = base // nhalf
        pairs = [
            (sci_s.at[pl.ds(base, rows_a)], sci_a.at[s]),
            (sci_s.at[pl.ds(base + rows_a, rows_dev - rows_a)], sci_b.at[s]),
        ]
        for slots, out in zip(slot_order(epochs, orders[part]), outs[part]):
            for place, j in enumerate(slots):
                pairs.append(
                    (num_s.at[j, pl.ds(base, rows_dev)], out.at[place, pl.ds(base - part * nhalf, rows_dev)])
                )
        return [pltpu.make_async_copy(a, b, sems.at[s, n]) for n, (a, b) in enumerate(pairs)]

    @pl.when(step == 0)
    def _():
        top_s[0] = lax.fori_loop(
            0, offset_in, lambda i, total: total + heights_ref[0, block, i], jnp.int32(0)
        )
        top_s[1] = 0
        first = kind_ref[0, 0]
        for i in range(kinds):
            ready_s[i] = 0
            for copy in fetches(lax.rem(first + i, kinds)):
                copy.start()
        if tiles != per_col:
            sci_s[...] = jnp.zeros_like(sci_s)
            num_s[...] = jnp.zeros_like(num_s)
            wt_s[...] = jnp.zeros_like(wt_s)

    for i in range(together):
        kind = kind_ref[0, step * together + i]

        @pl.when(ready_s[kind] == 0)
        def _():
            for copy in fetches(kind):
                copy.wait()
            ready_s[kind] = 1

            def divide(n, carry):
                here = pl.ds(pl.multiple_of(n * (tile_cols // 8), tile_cols // 8), tile_cols // 8)
                chi_s[kind, here, :], clo_s[kind, here, :] = split(cmat_s[kind, here, :])
                return carry

            lax.fori_loop(0, 8, divide, 0)

    top = top_s[0]
    local = lax.broadcasted_iota(jnp.int32, (span, share), 0)
    flat = lax.broadcasted_iota(jnp.int32, wt_s.shape, 0) * share + lax.broadcasted_iota(
        jnp.int32, wt_s.shape, 1
    )
    live = lax.broadcasted_iota(jnp.int32, (tile_rows, tile_rows), 1)
    tops, heights, kind_of = [], [], []
    for i in range(together):
        t = step * together + i
        tops.append(top)
        heights.append(heights_ref[0, block, offset_in + t])
        kind_of.append(kind_ref[0, t])
        top = top + heights[i]
    top_s[0] = top
    after = top
    starts = [pl.multiple_of(jnp.minimum(lax.div(x, 8) * 8, nrow - span), 8) for x in tops]
    images, wides, mixes, halves, placed = [{} for _ in range(5)]

    def load(i):
        images[i] = split(raw_ref[i])

    def across(i):
        wides[i] = dot3(images[i], (chi_s[kind_of[i]], clo_s[kind_of[i]]), trans_b=True)

    def divide_half(i):
        rows = jnp.concatenate(
            [jnp.where(live < heights[i], rmat_s[kind_of[i]], 0.0), jnp.zeros((8, tile_rows), F32)], axis=0
        )
        mixes[i] = split(pltpu.roll(rows, tops[i] - starts[i], 0))
        halves[i] = split(wides[i])

    def down(i):
        placed[i] = dot3(mixes[i], halves[i])

    def store(i):
        weight = invvar_ref[0, step * together + i]
        inside = local - (tops[i] - starts[i])
        own = (inside >= 0) & (inside < heights[i])
        here = pl.ds(starts[i], span)
        for q in range(epochs):
            columns = pl.ds(q * share, share)
            piece = placed[i][:, q * share : (q + 1) * share]
            slot = jnp.bitwise_xor(me, q)
            sci_s[here, columns] = jnp.where(own, piece, sci_s[here, columns])
            num_s[slot, here, :] = jnp.where(own, weight * piece, num_s[slot, here, :])
        wt_s[...] = jnp.where((flat >= tops[i]) & (flat < tops[i] + heights[i]), weight, wt_s[...])

    phases = (load, across, divide_half, down, store)
    for n in range(len(phases) + together - 1):
        for i in range(together):
            if 0 <= n - i < len(phases):
                phases[n - i](i)

    before = top_s[1]
    final = jnp.where(step == last, nrow, jnp.minimum(lax.div(after, 8) * 8, nrow - span))
    top_s[1] = final
    for s in range(strips):
        end = (s + 1) * rows_dev

        @pl.when((before < end) & (end <= final))
        def _():
            for copy in strip_copies(s):
                copy.start()

    @pl.when(step == last)
    def _():
        whalf = wt_s.shape[0] // 2
        copies = []
        for part, order in enumerate(orders):
            for slots, out in zip(slot_order(epochs, order), outs[part]):
                for place in range(len(slots)):
                    copies.append(
                        pltpu.make_async_copy(
                            wt_s.at[pl.ds(part * whalf, whalf)],
                            out.at[place, pl.ds(nhalf, whalf)],
                            wt_sems.at[len(copies)],
                        )
                    )
        start_and_wait(copies)
        for s in range(strips):
            for copy in strip_copies(s):
                copy.wait()
        for k in range(kinds):

            @pl.when(ready_s[k] == 0)
            def _():
                for copy in fetches(k):
                    copy.wait()


def template_kernel(terms, *refs):
    term_refs, out_refs, pad_s = refs[: 2 * terms], refs[2 * terms : -1], refs[-1]
    strips = len(out_refs)
    long, share = out_refs[0].shape
    rows_dev = long - 2 * HALO
    nrow = strips * rows_dev
    nhalf = nrow // 2
    whalf = nhalf // share
    edge = jnp.zeros((HALO, share), F32)
    pad_s[pl.ds(0, HALO), :] = edge
    pad_s[pl.ds(HALO + nrow, HALO), :] = edge
    for part in range(2):
        own = term_refs[part * terms : (part + 1) * terms]
        add = lambda place: functools.reduce(lambda a, b: a + b, [ref[0, place, :] for ref in own])
        weights = add(pl.ds(nhalf, whalf))
        for i in range(whalf):
            below = jnp.transpose(jnp.broadcast_to(weights[i : i + 1, :], (share, share)))
            pad_s[pl.ds(HALO + part * nhalf + i * share, share), :] = add(pl.ds(i * share, share)) / below
    for k in range(strips):
        strip = jnp.bitwise_xor(lax.axis_index("strip"), k)
        out_refs[k][...] = pad_s[pl.ds(pl.multiple_of(strip * rows_dev, rows_dev), long), :]


def bands_kernel(psf_ref, toep_hi, toep_lo, band_ref):
    basis, _, ksize = psf_ref.shape
    margin = ksize // 2
    for k in range(basis):
        shape = (2 * LANES, LANES)
        tap = lax.broadcasted_iota(jnp.int32, shape, 0) - lax.broadcasted_iota(jnp.int32, shape, 1)
        tap = tap - (LANES // 2 - margin)
        value = jnp.zeros(shape, F32)
        for j in range(ksize):
            value = jnp.where(tap == j, psf_ref[k, 1, j], value)
        toep_hi[:, pl.ds(k * LANES, LANES)], toep_lo[:, pl.ds(k * LANES, LANES)] = split(value)
        shape = (LANES, LANES + 2 * HALO)
        tap = lax.broadcasted_iota(jnp.int32, shape, 1) - lax.broadcasted_iota(jnp.int32, shape, 0)
        tap = tap - (HALO - margin)
        value = jnp.zeros(shape, F32)
        for j in range(ksize):
            value = jnp.where(tap == j, psf_ref[k, 0, j], value)
        band_ref[k, pl.ds(0, LANES), :], band_ref[k, pl.ds(LANES, LANES), :] = split(value)


def match_kernel(geom, *refs):
    slots, nrow, ncol = geom
    count = max(len(slots), 1) + (len(slots) > 1)
    tile_refs = refs[:count]
    poly_ref, toep_hi, toep_lo, band_ref, sci_ref, out_ref, pad_s, row_s = refs[count:]
    step = pl.program_id(0)
    blocks = pl.num_programs(0)
    tiles = pad_s.shape[0] - 2
    rows_dev = pad_s.shape[1] - 2 * HALO
    me = lax.axis_index("epoch")
    strip = lax.axis_index("strip")
    per_step = out_ref.shape[1] // LANES

    def bring(b):
        if not slots:
            for i in range(per_step):
                place = b * per_step + i
                pad_s[1 + place] = tile_refs[0][place]
            return
        at = jnp.bitwise_xor(strip, b)
        for n, slot in enumerate(slots[:-1]):
            pad_s[1 + b * per_step + jnp.bitwise_xor(me, slot)] = tile_refs[n][at]
        place = 1 + b * per_step + jnp.bitwise_xor(me, slots[-1])
        cut = tile_refs[-1].shape[0]

        @pl.when(at < cut)
        def _():
            pad_s[place] = tile_refs[-2][at]

        @pl.when(at >= cut)
        def _():
            pad_s[place] = tile_refs[-1][at - cut]

    @pl.when(step == 0)
    def _():
        bring(0)
        pad_s[0] = jnp.zeros(pad_s.shape[1:], F32)
        pad_s[tiles + 1] = jnp.zeros(pad_s.shape[1:], F32)
        shape = (rows_dev, LANES)
        counter = (strip * rows_dev + lax.broadcasted_iota(jnp.int32, shape, 0)).astype(F32)
        u = (2.0 * counter + 1.0) / nrow - 1.0
        for k in range(2):
            p = [poly_ref[me, k, i] for i in range(6)]
            row_s[k, 0] = p[0] + u * (p[1] + p[3] * u)
            row_s[k, 1] = p[2] + p[4] * u

    @pl.when(step < blocks - 1)
    def _():
        bring(step + 1)

    lane = lax.broadcasted_iota(jnp.int32, pad_s.shape[1:], 1)
    base = step * per_step
    shifted = []
    for m in range(per_step + 1):
        mixed = jnp.where(lane < LANES // 2, pad_s[base + m + 1], pad_s[base + m])
        shifted.append(split(pltpu.roll(mixed, LANES // 2, 1)))
    toep = (toep_hi[...], toep_lo[...])
    for pair in range(per_step // 2):
        across = []
        for c in (2 * pair, 2 * pair + 1):
            window = tuple(
                jnp.concatenate([shifted[c][i], shifted[c + 1][i]], axis=1) for i in range(2)
            )
            across.append(dot3(window, toep))
        width = 2 * LANES
        cols = lax.broadcasted_iota(jnp.int32, (1, width), 1) + (base + 2 * pair) * LANES
        v = (2.0 * cols.astype(F32) + 1.0) / ncol - 1.0
        for part in range(rows_dev // LANES):
            total = 0.0
            for k in range(2):
                both = jnp.concatenate(
                    [a[part * LANES : part * LANES + LANES + 2 * HALO, k * LANES : (k + 1) * LANES] for a in across],
                    axis=1,
                )
                hi, lo = split(both)
                wide = dot(band_ref[k], hi)
                done = wide[:LANES] + (wide[LANES:] + dot(band_ref[k, pl.ds(0, LANES), :], lo))
                place = pl.ds(part * LANES, LANES)
                one = jnp.concatenate([row_s[k, 0, place, :]] * 2, axis=1)
                two = jnp.concatenate([row_s[k, 1, place, :]] * 2, axis=1)
                coeff = one + v * (two + poly_ref[me, k, 5] * v)
                total = total + coeff * done
            columns = pl.ds(pair * width, width)
            ready = min(max(sci_ref.shape[1] - part * LANES, 0), LANES)
            if ready:
                here = pl.ds(part * LANES, ready)
                out_ref[here, columns] = sci_ref[0, here, columns] - total[:ready]
            if ready < LANES:
                out_ref[pl.ds(part * LANES + ready, LANES - ready), columns] = total[ready:]


def subtract_kernel(sci_ref, matched_ref, out_ref):
    i = pl.program_id(0)
    blocks, _, width = sci_ref.shape
    rows = out_ref.shape[1]
    for b in range(blocks):
        columns = pl.ds(b * width, width)
        science = sci_ref[b, pl.ds(pl.multiple_of(i * rows, rows), rows), :]
        out_ref[0, :, columns] = science - matched_ref[0, :, columns]


def swap(value, axis, bit):
    count = lax.axis_size(axis)
    return lax.ppermute(value, axis, [(i, i ^ (1 << bit)) for i in range(count)])


def shards(
    raw_tiles, tile_kind, tile_invvar, tile_heights, row_interp, col_interp, psf_profiles, psf_poly
):
    strips, epochs = lax.axis_size("strip"), lax.axis_size("epoch")
    _, tiles, tile_rows, tile_cols = raw_tiles.shape
    _, blocks, _ = tile_heights.shape
    ncol, nrow = blocks * tile_cols, ROWS_DEV * strips
    sources = strips // blocks
    share = tile_cols // epochs
    bits = epochs.bit_length() - 1
    orders = (tuple(range(bits)), tuple(reversed(range(bits))))
    nhalf = nrow // 2
    wrows = nrow // share
    long_half = nhalf + wrows // 2
    smem = pl.BlockSpec(memory_space=pltpu.SMEM)
    hbm = pl.BlockSpec(memory_space=pl.ANY)
    vmem = pl.BlockSpec(memory_space=pltpu.VMEM)
    kinds = col_interp.shape[0]

    first_rows = ROWS_DEV * FIRST_PART // 8
    sci_shapes = [
        jax.ShapeDtypeStruct((strips, rows, tile_cols), F32) for rows in (first_rows, ROWS_DEV - first_rows)
    ]
    send_shape = jax.ShapeDtypeStruct((epochs // 2, long_half, share), F32)
    together = 2 if tiles % 2 == 0 else 1
    sci_a, sci_b, keep_a, send_a, keep_b, send_b = pl.pallas_call(
        functools.partial(warp_kernel, (epochs, nrow, share, orders, tiles)),
        grid=(tiles // together,),
        in_specs=[
            smem,
            smem,
            smem,
            pl.BlockSpec((together, tile_rows, tile_cols), lambda t: (t, 0, 0)),
            hbm,
            hbm,
        ],
        out_specs=[hbm] * 6,
        out_shape=sci_shapes + [send_shape] * 4,
        scratch_shapes=[
            pltpu.VMEM((nrow, tile_cols), F32),
            pltpu.VMEM((epochs, nrow, share), F32),
            pltpu.VMEM((wrows, share), F32),
            pltpu.VMEM((kinds, tile_rows, tile_rows), F32),
            pltpu.VMEM((kinds, tile_cols, tile_cols), F32),
            pltpu.VMEM((kinds, tile_cols, tile_cols), BF16),
            pltpu.VMEM((kinds, tile_cols, tile_cols), BF16),
            pltpu.SMEM((2,), jnp.int32),
            pltpu.SMEM((kinds,), jnp.int32),
            pltpu.SemaphoreType.DMA((kinds, 2)),
            pltpu.SemaphoreType.DMA((strips, 2 + epochs)),
            pltpu.SemaphoreType.DMA((2 * epochs,)),
        ],
        name="warp",
        cost_estimate=pl.CostEstimate(flops=8_000_000_000, bytes_accessed=20_000_000, transcendentals=0),
    )(tile_kind, tile_heights, tile_invvar, raw_tiles[0], row_interp, col_interp)

    got_a = lax.all_to_all(sci_a, "strip", split_axis=0, concat_axis=0, tiled=True)

    basis, _, _ = psf_profiles.shape
    build_bands = pl.pallas_call(
        bands_kernel,
        in_specs=[smem],
        out_specs=[vmem] * 3,
        out_shape=[
            jax.ShapeDtypeStruct((2 * LANES, 2 * LANES), BF16),
            jax.ShapeDtypeStruct((2 * LANES, 2 * LANES), BF16),
            jax.ShapeDtypeStruct((basis, 2 * LANES, LANES + 2 * HALO), BF16),
        ],
        name="bands",
        cost_estimate=pl.CostEstimate(flops=10_000_000, bytes_accessed=500_000, transcendentals=0),
    )
    toep_hi, toep_lo, band = build_bands(psf_profiles)

    terms = [[keep_a], [keep_b]]
    sends = [send_a, send_b]
    for i in range(bits):
        for part in range(2):
            terms[part].append(swap(sends[part], "epoch", orders[part][i]))
        left = epochs >> (i + 1)
        if left > 1:
            sends = [
                functools.reduce(lambda a, b: a + b, [t[left // 2 : left] for t in own]) for own in terms
            ]
    if sources > 1:
        fixed = []
        for own in terms:
            total = functools.reduce(lambda a, b: a + b, [t[:1] for t in own])
            around = total
            for k in range(1, sources):
                ring = [(i, i // sources * sources + (i + k) % sources) for i in range(strips)]
                around = around + lax.ppermute(total, "strip", ring)
            fixed.append([around])
        terms = fixed

    long = ROWS_DEV + 2 * HALO
    first_slot = pl.BlockSpec((1, long_half, share), lambda i: (0, 0, 0))
    kinds_of_term = [first_slot] * (len(terms[0]) - 1) + [vmem]
    for own in terms:
        own[-1] = pltpu.with_memory_space_constraint(own[-1], pltpu.VMEM)
    parts = pl.pallas_call(
        functools.partial(template_kernel, len(terms[0])),
        grid=(1,),
        in_specs=kinds_of_term * 2,
        out_specs=[pl.BlockSpec((long, share), lambda i: (0, 0))] * strips,
        out_shape=[jax.ShapeDtypeStruct((long, share), F32)] * strips,
        scratch_shapes=[pltpu.VMEM((nrow + 2 * HALO, share), F32)],
        name="template",
        cost_estimate=pl.CostEstimate(flops=2_000_000, bytes_accessed=5_000_000, transcendentals=0),
    )(*terms[0], *terms[1])
    came = [None] * strips
    came[0] = parts[0]
    for k in reversed(range(1, strips)):
        came[k] = lax.ppermute(parts[k], "strip", [(i, i ^ k) for i in range(strips)])
    came[strips // 2], got_a = lax.optimization_barrier((came[strips // 2], got_a))
    mine = jnp.stack(came[:: sources])
    sci_b, mine = lax.optimization_barrier((sci_b, mine))
    got_b = lax.all_to_all(sci_b, "strip", split_axis=0, concat_axis=0, tiled=True)
    if sources > 1:
        got_a = jnp.sum(got_a.reshape((blocks, sources) + got_a.shape[1:]), axis=1)
        got_b = jnp.sum(got_b.reshape((blocks, sources) + got_b.shape[1:]), axis=1)

    per_block = tile_cols // LANES
    if epochs == 4 and share == LANES:
        near = []
        for b in range(2):
            near.append(swap(mine, "epoch", b))
        cut = blocks // 2
        far_low = swap(near[1][:cut], "epoch", 0)
        far_high = swap(near[0][cut:], "epoch", 1)
        arrays = [mine, near[0], near[1], far_low, far_high]
        held = (0, 1, 2, 3)
    else:
        slots = [mine]
        for b in range(bits):
            slots = slots + [swap(s, "epoch", b) for s in slots]
        me = lax.axis_index("epoch")
        every = jnp.take(jnp.stack(slots), jnp.bitwise_xor(jnp.arange(epochs), me), axis=0)
        home = lax.axis_index("strip") // sources
        every = jnp.take(every, jnp.bitwise_xor(jnp.arange(blocks), home), axis=1)
        flat = jnp.transpose(every, (1, 2, 0, 3)).reshape(blocks, long, per_block, LANES)
        arrays = [jnp.transpose(flat, (0, 2, 1, 3)).reshape(blocks * per_block, long, LANES)]
        held = ()

    const = lambda b: (0, 0)
    convolve = pl.pallas_call(
        functools.partial(match_kernel, (held, nrow, ncol)),
        grid=(blocks,),
        in_specs=[vmem] * len(arrays)
        + [
            smem,
            pl.BlockSpec(toep_hi.shape, const),
            pl.BlockSpec(toep_lo.shape, const),
            pl.BlockSpec(band.shape, lambda b: (0, 0, 0)),
            pl.BlockSpec((1,) + got_a.shape[1:], lambda b: (b, 0, 0)),
        ],
        out_specs=pl.BlockSpec((ROWS_DEV, tile_cols), lambda b: (0, b)),
        out_shape=jax.ShapeDtypeStruct((ROWS_DEV, ncol), F32),
        scratch_shapes=[
            pltpu.VMEM((blocks * per_block + 2, long, LANES), F32),
            pltpu.VMEM((2, 2, ROWS_DEV, LANES), F32),
        ],
        name="convolve",
        compiler_params=pltpu.CompilerParams(vmem_limit_bytes=28 << 20),
        cost_estimate=pl.CostEstimate(flops=15_000_000_000, bytes_accessed=10_000_000, transcendentals=0),
    )
    arrays = [pltpu.with_memory_space_constraint(x, pltpu.VMEM) for x in arrays]
    matched = convolve(*arrays, psf_poly, toep_hi, toep_lo, band, got_a)
    unit = ROWS_DEV // 8
    rest = pl.BlockSpec((1, unit, ncol), lambda i: (0, FIRST_PART + i, 0))
    return pl.pallas_call(
        subtract_kernel,
        grid=(8 - FIRST_PART,),
        in_specs=[vmem, rest],
        out_specs=rest,
        out_shape=jax.ShapeDtypeStruct((1, ROWS_DEV, ncol), F32),
        input_output_aliases={1: 0},
        name="subtract",
        compiler_params=pltpu.CompilerParams(vmem_limit_bytes=16 << 20),
        cost_estimate=pl.CostEstimate(flops=1_000_000, bytes_accessed=6_000_000, transcendentals=0),
    )(pltpu.with_memory_space_constraint(got_b, pltpu.VMEM), matched[None])


def solution(mesh):
    in_specs = (
        P("epoch", "strip", None, None),
        P("epoch", "strip"),
        P("epoch", "strip"),
        P("epoch", None, None),
        P(),
        P(),
        P(),
        P(),
    )
    out_specs = P("epoch", "strip", None)

    return jax.shard_map(shards, mesh=mesh, in_specs=in_specs, out_specs=out_specs, check_vma=False)
```

```python
import functools

import jax
import jax.numpy as jnp
from jax import lax
from jax.experimental import pallas as pl
from jax.experimental.pallas import tpu as pltpu
from jax.sharding import PartitionSpec as P


ROWS_DEV = 256
HALO = 16
FIRST_PART = 3
LANES = 128
F32 = jnp.float32
BF16 = jnp.bfloat16


def split(x):
    hi = x.astype(BF16)
    lo = (x - hi.astype(F32)).astype(BF16)
    return hi, lo


def dot(a, b, trans_b=False):
    dims = (((1,), (1 if trans_b else 0,)), ((), ()))
    return lax.dot_general(a, b, dims, preferred_element_type=F32)


def dot3(a, b, trans_b=False):
    a_hi, a_lo = a
    b_hi, b_lo = b
    both = dot(jnp.concatenate([a_hi, a_lo], axis=0), b_hi, trans_b)
    rows = a_hi.shape[0]
    return both[:rows] + (both[rows:] + dot(a_hi, b_lo, trans_b))


def start_and_wait(copies):
    for copy in copies:
        copy.start()
    for copy in copies:
        copy.wait()


def slot_order(count, order):
    bits = len(order)
    key = lambda j: sum(((j >> order[i]) & 1) << (bits - 1 - i) for i in range(bits))
    slots = sorted(range(count), key=key)
    return slots[: count // 2], slots[count // 2 :]


def warp_kernel(
    geom, kind_ref, heights_ref, invvar_ref, raw_ref, rmat_ref, cmat_ref,
    sci_a, sci_b, keep_a, send_a, keep_b, send_b,
    sci_s, num_s, wt_s, rmat_s, cmat_s, chi_s, clo_s, top_s, ready_s, fetch_sems, sems, wt_sems,
):
    epochs, nrow, share, orders, tiles = geom
    step = pl.program_id(0)
    together, tile_rows, tile_cols = raw_ref.shape
    last = pl.num_programs(0) - 1
    per_col = heights_ref.shape[2]
    span = tile_rows + 8
    me = lax.axis_index("epoch")
    first_tile = lax.axis_index("strip") * tiles
    block = lax.div(first_tile, per_col)
    offset_in = lax.rem(first_tile, per_col)
    kinds = cmat_ref.shape[0]
    strips, rows_a, _ = sci_a.shape
    rows_dev = rows_a + sci_b.shape[1]
    nhalf = nrow // 2
    outs = (keep_a, send_a), (keep_b, send_b)

    def fetches(k):
        return [
            pltpu.make_async_copy(cmat_ref.at[k], cmat_s.at[k], fetch_sems.at[k, 0]),
            pltpu.make_async_copy(rmat_ref.at[k], rmat_s.at[k], fetch_sems.at[k, 1]),
        ]

    def strip_copies(s):
        base = s * rows_dev
        part = base // nhalf
        pairs = [
            (sci_s.at[pl.ds(base + rows_dev - rows_a, rows_a)], sci_a.at[s]),
            (sci_s.at[pl.ds(base, rows_dev - rows_a)], sci_b.at[s]),
        ]
        for slots, out in zip(slot_order(epochs, orders[part]), outs[part]):
            for place, j in enumerate(slots):
                pairs.append(
                    (num_s.at[j, pl.ds(base, rows_dev)], out.at[place, pl.ds(base - part * nhalf, rows_dev)])
                )
        return [pltpu.make_async_copy(a, b, sems.at[s, n]) for n, (a, b) in enumerate(pairs)]

    @pl.when(step == 0)
    def _():
        top_s[0] = lax.fori_loop(
            0, offset_in, lambda i, total: total + heights_ref[0, block, i], jnp.int32(0)
        )
        top_s[1] = 0
        first = kind_ref[0, 0]
        for i in range(kinds):
            ready_s[i] = 0
            for copy in fetches(lax.rem(first + i, kinds)):
                copy.start()
        if tiles != per_col:
            sci_s[...] = jnp.zeros_like(sci_s)
            num_s[...] = jnp.zeros_like(num_s)
            wt_s[...] = jnp.zeros_like(wt_s)

    for i in range(together):
        kind = kind_ref[0, step * together + i]

        @pl.when(ready_s[kind] == 0)
        def _():
            for copy in fetches(kind):
                copy.wait()
            ready_s[kind] = 1

            def divide(n, carry):
                here = pl.ds(pl.multiple_of(n * (tile_cols // 8), tile_cols // 8), tile_cols // 8)
                chi_s[kind, here, :], clo_s[kind, here, :] = split(cmat_s[kind, here, :])
                return carry

            lax.fori_loop(0, 8, divide, 0)

    top = top_s[0]
    local = lax.broadcasted_iota(jnp.int32, (span, share), 0)
    flat = lax.broadcasted_iota(jnp.int32, wt_s.shape, 0) * share + lax.broadcasted_iota(
        jnp.int32, wt_s.shape, 1
    )
    live = lax.broadcasted_iota(jnp.int32, (tile_rows, tile_rows), 1)
    tops, heights, kind_of = [], [], []
    for i in range(together):
        t = step * together + i
        tops.append(top)
        heights.append(heights_ref[0, block, offset_in + t])
        kind_of.append(kind_ref[0, t])
        top = top + heights[i]
    top_s[0] = top
    after = top
    starts = [pl.multiple_of(jnp.minimum(lax.div(x, 8) * 8, nrow - span), 8) for x in tops]
    images, wides, mixes, halves, placed = [{} for _ in range(5)]

    def load(i):
        images[i] = split(raw_ref[i])

    def across(i):
        wides[i] = dot3(images[i], (chi_s[kind_of[i]], clo_s[kind_of[i]]), trans_b=True)

    def divide_half(i):
        rows = jnp.concatenate(
            [jnp.where(live < heights[i], rmat_s[kind_of[i]], 0.0), jnp.zeros((8, tile_rows), F32)], axis=0
        )
        mixes[i] = split(pltpu.roll(rows, tops[i] - starts[i], 0))
        halves[i] = split(wides[i])

    def down(i):
        placed[i] = dot3(mixes[i], halves[i])

    def store(i):
        weight = invvar_ref[0, step * together + i]
        inside = local - (tops[i] - starts[i])
        own = (inside >= 0) & (inside < heights[i])
        here = pl.ds(starts[i], span)
        for q in range(epochs):
            columns = pl.ds(q * share, share)
            piece = placed[i][:, q * share : (q + 1) * share]
            slot = jnp.bitwise_xor(me, q)
            sci_s[here, columns] = jnp.where(own, piece, sci_s[here, columns])
            num_s[slot, here, :] = jnp.where(own, weight * piece, num_s[slot, here, :])
        wt_s[...] = jnp.where((flat >= tops[i]) & (flat < tops[i] + heights[i]), weight, wt_s[...])

    phases = (load, across, divide_half, down, store)
    for n in range(len(phases) + together - 1):
        for i in range(together):
            if 0 <= n - i < len(phases):
                phases[n - i](i)

    before = top_s[1]
    final = jnp.where(step == last, nrow, jnp.minimum(lax.div(after, 8) * 8, nrow - span))
    top_s[1] = final
    for s in range(strips):
        end = (s + 1) * rows_dev

        @pl.when((before < end) & (end <= final))
        def _():
            for copy in strip_copies(s):
                copy.start()

    @pl.when(step == last)
    def _():
        whalf = wt_s.shape[0] // 2
        copies = []
        for part, order in enumerate(orders):
            for slots, out in zip(slot_order(epochs, order), outs[part]):
                for place in range(len(slots)):
                    copies.append(
                        pltpu.make_async_copy(
                            wt_s.at[pl.ds(part * whalf, whalf)],
                            out.at[place, pl.ds(nhalf, whalf)],
                            wt_sems.at[len(copies)],
                        )
                    )
        start_and_wait(copies)
        for s in range(strips):
            for copy in strip_copies(s):
                copy.wait()
        for k in range(kinds):

            @pl.when(ready_s[k] == 0)
            def _():
                for copy in fetches(k):
                    copy.wait()


def template_kernel(terms, *refs):
    term_refs, out_refs, pad_s = refs[: 2 * terms], refs[2 * terms : -1], refs[-1]
    strips = len(out_refs)
    long, share = out_refs[0].shape
    rows_dev = long - 2 * HALO
    nrow = strips * rows_dev
    nhalf = nrow // 2
    whalf = nhalf // share
    edge = jnp.zeros((HALO, share), F32)
    pad_s[pl.ds(0, HALO), :] = edge
    pad_s[pl.ds(HALO + nrow, HALO), :] = edge
    for part in range(2):
        own = term_refs[part * terms : (part + 1) * terms]
        add = lambda place: functools.reduce(lambda a, b: a + b, [ref[0, place, :] for ref in own])
        weights = add(pl.ds(nhalf, whalf))
        for i in range(whalf):
            below = jnp.transpose(jnp.broadcast_to(weights[i : i + 1, :], (share, share)))
            pad_s[pl.ds(HALO + part * nhalf + i * share, share), :] = add(pl.ds(i * share, share)) / below
    for k in range(strips):
        strip = jnp.bitwise_xor(lax.axis_index("strip"), k)
        out_refs[k][...] = pad_s[pl.ds(pl.multiple_of(strip * rows_dev, rows_dev), long), :]


def bands_kernel(psf_ref, toep_hi, toep_lo, band_ref):
    basis, _, ksize = psf_ref.shape
    margin = ksize // 2
    for k in range(basis):
        shape = (2 * LANES, LANES)
        tap = lax.broadcasted_iota(jnp.int32, shape, 0) - lax.broadcasted_iota(jnp.int32, shape, 1)
        tap = tap - (LANES // 2 - margin)
        value = jnp.zeros(shape, F32)
        for j in range(ksize):
            value = jnp.where(tap == j, psf_ref[k, 1, j], value)
        toep_hi[:, pl.ds(k * LANES, LANES)], toep_lo[:, pl.ds(k * LANES, LANES)] = split(value)
        shape = (LANES, LANES + 2 * HALO)
        tap = lax.broadcasted_iota(jnp.int32, shape, 1) - lax.broadcasted_iota(jnp.int32, shape, 0)
        tap = tap - (HALO - margin)
        value = jnp.zeros(shape, F32)
        for j in range(ksize):
            value = jnp.where(tap == j, psf_ref[k, 0, j], value)
        band_ref[k, pl.ds(0, LANES), :], band_ref[k, pl.ds(LANES, LANES), :] = split(value)


def match_kernel(geom, *refs):
    slots, nrow, ncol = geom
    count = max(len(slots), 1) + (len(slots) > 1)
    tile_refs = refs[:count]
    poly_ref, toep_hi, toep_lo, band_ref, sci_ref, out_ref, pad_s, row_s = refs[count:]
    step = pl.program_id(0)
    blocks = pl.num_programs(0)
    tiles = pad_s.shape[0] - 2
    rows_dev = pad_s.shape[1] - 2 * HALO
    me = lax.axis_index("epoch")
    strip = lax.axis_index("strip")
    per_step = out_ref.shape[1] // LANES

    def bring(b):
        if not slots:
            for i in range(per_step):
                place = b * per_step + i
                pad_s[1 + place] = tile_refs[0][place]
            return
        at = jnp.bitwise_xor(strip, b)
        for n, slot in enumerate(slots[:-1]):
            pad_s[1 + b * per_step + jnp.bitwise_xor(me, slot)] = tile_refs[n][at]
        place = 1 + b * per_step + jnp.bitwise_xor(me, slots[-1])
        cut = tile_refs[-1].shape[0]

        @pl.when(at < cut)
        def _():
            pad_s[place] = tile_refs[-2][at]

        @pl.when(at >= cut)
        def _():
            pad_s[place] = tile_refs[-1][at - cut]

    @pl.when(step == 0)
    def _():
        bring(0)
        pad_s[0] = jnp.zeros(pad_s.shape[1:], F32)
        pad_s[tiles + 1] = jnp.zeros(pad_s.shape[1:], F32)
        shape = (rows_dev, LANES)
        counter = (strip * rows_dev + lax.broadcasted_iota(jnp.int32, shape, 0)).astype(F32)
        u = (2.0 * counter + 1.0) / nrow - 1.0
        for k in range(2):
            p = [poly_ref[me, k, i] for i in range(6)]
            row_s[k, 0] = p[0] + u * (p[1] + p[3] * u)
            row_s[k, 1] = p[2] + p[4] * u

    @pl.when(step < blocks - 1)
    def _():
        bring(step + 1)

    lane = lax.broadcasted_iota(jnp.int32, pad_s.shape[1:], 1)
    base = step * per_step
    shifted = []
    for m in range(per_step + 1):
        mixed = jnp.where(lane < LANES // 2, pad_s[base + m + 1], pad_s[base + m])
        shifted.append(split(pltpu.roll(mixed, LANES // 2, 1)))
    toep = (toep_hi[...], toep_lo[...])
    for pair in range(per_step // 2):
        across = []
        for c in (2 * pair, 2 * pair + 1):
            window = tuple(
                jnp.concatenate([shifted[c][i], shifted[c + 1][i]], axis=1) for i in range(2)
            )
            across.append(dot3(window, toep))
        width = 2 * LANES
        cols = lax.broadcasted_iota(jnp.int32, (1, width), 1) + (base + 2 * pair) * LANES
        v = (2.0 * cols.astype(F32) + 1.0) / ncol - 1.0
        for part in range(rows_dev // LANES):
            total = 0.0
            for k in range(2):
                both = jnp.concatenate(
                    [a[part * LANES : part * LANES + LANES + 2 * HALO, k * LANES : (k + 1) * LANES] for a in across],
                    axis=1,
                )
                hi, lo = split(both)
                wide = dot(band_ref[k], hi)
                done = wide[:LANES] + (wide[LANES:] + dot(band_ref[k, pl.ds(0, LANES), :], lo))
                place = pl.ds(part * LANES, LANES)
                one = jnp.concatenate([row_s[k, 0, place, :]] * 2, axis=1)
                two = jnp.concatenate([row_s[k, 1, place, :]] * 2, axis=1)
                coeff = one + v * (two + poly_ref[me, k, 5] * v)
                total = total + coeff * done
            columns = pl.ds(pair * width, width)
            first = rows_dev - sci_ref.shape[1]
            late = min(max(first - part * LANES, 0), LANES)
            if late:
                out_ref[pl.ds(part * LANES, late), columns] = total[:late]
            if late < LANES:
                here = pl.ds(part * LANES + late, LANES - late)
                own = pl.ds(part * LANES + late - first, LANES - late)
                out_ref[here, columns] = sci_ref[0, own, columns] - total[late:]


def subtract_kernel(sci_ref, matched_ref, out_ref):
    i = pl.program_id(0)
    blocks, _, width = sci_ref.shape
    rows = out_ref.shape[1]
    for b in range(blocks):
        columns = pl.ds(b * width, width)
        science = sci_ref[b, pl.ds(pl.multiple_of(i * rows, rows), rows), :]
        out_ref[0, :, columns] = science - matched_ref[0, :, columns]


def swap(value, axis, bit):
    count = lax.axis_size(axis)
    return lax.ppermute(value, axis, [(i, i ^ (1 << bit)) for i in range(count)])


def shards(
    raw_tiles, tile_kind, tile_invvar, tile_heights, row_interp, col_interp, psf_profiles, psf_poly
):
    strips, epochs = lax.axis_size("strip"), lax.axis_size("epoch")
    _, tiles, tile_rows, tile_cols = raw_tiles.shape
    _, blocks, _ = tile_heights.shape
    ncol, nrow = blocks * tile_cols, ROWS_DEV * strips
    sources = strips // blocks
    share = tile_cols // epochs
    bits = epochs.bit_length() - 1
    orders = (tuple(range(bits)), tuple(reversed(range(bits))))
    nhalf = nrow // 2
    wrows = nrow // share
    long_half = nhalf + wrows // 2
    smem = pl.BlockSpec(memory_space=pltpu.SMEM)
    hbm = pl.BlockSpec(memory_space=pl.ANY)
    vmem = pl.BlockSpec(memory_space=pltpu.VMEM)
    kinds = col_interp.shape[0]

    first_rows = ROWS_DEV * FIRST_PART // 8
    sci_shapes = [
        jax.ShapeDtypeStruct((strips, rows, tile_cols), F32) for rows in (first_rows, ROWS_DEV - first_rows)
    ]
    send_shape = jax.ShapeDtypeStruct((epochs // 2, long_half, share), F32)
    together = 2 if tiles % 2 == 0 else 1
    sci_a, sci_b, keep_a, send_a, keep_b, send_b = pl.pallas_call(
        functools.partial(warp_kernel, (epochs, nrow, share, orders, tiles)),
        grid=(tiles // together,),
        in_specs=[
            smem,
            smem,
            smem,
            pl.BlockSpec((together, tile_rows, tile_cols), lambda t: (t, 0, 0)),
            hbm,
            hbm,
        ],
        out_specs=[hbm] * 6,
        out_shape=sci_shapes + [send_shape] * 4,
        scratch_shapes=[
            pltpu.VMEM((nrow, tile_cols), F32),
            pltpu.VMEM((epochs, nrow, share), F32),
            pltpu.VMEM((wrows, share), F32),
            pltpu.VMEM((kinds, tile_rows, tile_rows), F32),
            pltpu.VMEM((kinds, tile_cols, tile_cols), F32),
            pltpu.VMEM((kinds, tile_cols, tile_cols), BF16),
            pltpu.VMEM((kinds, tile_cols, tile_cols), BF16),
            pltpu.SMEM((2,), jnp.int32),
            pltpu.SMEM((kinds,), jnp.int32),
            pltpu.SemaphoreType.DMA((kinds, 2)),
            pltpu.SemaphoreType.DMA((strips, 2 + epochs)),
            pltpu.SemaphoreType.DMA((2 * epochs,)),
        ],
        name="warp",
        cost_estimate=pl.CostEstimate(flops=8_000_000_000, bytes_accessed=20_000_000, transcendentals=0),
    )(tile_kind, tile_heights, tile_invvar, raw_tiles[0], row_interp, col_interp)

    got_a = lax.all_to_all(sci_a, "strip", split_axis=0, concat_axis=0, tiled=True)

    basis, _, _ = psf_profiles.shape
    build_bands = pl.pallas_call(
        bands_kernel,
        in_specs=[smem],
        out_specs=[vmem] * 3,
        out_shape=[
            jax.ShapeDtypeStruct((2 * LANES, 2 * LANES), BF16),
            jax.ShapeDtypeStruct((2 * LANES, 2 * LANES), BF16),
            jax.ShapeDtypeStruct((basis, 2 * LANES, LANES + 2 * HALO), BF16),
        ],
        name="bands",
        cost_estimate=pl.CostEstimate(flops=10_000_000, bytes_accessed=500_000, transcendentals=0),
    )
    toep_hi, toep_lo, band = build_bands(psf_profiles)

    terms = [[keep_a], [keep_b]]
    sends = [send_a, send_b]
    for i in range(bits):
        for part in range(2):
            terms[part].append(swap(sends[part], "epoch", orders[part][i]))
        left = epochs >> (i + 1)
        if left > 1:
            sends = [
                functools.reduce(lambda a, b: a + b, [t[left // 2 : left] for t in own]) for own in terms
            ]
    if sources > 1:
        fixed = []
        for own in terms:
            total = functools.reduce(lambda a, b: a + b, [t[:1] for t in own])
            around = total
            for k in range(1, sources):
                ring = [(i, i // sources * sources + (i + k) % sources) for i in range(strips)]
                around = around + lax.ppermute(total, "strip", ring)
            fixed.append([around])
        terms = fixed

    long = ROWS_DEV + 2 * HALO
    first_slot = pl.BlockSpec((1, long_half, share), lambda i: (0, 0, 0))
    kinds_of_term = [first_slot] * (len(terms[0]) - 1) + [vmem]
    for own in terms:
        own[-1] = pltpu.with_memory_space_constraint(own[-1], pltpu.VMEM)
    parts = pl.pallas_call(
        functools.partial(template_kernel, len(terms[0])),
        grid=(1,),
        in_specs=kinds_of_term * 2,
        out_specs=[pl.BlockSpec((long, share), lambda i: (0, 0))] * strips,
        out_shape=[jax.ShapeDtypeStruct((long, share), F32)] * strips,
        scratch_shapes=[pltpu.VMEM((nrow + 2 * HALO, share), F32)],
        name="template",
        cost_estimate=pl.CostEstimate(flops=2_000_000, bytes_accessed=5_000_000, transcendentals=0),
    )(*terms[0], *terms[1])
    came = [None] * strips
    came[0] = parts[0]
    for k in reversed(range(1, strips)):
        came[k] = lax.ppermute(parts[k], "strip", [(i, i ^ k) for i in range(strips)])
    came[strips // 2], got_a = lax.optimization_barrier((came[strips // 2], got_a))
    far = range(strips // 2, strips, sources)
    sci_b, got_a, *arrived = lax.optimization_barrier((sci_b, got_a, *[came[k] for k in far]))
    for k, value in zip(far, arrived):
        came[k] = value
    mine = jnp.stack(came[:: sources])
    got_b = lax.all_to_all(sci_b, "strip", split_axis=0, concat_axis=0, tiled=True)
    if sources > 1:
        got_a = jnp.sum(got_a.reshape((blocks, sources) + got_a.shape[1:]), axis=1)
        got_b = jnp.sum(got_b.reshape((blocks, sources) + got_b.shape[1:]), axis=1)

    per_block = tile_cols // LANES
    if epochs == 4 and share == LANES:
        near = []
        for b in range(2):
            near.append(swap(mine, "epoch", b))
        cut = blocks // 2
        far_low = swap(near[1][:cut], "epoch", 0)
        far_high = swap(near[0][cut:], "epoch", 1)
        arrays = [mine, near[0], near[1], far_low, far_high]
        held = (0, 1, 2, 3)
    else:
        slots = [mine]
        for b in range(bits):
            slots = slots + [swap(s, "epoch", b) for s in slots]
        me = lax.axis_index("epoch")
        every = jnp.take(jnp.stack(slots), jnp.bitwise_xor(jnp.arange(epochs), me), axis=0)
        home = lax.axis_index("strip") // sources
        every = jnp.take(every, jnp.bitwise_xor(jnp.arange(blocks), home), axis=1)
        flat = jnp.transpose(every, (1, 2, 0, 3)).reshape(blocks, long, per_block, LANES)
        arrays = [jnp.transpose(flat, (0, 2, 1, 3)).reshape(blocks * per_block, long, LANES)]
        held = ()

    const = lambda b: (0, 0)
    convolve = pl.pallas_call(
        functools.partial(match_kernel, (held, nrow, ncol)),
        grid=(blocks,),
        in_specs=[vmem] * len(arrays)
        + [
            smem,
            pl.BlockSpec(toep_hi.shape, const),
            pl.BlockSpec(toep_lo.shape, const),
            pl.BlockSpec(band.shape, lambda b: (0, 0, 0)),
            pl.BlockSpec((1,) + got_a.shape[1:], lambda b: (b, 0, 0)),
        ],
        out_specs=pl.BlockSpec((ROWS_DEV, tile_cols), lambda b: (0, b)),
        out_shape=jax.ShapeDtypeStruct((ROWS_DEV, ncol), F32),
        scratch_shapes=[
            pltpu.VMEM((blocks * per_block + 2, long, LANES), F32),
            pltpu.VMEM((2, 2, ROWS_DEV, LANES), F32),
        ],
        name="convolve",
        compiler_params=pltpu.CompilerParams(vmem_limit_bytes=28 << 20),
        cost_estimate=pl.CostEstimate(flops=15_000_000_000, bytes_accessed=10_000_000, transcendentals=0),
    )
    arrays = [pltpu.with_memory_space_constraint(x, pltpu.VMEM) for x in arrays]
    matched = convolve(*arrays, psf_poly, toep_hi, toep_lo, band, got_a)
    unit = (ROWS_DEV - first_rows) // 2
    late_rows = pl.BlockSpec((1, unit, ncol), lambda i: (0, i, 0))
    return pl.pallas_call(
        subtract_kernel,
        grid=(2,),
        in_specs=[vmem, late_rows],
        out_specs=late_rows,
        out_shape=jax.ShapeDtypeStruct((1, ROWS_DEV, ncol), F32),
        input_output_aliases={1: 0},
        name="subtract",
        compiler_params=pltpu.CompilerParams(vmem_limit_bytes=16 << 20),
        cost_estimate=pl.CostEstimate(flops=1_000_000, bytes_accessed=6_000_000, transcendentals=0),
    )(pltpu.with_memory_space_constraint(got_b, pltpu.VMEM), matched[None])


def solution(mesh):
    in_specs = (
        P("epoch", "strip", None, None),
        P("epoch", "strip"),
        P("epoch", "strip"),
        P("epoch", None, None),
        P(),
        P(),
        P(),
        P(),
    )
    out_specs = P("epoch", "strip", None)

    return jax.shard_map(shards, mesh=mesh, in_specs=in_specs, out_specs=out_specs, check_vma=False)
```

```python
import functools

import jax
import jax.numpy as jnp
from jax import lax
from jax.experimental import pallas as pl
from jax.experimental.pallas import tpu as pltpu
from jax.sharding import PartitionSpec as P


ROWS_DEV = 256
HALO = 16
FIRST_PART = 3
LANES = 128
F32 = jnp.float32
BF16 = jnp.bfloat16


def split(x):
    hi = x.astype(BF16)
    lo = (x - hi.astype(F32)).astype(BF16)
    return hi, lo


def dot(a, b, trans_b=False):
    dims = (((1,), (1 if trans_b else 0,)), ((), ()))
    return lax.dot_general(a, b, dims, preferred_element_type=F32)


def dot3(a, b, trans_b=False):
    a_hi, a_lo = a
    b_hi, b_lo = b
    both = dot(jnp.concatenate([a_hi, a_lo], axis=0), b_hi, trans_b)
    rows = a_hi.shape[0]
    return both[:rows] + (both[rows:] + dot(a_hi, b_lo, trans_b))


def start_and_wait(copies):
    for copy in copies:
        copy.start()
    for copy in copies:
        copy.wait()


def slot_order(count, order):
    bits = len(order)
    key = lambda j: sum(((j >> order[i]) & 1) << (bits - 1 - i) for i in range(bits))
    slots = sorted(range(count), key=key)
    return slots[: count // 2], slots[count // 2 :]


def warp_kernel(
    geom, kind_ref, heights_ref, invvar_ref, raw_ref, rmat_ref, cmat_ref,
    sci_a, sci_b, keep_a, send_a, keep_b, send_b,
    sci_s, num_s, wt_s, rmat_s, cmat_s, chi_s, clo_s, top_s, ready_s, fetch_sems, sems, wt_sems,
):
    epochs, nrow, share, orders, tiles = geom
    step = pl.program_id(0)
    together, tile_rows, tile_cols = raw_ref.shape
    last = pl.num_programs(0) - 1
    per_col = heights_ref.shape[2]
    span = tile_rows + 8
    me = lax.axis_index("epoch")
    first_tile = lax.axis_index("strip") * tiles
    block = lax.div(first_tile, per_col)
    offset_in = lax.rem(first_tile, per_col)
    kinds = cmat_ref.shape[0]
    strips, rows_a, _ = sci_a.shape
    rows_dev = rows_a + sci_b.shape[1]
    nhalf = nrow // 2
    outs = (keep_a, send_a), (keep_b, send_b)

    def fetches(k):
        return [
            pltpu.make_async_copy(cmat_ref.at[k], cmat_s.at[k], fetch_sems.at[k, 0]),
            pltpu.make_async_copy(rmat_ref.at[k], rmat_s.at[k], fetch_sems.at[k, 1]),
        ]

    def strip_copies(s):
        base = s * rows_dev
        part = base // nhalf
        pairs = [
            (sci_s.at[pl.ds(base + rows_dev - rows_a, rows_a)], sci_a.at[s]),
            (sci_s.at[pl.ds(base, rows_dev - rows_a)], sci_b.at[s]),
        ]
        for slots, out in zip(slot_order(epochs, orders[part]), outs[part]):
            for place, j in enumerate(slots):
                pairs.append(
                    (num_s.at[j, pl.ds(base, rows_dev)], out.at[place, pl.ds(base - part * nhalf, rows_dev)])
                )
        return [pltpu.make_async_copy(a, b, sems.at[s, n]) for n, (a, b) in enumerate(pairs)]

    @pl.when(step == 0)
    def _():
        top_s[0] = lax.fori_loop(
            0, offset_in, lambda i, total: total + heights_ref[0, block, i], jnp.int32(0)
        )
        top_s[1] = 0
        first = kind_ref[0, 0]
        for i in range(kinds):
            ready_s[i] = 0
            for copy in fetches(lax.rem(first + i, kinds)):
                copy.start()
        if tiles != per_col:
            sci_s[...] = jnp.zeros_like(sci_s)
            num_s[...] = jnp.zeros_like(num_s)
            wt_s[...] = jnp.zeros_like(wt_s)

    for i in range(together):
        kind = kind_ref[0, step * together + i]

        @pl.when(ready_s[kind] == 0)
        def _():
            for copy in fetches(kind):
                copy.wait()
            ready_s[kind] = 1

            def divide(n, carry):
                here = pl.ds(pl.multiple_of(n * (tile_cols // 8), tile_cols // 8), tile_cols // 8)
                chi_s[kind, here, :], clo_s[kind, here, :] = split(cmat_s[kind, here, :])
                return carry

            lax.fori_loop(0, 8, divide, 0)

    top = top_s[0]
    local = lax.broadcasted_iota(jnp.int32, (span, share), 0)
    flat = lax.broadcasted_iota(jnp.int32, wt_s.shape, 0) * share + lax.broadcasted_iota(
        jnp.int32, wt_s.shape, 1
    )
    live = lax.broadcasted_iota(jnp.int32, (tile_rows, tile_rows), 1)
    tops, heights, kind_of = [], [], []
    for i in range(together):
        t = step * together + i
        tops.append(top)
        heights.append(heights_ref[0, block, offset_in + t])
        kind_of.append(kind_ref[0, t])
        top = top + heights[i]
    top_s[0] = top
    after = top
    starts = [pl.multiple_of(jnp.minimum(lax.div(x, 8) * 8, nrow - span), 8) for x in tops]
    images, wides, mixes, halves, placed = [{} for _ in range(5)]

    def load(i):
        images[i] = split(raw_ref[i])

    def across(i):
        wides[i] = dot3(images[i], (chi_s[kind_of[i]], clo_s[kind_of[i]]), trans_b=True)

    def divide_half(i):
        rows = jnp.concatenate(
            [jnp.where(live < heights[i], rmat_s[kind_of[i]], 0.0), jnp.zeros((8, tile_rows), F32)], axis=0
        )
        mixes[i] = split(pltpu.roll(rows, tops[i] - starts[i], 0))
        halves[i] = split(wides[i])

    def down(i):
        placed[i] = dot3(mixes[i], halves[i])

    def store(i):
        weight = invvar_ref[0, step * together + i]
        inside = local - (tops[i] - starts[i])
        own = (inside >= 0) & (inside < heights[i])
        here = pl.ds(starts[i], span)
        for q in range(epochs):
            columns = pl.ds(q * share, share)
            piece = placed[i][:, q * share : (q + 1) * share]
            slot = jnp.bitwise_xor(me, q)
            sci_s[here, columns] = jnp.where(own, piece, sci_s[here, columns])
            num_s[slot, here, :] = jnp.where(own, weight * piece, num_s[slot, here, :])
        wt_s[...] = jnp.where((flat >= tops[i]) & (flat < tops[i] + heights[i]), weight, wt_s[...])

    phases = (load, across, divide_half, down, store)
    for n in range(len(phases) + together - 1):
        for i in range(together):
            if 0 <= n - i < len(phases):
                phases[n - i](i)

    before = top_s[1]
    final = jnp.where(step == last, nrow, jnp.minimum(lax.div(after, 8) * 8, nrow - span))
    top_s[1] = final
    for s in range(strips):
        end = (s + 1) * rows_dev

        @pl.when((before < end) & (end <= final))
        def _():
            for copy in strip_copies(s):
                copy.start()

    @pl.when(step == last)
    def _():
        whalf = wt_s.shape[0] // 2
        copies = []
        for part, order in enumerate(orders):
            for slots, out in zip(slot_order(epochs, order), outs[part]):
                for place in range(len(slots)):
                    copies.append(
                        pltpu.make_async_copy(
                            wt_s.at[pl.ds(part * whalf, whalf)],
                            out.at[place, pl.ds(nhalf, whalf)],
                            wt_sems.at[len(copies)],
                        )
                    )
        start_and_wait(copies)
        for s in range(strips):
            for copy in strip_copies(s):
                copy.wait()
        for k in range(kinds):

            @pl.when(ready_s[k] == 0)
            def _():
                for copy in fetches(k):
                    copy.wait()


def template_kernel(terms, *refs):
    term_refs, out_refs, pad_s = refs[: 2 * terms], refs[2 * terms : -1], refs[-1]
    strips = len(out_refs)
    long, share = out_refs[0].shape
    rows_dev = long - 2 * HALO
    nrow = strips * rows_dev
    nhalf = nrow // 2
    whalf = nhalf // share
    edge = jnp.zeros((HALO, share), F32)
    pad_s[pl.ds(0, HALO), :] = edge
    pad_s[pl.ds(HALO + nrow, HALO), :] = edge
    for part in range(2):
        own = term_refs[part * terms : (part + 1) * terms]
        add = lambda place: functools.reduce(lambda a, b: a + b, [ref[0, place, :] for ref in own])
        weights = add(pl.ds(nhalf, whalf))
        for i in range(whalf):
            below = jnp.transpose(jnp.broadcast_to(weights[i : i + 1, :], (share, share)))
            pad_s[pl.ds(HALO + part * nhalf + i * share, share), :] = add(pl.ds(i * share, share)) / below
    for k in range(strips):
        strip = jnp.bitwise_xor(lax.axis_index("strip"), k)
        out_refs[k][...] = pad_s[pl.ds(pl.multiple_of(strip * rows_dev, rows_dev), long), :]


def bands_kernel(psf_ref, toep_hi, toep_lo, band_ref):
    basis, _, ksize = psf_ref.shape
    margin = ksize // 2
    for k in range(basis):
        shape = (2 * LANES, LANES)
        tap = lax.broadcasted_iota(jnp.int32, shape, 0) - lax.broadcasted_iota(jnp.int32, shape, 1)
        tap = tap - (LANES // 2 - margin)
        value = jnp.zeros(shape, F32)
        for j in range(ksize):
            value = jnp.where(tap == j, psf_ref[k, 1, j], value)
        toep_hi[:, pl.ds(k * LANES, LANES)], toep_lo[:, pl.ds(k * LANES, LANES)] = split(value)
        shape = (LANES, LANES + 2 * HALO)
        tap = lax.broadcasted_iota(jnp.int32, shape, 1) - lax.broadcasted_iota(jnp.int32, shape, 0)
        tap = tap - (HALO - margin)
        value = jnp.zeros(shape, F32)
        for j in range(ksize):
            value = jnp.where(tap == j, psf_ref[k, 0, j], value)
        band_ref[k, pl.ds(0, LANES), :], band_ref[k, pl.ds(LANES, LANES), :] = split(value)


def match_kernel(geom, *refs):
    slots, nrow, ncol = geom
    count = max(len(slots), 1) + (len(slots) > 1)
    tile_refs = refs[:count]
    poly_ref, toep_hi, toep_lo, band_ref, sci_ref, out_ref, pad_s, row_s = refs[count:]
    step = pl.program_id(0)
    blocks = pl.num_programs(0)
    tiles = pad_s.shape[0] - 2
    rows_dev = pad_s.shape[1] - 2 * HALO
    me = lax.axis_index("epoch")
    strip = lax.axis_index("strip")
    per_step = out_ref.shape[1] // LANES

    def bring(b):
        if not slots:
            for i in range(per_step):
                place = b * per_step + i
                pad_s[1 + place] = tile_refs[0][place]
            return
        at = jnp.bitwise_xor(strip, b)
        for n, slot in enumerate(slots[:-1]):
            pad_s[1 + b * per_step + jnp.bitwise_xor(me, slot)] = tile_refs[n][at]
        place = 1 + b * per_step + jnp.bitwise_xor(me, slots[-1])
        cut = tile_refs[-1].shape[0]

        @pl.when(at < cut)
        def _():
            pad_s[place] = tile_refs[-2][at]

        @pl.when(at >= cut)
        def _():
            pad_s[place] = tile_refs[-1][at - cut]

    @pl.when(step == 0)
    def _():
        bring(0)
        pad_s[0] = jnp.zeros(pad_s.shape[1:], F32)
        pad_s[tiles + 1] = jnp.zeros(pad_s.shape[1:], F32)
        shape = (rows_dev, LANES)
        counter = (strip * rows_dev + lax.broadcasted_iota(jnp.int32, shape, 0)).astype(F32)
        u = (2.0 * counter + 1.0) / nrow - 1.0
        for k in range(2):
            p = [poly_ref[me, k, i] for i in range(6)]
            row_s[k, 0] = p[0] + u * (p[1] + p[3] * u)
            row_s[k, 1] = p[2] + p[4] * u

    @pl.when(step < blocks - 1)
    def _():
        bring(step + 1)

    lane = lax.broadcasted_iota(jnp.int32, pad_s.shape[1:], 1)
    base = step * per_step
    shifted = []
    for m in range(per_step + 1):
        mixed = jnp.where(lane < LANES // 2, pad_s[base + m + 1], pad_s[base + m])
        shifted.append(split(pltpu.roll(mixed, LANES // 2, 1)))
    toep = (toep_hi[...], toep_lo[...])
    for pair in range(per_step // 2):
        across = []
        for c in (2 * pair, 2 * pair + 1):
            window = tuple(
                jnp.concatenate([shifted[c][i], shifted[c + 1][i]], axis=1) for i in range(2)
            )
            across.append(dot3(window, toep))
        width = 2 * LANES
        cols = lax.broadcasted_iota(jnp.int32, (1, width), 1) + (base + 2 * pair) * LANES
        v = (2.0 * cols.astype(F32) + 1.0) / ncol - 1.0
        for part in range(rows_dev // LANES):
            total = 0.0
            for k in range(2):
                both = jnp.concatenate(
                    [a[part * LANES : part * LANES + LANES + 2 * HALO, k * LANES : (k + 1) * LANES] for a in across],
                    axis=1,
                )
                hi, lo = split(both)
                wide = dot(band_ref[k], hi)
                done = wide[:LANES] + (wide[LANES:] + dot(band_ref[k, pl.ds(0, LANES), :], lo))
                place = pl.ds(part * LANES, LANES)
                one = jnp.concatenate([row_s[k, 0, place, :]] * 2, axis=1)
                two = jnp.concatenate([row_s[k, 1, place, :]] * 2, axis=1)
                coeff = one + v * (two + poly_ref[me, k, 5] * v)
                total = total + coeff * done
            columns = pl.ds(pair * width, width)
            first = rows_dev - sci_ref.shape[1]
            late = min(max(first - part * LANES, 0), LANES)
            if late:
                out_ref[pl.ds(part * LANES, late), columns] = total[:late]
            if late < LANES:
                here = pl.ds(part * LANES + late, LANES - late)
                own = pl.ds(part * LANES + late - first, LANES - late)
                out_ref[here, columns] = sci_ref[0, own, columns] - total[late:]


def subtract_kernel(sci_ref, matched_ref, out_ref):
    i = pl.program_id(0)
    blocks, _, width = sci_ref.shape
    rows = out_ref.shape[1]
    for b in range(blocks):
        columns = pl.ds(b * width, width)
        science = sci_ref[b, pl.ds(pl.multiple_of(i * rows, rows), rows), :]
        out_ref[0, :, columns] = science - matched_ref[0, :, columns]


def swap(value, axis, bit):
    count = lax.axis_size(axis)
    return lax.ppermute(value, axis, [(i, i ^ (1 << bit)) for i in range(count)])


def shards(
    raw_tiles, tile_kind, tile_invvar, tile_heights, row_interp, col_interp, psf_profiles, psf_poly
):
    strips, epochs = lax.axis_size("strip"), lax.axis_size("epoch")
    _, tiles, tile_rows, tile_cols = raw_tiles.shape
    _, blocks, _ = tile_heights.shape
    ncol, nrow = blocks * tile_cols, ROWS_DEV * strips
    sources = strips // blocks
    share = tile_cols // epochs
    bits = epochs.bit_length() - 1
    orders = (tuple(range(bits)), tuple(reversed(range(bits))))
    nhalf = nrow // 2
    wrows = nrow // share
    long_half = nhalf + wrows // 2
    smem = pl.BlockSpec(memory_space=pltpu.SMEM)
    hbm = pl.BlockSpec(memory_space=pl.ANY)
    vmem = pl.BlockSpec(memory_space=pltpu.VMEM)
    kinds = col_interp.shape[0]

    first_rows = ROWS_DEV * FIRST_PART // 8
    sci_shapes = [
        jax.ShapeDtypeStruct((strips, rows, tile_cols), F32) for rows in (first_rows, ROWS_DEV - first_rows)
    ]
    send_shape = jax.ShapeDtypeStruct((epochs // 2, long_half, share), F32)
    together = 2 if tiles % 2 == 0 else 1
    sci_a, sci_b, keep_a, send_a, keep_b, send_b = pl.pallas_call(
        functools.partial(warp_kernel, (epochs, nrow, share, orders, tiles)),
        grid=(tiles // together,),
        in_specs=[
            smem,
            smem,
            smem,
            pl.BlockSpec((together, tile_rows, tile_cols), lambda t: (t, 0, 0)),
            hbm,
            hbm,
        ],
        out_specs=[hbm] * 6,
        out_shape=sci_shapes + [send_shape] * 4,
        scratch_shapes=[
            pltpu.VMEM((nrow, tile_cols), F32),
            pltpu.VMEM((epochs, nrow, share), F32),
            pltpu.VMEM((wrows, share), F32),
            pltpu.VMEM((kinds, tile_rows, tile_rows), F32),
            pltpu.VMEM((kinds, tile_cols, tile_cols), F32),
            pltpu.VMEM((kinds, tile_cols, tile_cols), BF16),
            pltpu.VMEM((kinds, tile_cols, tile_cols), BF16),
            pltpu.SMEM((2,), jnp.int32),
            pltpu.SMEM((kinds,), jnp.int32),
            pltpu.SemaphoreType.DMA((kinds, 2)),
            pltpu.SemaphoreType.DMA((strips, 2 + epochs)),
            pltpu.SemaphoreType.DMA((2 * epochs,)),
        ],
        name="warp",
        cost_estimate=pl.CostEstimate(flops=8_000_000_000, bytes_accessed=20_000_000, transcendentals=0),
    )(tile_kind, tile_heights, tile_invvar, raw_tiles[0], row_interp, col_interp)

    got_a = lax.all_to_all(sci_a, "strip", split_axis=0, concat_axis=0, tiled=True)

    basis, _, _ = psf_profiles.shape
    build_bands = pl.pallas_call(
        bands_kernel,
        in_specs=[smem],
        out_specs=[vmem] * 3,
        out_shape=[
            jax.ShapeDtypeStruct((2 * LANES, 2 * LANES), BF16),
            jax.ShapeDtypeStruct((2 * LANES, 2 * LANES), BF16),
            jax.ShapeDtypeStruct((basis, 2 * LANES, LANES + 2 * HALO), BF16),
        ],
        name="bands",
        cost_estimate=pl.CostEstimate(flops=10_000_000, bytes_accessed=500_000, transcendentals=0),
    )
    toep_hi, toep_lo, band = build_bands(psf_profiles)

    terms = [[keep_a], [keep_b]]
    sends = [send_a, send_b]
    for i in range(bits):
        for part in range(2):
            terms[part].append(swap(sends[part], "epoch", orders[part][i]))
        left = epochs >> (i + 1)
        if left > 1:
            sends = [
                functools.reduce(lambda a, b: a + b, [t[left // 2 : left] for t in own]) for own in terms
            ]
    if sources > 1:
        fixed = []
        for own in terms:
            total = functools.reduce(lambda a, b: a + b, [t[:1] for t in own])
            around = total
            for k in range(1, sources):
                ring = [(i, i // sources * sources + (i + k) % sources) for i in range(strips)]
                around = around + lax.ppermute(total, "strip", ring)
            fixed.append([around])
        terms = fixed

    long = ROWS_DEV + 2 * HALO
    first_slot = pl.BlockSpec((1, long_half, share), lambda i: (0, 0, 0))
    kinds_of_term = [first_slot] * (len(terms[0]) - 1) + [vmem]
    for own in terms:
        own[-1] = pltpu.with_memory_space_constraint(own[-1], pltpu.VMEM)
    parts = pl.pallas_call(
        functools.partial(template_kernel, len(terms[0])),
        grid=(1,),
        in_specs=kinds_of_term * 2,
        out_specs=[pl.BlockSpec((long, share), lambda i: (0, 0))] * strips,
        out_shape=[jax.ShapeDtypeStruct((long, share), F32)] * strips,
        scratch_shapes=[pltpu.VMEM((nrow + 2 * HALO, share), F32)],
        name="template",
        cost_estimate=pl.CostEstimate(flops=2_000_000, bytes_accessed=5_000_000, transcendentals=0),
    )(*terms[0], *terms[1])
    came = [None] * strips
    came[0] = parts[0]
    for k in reversed(range(1, strips)):
        came[k] = lax.ppermute(parts[k], "strip", [(i, i ^ k) for i in range(strips)])
    came[strips // 2], got_a = lax.optimization_barrier((came[strips // 2], got_a))
    mine = jnp.stack(came[:: sources])
    sci_b, mine = lax.optimization_barrier((sci_b, mine))
    got_b = lax.all_to_all(sci_b, "strip", split_axis=0, concat_axis=0, tiled=True)
    if sources > 1:
        got_a = jnp.sum(got_a.reshape((blocks, sources) + got_a.shape[1:]), axis=1)
        got_b = jnp.sum(got_b.reshape((blocks, sources) + got_b.shape[1:]), axis=1)

    per_block = tile_cols // LANES
    if epochs == 4 and share == LANES:
        near = []
        for b in range(2):
            near.append(swap(mine, "epoch", b))
        cut = blocks // 2
        far_low = swap(near[1][:cut], "epoch", 0)
        far_high = swap(near[0][cut:], "epoch", 1)
        arrays = [mine, near[0], near[1], far_low, far_high]
        held = (0, 1, 2, 3)
    else:
        slots = [mine]
        for b in range(bits):
            slots = slots + [swap(s, "epoch", b) for s in slots]
        me = lax.axis_index("epoch")
        every = jnp.take(jnp.stack(slots), jnp.bitwise_xor(jnp.arange(epochs), me), axis=0)
        home = lax.axis_index("strip") // sources
        every = jnp.take(every, jnp.bitwise_xor(jnp.arange(blocks), home), axis=1)
        flat = jnp.transpose(every, (1, 2, 0, 3)).reshape(blocks, long, per_block, LANES)
        arrays = [jnp.transpose(flat, (0, 2, 1, 3)).reshape(blocks * per_block, long, LANES)]
        held = ()

    const = lambda b: (0, 0)
    convolve = pl.pallas_call(
        functools.partial(match_kernel, (held, nrow, ncol)),
        grid=(blocks,),
        in_specs=[vmem] * len(arrays)
        + [
            smem,
            pl.BlockSpec(toep_hi.shape, const),
            pl.BlockSpec(toep_lo.shape, const),
            pl.BlockSpec(band.shape, lambda b: (0, 0, 0)),
            pl.BlockSpec((1,) + got_a.shape[1:], lambda b: (b, 0, 0)),
        ],
        out_specs=pl.BlockSpec((ROWS_DEV, tile_cols), lambda b: (0, b)),
        out_shape=jax.ShapeDtypeStruct((ROWS_DEV, ncol), F32),
        scratch_shapes=[
            pltpu.VMEM((blocks * per_block + 2, long, LANES), F32),
            pltpu.VMEM((2, 2, ROWS_DEV, LANES), F32),
        ],
        name="convolve",
        compiler_params=pltpu.CompilerParams(vmem_limit_bytes=28 << 20),
        cost_estimate=pl.CostEstimate(flops=15_000_000_000, bytes_accessed=10_000_000, transcendentals=0),
    )
    arrays = arrays[:1] + [pltpu.with_memory_space_constraint(x, pltpu.VMEM) for x in arrays[1:]]
    matched = convolve(*arrays, psf_poly, toep_hi, toep_lo, band, got_a)
    unit = (ROWS_DEV - first_rows) // 2
    late_rows = pl.BlockSpec((1, unit, ncol), lambda i: (0, i, 0))
    return pl.pallas_call(
        subtract_kernel,
        grid=(2,),
        in_specs=[vmem, late_rows],
        out_specs=late_rows,
        out_shape=jax.ShapeDtypeStruct((1, ROWS_DEV, ncol), F32),
        input_output_aliases={1: 0},
        name="subtract",
        compiler_params=pltpu.CompilerParams(vmem_limit_bytes=16 << 20),
        cost_estimate=pl.CostEstimate(flops=1_000_000, bytes_accessed=6_000_000, transcendentals=0),
    )(pltpu.with_memory_space_constraint(got_b, pltpu.VMEM), matched[None])


def solution(mesh):
    in_specs = (
        P("epoch", "strip", None, None),
        P("epoch", "strip"),
        P("epoch", "strip"),
        P("epoch", None, None),
        P(),
        P(),
        P(),
        P(),
    )
    out_specs = P("epoch", "strip", None)

    return jax.shard_map(shards, mesh=mesh, in_specs=in_specs, out_specs=out_specs, check_vma=False)
```
